32 devices in a mesh: dp: 16 (over z, y, core), mp: 2 (over x).
Axes of the slice: x: 2, y: 2, z: 4, core: 2. Of those that a mesh axis runs over, the one named last changes fastest.
Arguments:
- tokens: bfloat16 [32768, 768], P('dp'), may hold values from -6 to 6
- grad_out: bfloat16 [32768, 768], P('dp'), may hold values from -6 to 6
- head_perm: int32 [32, 12], P('dp', 'mp'), may hold values from 0 to 1
- block_mask: int32 [32, 12, 3], P('dp', 'mp'), may hold values 0 or 1
- w_qkv: bfloat16 [768, 3, 768], P('dp', None, 'mp'), may hold values from -0.3125 to 0.3125
- b_qv: bfloat16 [2, 768], P(None, ('mp', 'dp')), may hold values from -3 to 3
- w_out: bfloat16 [768, 768], P('mp', 'dp'), may hold values from -0.625 to 0.625
- b_out: bfloat16 [768], P('dp'), may hold values from -3 to 3
- gain_one: bfloat16 [768], P('dp'), may hold values from 0.25 to 1.75
- shift_one: bfloat16 [768], P('dp'), may hold values from -2 to 2
- w_up: bfloat16 [768, 3072], P('dp', 'mp'), may hold values from -0.21875 to 0.21875
- b_up: bfloat16 [3072], P(('mp', 'dp')), may hold values from -3 to 3
- w_down: bfloat16 [3072, 768], P('mp', 'dp'), may hold values from -0.15625 to 0.15625
- b_down: bfloat16 [768], P('dp'), may hold values from -2 to 2
- gain_two: bfloat16 [768], P('dp'), may hold values from 0.25 to 1.75
- shift_two: bfloat16 [768], P('dp'), may hold values from -2 to 2
Outputs:
- output: bfloat16 [32768, 768], P('dp')
- input_grad: float32 [32768, 768], P('dp')
- grad_w_qkv: float32 [768, 3, 768], P('dp', None, 'mp')
- grad_b_qv: float32 [2, 768], P(None, ('mp', 'dp'))
- grad_w_out: float32 [768, 768], P('mp', 'dp')
- grad_b_out: float32 [768], P('dp')
- grad_gain_one: float32 [768], P('dp')
- grad_shift_one: float32 [768], P('dp')
- grad_w_up: float32 [768, 3072], P('dp', 'mp')
- grad_b_up: float32 [3072], P(('mp', 'dp'))
- grad_w_down: float32 [3072, 768], P('mp', 'dp')
- grad_b_down: float32 [768], P('dp')
- grad_gain_two: float32 [768], P('dp')
- grad_shift_two: float32 [768], P('dp')
The draws below stay inside these ranges and needn't reach their ends.
Inputs may be any that keep to these rules, and one draw needn't show every extreme that they name: `head_perm`: 0 pairs each half with itself, 1 pairs it with the other half. `block_mask`: entry a + b is the keep flag of block a of the queries with block b of the keys (b <= a).
All inputs are finite; a program needn't handle non-finite values.
Results may differ from the reference program's by a relative error of at most 0.015.
The reference program's roundings to bfloat16 on the way count: a program that leaves them out, or rounds other values in their place, can miss the bound.
Values may be sent and summed in bfloat16 or wider, within the bound.
No kernel may reach another device: no remote copies, remote signals or barrier semaphores. Data moves between devices by JAX's collectives and lax.ppermute only.
A program may use at most 256 MiB of HBM per device.

```python
import jax
import jax.numpy as jnp
from jax import lax

D = 768
H = 12
FF = 3072
SEQ_LEN = 1024
MB = 2
SEQS = 32
TOKENS = 32768
N_DP = 16


def with_ends(drawn, rng, smallest, high):
    dims = drawn.shape
    index_at = [jax.random.randint(jax.random.fold_in(rng, axis), (), 0, dims[axis]) for axis in range(len(dims))]
    drawn = drawn.at[tuple(index_at)].set(smallest)
    longest = dims.index(max(dims))
    index_at[longest] = (index_at[longest] + 1) % dims[longest]
    return drawn.at[tuple(index_at)].set(high)


def spiked(array, key, source, target, blocks, factor):
    owner, partner = [(jnp.arange(array.shape[position]) // (array.shape[position] // blocks)).reshape([-1 if axis == position else 1 for axis in range(array.ndim)]) for position in (source, target)]
    chosen = jax.random.permutation(key, blocks)[partner]
    strong = (owner == chosen) | (owner == (partner + blocks // 2) % blocks)
    return jnp.where(strong, factor * array, array)


def steps_of(rng, shape, split, least, high):
    def one(dim, parts):
        steps = jax.random.uniform(jax.random.fold_in(jax.random.fold_in(rng, 6), dim), (parts,), jnp.float32, least / len(split), high / len(split))
        return jnp.repeat(jnp.exp(steps), shape[dim] // parts).reshape((-1,) + (1,) * (len(shape) - dim - 1))

    loudness = one(*split[0])
    for cut in split[1:]:
        loudness = loudness * one(*cut)
    return loudness


def centred(key, dims, spread, reach, cuts=(), held_as=jnp.bfloat16):
    entries = spread * jax.random.normal(key, dims, jnp.float32)
    if cuts:
        entries = entries * steps_of(key, dims, cuts, -0.22, 0.18)
    return jnp.clip(entries, -reach, reach).astype(held_as)


def bell_draw_with(own_key, extent, scale, limit, split, heavy, kind=jnp.bfloat16):
    array = scale * jax.random.normal(own_key, extent, jnp.float32)
    if split:
        array = array * steps_of(own_key, extent, split, -0.22, 0.18)
    return jnp.clip(spiked(array, jax.random.fold_in(own_key, 3), *heavy), -limit, limit).astype(kind)


def setup_inputs(seed: int = 0) -> dict:
    key_list = jax.random.split(jax.random.key(seed), 17)
    tokens = centred(key_list[0], (TOKENS, D), 1.0, 6.0, ((0, 16),))
    grad_out = bell_draw_with(key_list[1], (TOKENS, D), 1.0, 6.0, ((0, 16),), (0, 1, 16, 2.0))
    head_perm = with_ends(jax.random.randint(key_list[2], (SEQS, H), 0, 2), jax.random.fold_in(key_list[2], 1), 0, 1).astype(jnp.int32)
    block_mask = with_ends((jax.random.randint(key_list[3], (SEQS, H, 3), 0, 4) < 3).astype(jnp.int32), jax.random.fold_in(key_list[3], 1), 0, 1)
    w_qkv = centred(key_list[4], (D, 3, D), (D // 2) ** -0.5, 0.3125, ((0, 16), (2, 2)))
    b_qv = centred(key_list[5], (2, D), 0.5, 3.0, ((1, 32),))
    w_out = centred(key_list[6], (D, D), (D // 8) ** -0.5, 0.625, ((0, 2), (1, 16)))
    b_out = centred(key_list[7], (D,), 0.5, 3.0, ((0, 16),))
    gain_one = jnp.clip(1.0 + 0.15 * jax.random.normal(key_list[8], (D,), jnp.float32), 0.25, 1.75).astype(jnp.bfloat16)
    shift_one = centred(key_list[9], (D,), 0.3, 2.0, ((0, 16),))
    w_up = centred(key_list[10], (D, FF), D ** -0.5, 0.21875, ((0, 16), (1, 2)))
    b_up = centred(key_list[11], (FF,), 0.5, 3.0, ((0, 32),))
    w_down = centred(key_list[12], (FF, D), (FF // 2) ** -0.5, 0.15625, ((0, 2), (1, 16)))
    b_down = centred(key_list[13], (D,), 0.3, 2.0, ((0, 16),))
    gain_two = jnp.clip(1.0 + 0.15 * jax.random.normal(key_list[14], (D,), jnp.float32), 0.25, 1.75).astype(jnp.bfloat16)
    shift_two = centred(key_list[15], (D,), 0.3, 2.0, ((0, 16),))
    return dict(tokens=tokens, grad_out=grad_out, head_perm=head_perm, block_mask=block_mask, w_qkv=w_qkv, b_qv=b_qv, w_out=w_out, b_out=b_out, gain_one=gain_one, shift_one=shift_one, w_up=w_up, b_up=b_up, w_down=w_down, b_down=b_down, gain_two=gain_two, shift_two=shift_two)


highest = lax.Precision.HIGHEST
norm_eps = 1e-05
masked_fill = -1e+30

@jax.custom_vjp
def low(v):
    return lax.optimization_barrier(v.astype(jnp.bfloat16)).astype(jnp.float32)

@jax.custom_vjp
def low_back(v):
    return v

def low_keep(v):
    return (low(v), None)

def low_pass(kept, grad):
    return (grad,)

def back_keep(v):
    return (v, None)

def back_low(kept, grad):
    return (low(grad),)
low.defvjp(low_keep, low_pass)
low_back.defvjp(back_keep, back_low)

def layer_norm(hidden, gain_vec, shift_vec):
    centered = hidden - lax.optimization_barrier(jnp.mean(hidden, axis=-1, keepdims=True))
    variance = lax.optimization_barrier(jnp.mean(centered * centered, axis=-1, keepdims=True))
    return centered * lax.rsqrt(variance + norm_eps) * gain_vec + shift_vec

def gelu_exact(values):
    return jax.nn.gelu(values, approximate=False)

def pair_pattern(mask_rows, half_len, block_len):
    blocks = jnp.arange(half_len) // block_len
    row_block = blocks[:, None]
    col_block = blocks[None, :]
    entry_index = row_block + col_block
    chosen = jnp.zeros((mask_rows.shape[0], half_len, half_len), dtype=jnp.bool_)
    for entry_id in range(3):
        chosen = chosen | (mask_rows[:, entry_id, None, None] == 1) & (entry_index == entry_id)[None]
    allowed = chosen & (col_block <= row_block)[None]
    allowed_f = allowed.astype(jnp.float32)
    dead_f = 1.0 - lax.optimization_barrier(jnp.max(allowed_f, axis=-1))
    return (allowed, allowed_f, dead_f)

def pair_keys(values, swapped):
    return jnp.where(swapped[None, :, None], jnp.roll(values, values.shape[0] // 2, axis=0), values)

def attend(pieces):
    queries, key_rows, value_rows, perm_seq, mask_seq = pieces
    seq_len, head_count, head_dim = queries.shape
    half_len = seq_len // 2
    swapped = perm_seq == 1
    query_pair = queries.reshape(2, half_len, head_count, head_dim)
    key_pair = pair_keys(key_rows, swapped).reshape(2, half_len, head_count, head_dim)
    value_pair = pair_keys(value_rows, swapped).reshape(2, half_len, head_count, head_dim)
    allowed, allowed_f, dead_f = pair_pattern(mask_seq, half_len, half_len // 2)
    raw_scores = jnp.einsum('iqhd,ikhd->ihqk', query_pair, key_pair, precision=highest) * head_dim ** (-0.5)
    scores = low_back(raw_scores)
    masked = jnp.where(allowed[None], scores, masked_fill)
    row_max = lax.optimization_barrier(jnp.max(masked, axis=-1))
    row_total = lax.optimization_barrier(jnp.sum(jnp.exp(masked - row_max[..., None]) * allowed_f[None], axis=-1))
    log_total = row_max + jnp.log(row_total + dead_f[None])
    attn_weights = low(jnp.exp(masked - log_total[..., None]) * allowed_f[None])
    context = jnp.einsum('ihqk,ikhd->iqhd', attn_weights, value_pair, precision=highest)
    return context.reshape(seq_len, head_count * head_dim)

def forward(tokens_grp, perm_grp, mask_grp, w_qkv, b_qv, w_out, b_out, gain_one, shift_one, w_up, b_up, w_down, b_down, gain_two, shift_two):
    seq_count = perm_grp.shape[0]
    token_count = tokens_grp.shape[0]
    seq_len = token_count // seq_count
    head_count = perm_grp.shape[1]
    head_dim = w_qkv.shape[2] // head_count
    projected = jnp.einsum('td,dcf->tcf', tokens_grp, w_qkv, precision=highest)
    bias_rows = jnp.stack([b_qv[0], jnp.zeros_like(b_qv[0]), b_qv[1]])
    projected = low(low_back(projected + bias_rows[None]))
    split_heads = projected.reshape(seq_count, seq_len, 3, head_count, head_dim)
    context = lax.map(jax.checkpoint(attend), (split_heads[:, :, 0], split_heads[:, :, 1], split_heads[:, :, 2], perm_grp, mask_grp))
    context = low(low_back(context.reshape(token_count, head_count * head_dim)))
    attn_out = low_back(jnp.dot(context, w_out, precision=highest, preferred_element_type=jnp.float32)) + b_out
    resid_one = tokens_grp + attn_out
    normed_one = layer_norm(resid_one, gain_one, shift_one)
    pre_act = low_back(jnp.dot(low(normed_one), w_up, precision=highest, preferred_element_type=jnp.float32) + b_up)
    hidden = low(gelu_exact(pre_act))
    ffn_out = low_back(jnp.dot(hidden, w_down, precision=highest, preferred_element_type=jnp.float32)) + b_down
    return layer_norm(normed_one + ffn_out, gain_two, shift_two)

def reference(tokens, grad_out, head_perm, block_mask, w_qkv, b_qv, w_out, b_out, gain_one, shift_one, w_up, b_up, w_down, b_down, gain_two, shift_two):
    params = tuple((argument.astype(jnp.float32) for argument in (w_qkv, b_qv, w_out, b_out, gain_one, shift_one, w_up, b_up, w_down, b_down, gain_two, shift_two)))
    group_tokens = MB * SEQ_LEN
    tokens_grp = tokens.astype(jnp.float32).reshape(N_DP, group_tokens, D)
    cotangent = grad_out.astype(jnp.float32).reshape(N_DP, group_tokens, D)
    perm_grp = head_perm.reshape(N_DP, MB, H)
    mask_grp = block_mask.reshape(N_DP, MB, H, 3)

    def group_step(running, pieces):
        tokens_one, cot_one, perm_one, mask_one = pieces

        def run_group(tokens_in, *weights):
            return forward(tokens_in, perm_one, mask_one, *weights)
        out_one, pullback = jax.vjp(run_group, tokens_one, *params)
        gradients = pullback(cot_one)
        running = tuple((summed + latest for summed, latest in zip(running, gradients[1:])))
        return (running, (out_one.astype(jnp.bfloat16), gradients[0]))
    initial = tuple((jnp.zeros_like(argument) for argument in params))
    totals, (out_rows, input_rows) = lax.scan(group_step, initial, (tokens_grp, cotangent, perm_grp, mask_grp))
    return (out_rows.reshape(TOKENS, D), input_rows.reshape(TOKENS, D), totals[0], totals[1], totals[2], totals[3], totals[4], totals[5], totals[6], totals[7], totals[8], totals[9], totals[10], totals[11])
```

```python
import functools

import jax
import jax.numpy as jnp
from jax import lax
from jax.experimental import pallas as pl
from jax.experimental.pallas import tpu as pltpu
from jax.sharding import PartitionSpec as P

HD = 64
PAIR = 2 * HD
BLOCK = 256
HALF = 2 * BLOCK
NORM_EPS = 1e-05
BF = jnp.bfloat16
F32 = jnp.float32
AXES = ("dp", "mp")
NN = (((1,), (0,)), ((), ()))
NT = (((1,), (1,)), ((), ()))
TN = (((0,), (0,)), ((), ()))
SMALL = 128


def mm(first, second, dims):
    return lax.dot_general(first, second, dims, preferred_element_type=F32)


def pairs_of(step):
    moves = []
    for d in range(16):
        for m in range(2):
            d2, m2 = step(d, m)
            moves.append((2 * d + m, 2 * d2 + m2))
    return moves


MOVE_X = pairs_of(lambda d, m: (d, 1 - m))
MOVE_Y = pairs_of(lambda d, m: (d ^ 2, m))
MOVE_CORE = pairs_of(lambda d, m: (d ^ 1, m))
MOVE_Z = [pairs_of(lambda d, m, k=k: ((d + 4 * k) % 16, m)) for k in (1, 2, 3)]
MOVE_FIRST = pairs_of(lambda d, m: (d ^ 2, m) if d & 1 else (d, 1 - m))
MOVE_SECOND = pairs_of(lambda d, m: (d, 1 - m) if d & 1 else (d ^ 2, m))


def move(values, moves):
    return lax.ppermute(values, AXES, moves)


def swap_mp(values):
    return lax.ppermute(values, "mp", [(0, 1), (1, 0)])


def assemble_kernel(where, *refs):
    pieces, (own_ref, other_ref), sem = refs[:8], refs[8:10], refs[10]
    rows = pieces[0].shape[1]
    z, y, core = where[0], where[1], where[2]
    z0, a0, b0, c0, z1, a1, b1, c1 = pieces
    first = core == 0

    def copies(ref, target, dy, dcore, slot):
        out = []
        for k in range(4):
            block = ((lax.rem(z + 4 - k, 4) * 2 + (y ^ dy)) * 2 + (core ^ dcore)) * rows
            out.append(
                pltpu.make_async_copy(
                    ref.at[k], target.at[pl.ds(pl.multiple_of(block, 16), rows), :], sem.at[slot, k]
                )
            )
        return out

    def both(cond, ref_if, ref_else, target, dy, dcore, slot):
        @pl.when(cond)
        def _():
            for copy in copies(ref_if, target, dy, dcore, slot):
                copy.start()

        @pl.when(jnp.logical_not(cond))
        def _():
            for copy in copies(ref_else, target, dy, dcore, slot):
                copy.start()

        return copies(ref_if, target, dy, dcore, slot)

    waits = []
    for slot, (ref, target, dy, dcore) in enumerate(
        ((z0, own_ref, 0, 0), (c0, other_ref, 1, 0), (z1, own_ref, 0, 1), (c1, other_ref, 1, 1))
    ):
        for copy in copies(ref, target, dy, dcore, slot):
            copy.start()
            waits.append(copy)
    waits += both(first, b0, a0, own_ref, 1, 0, 4)
    waits += both(first, a0, b0, other_ref, 0, 0, 5)
    waits += both(first, a1, b1, own_ref, 1, 1, 6)
    waits += both(first, b1, a1, other_ref, 0, 1, 7)
    for copy in waits:
        copy.wait()


def assemble(where, pieces):
    rows, cols = pieces[0].shape[1:]
    full = jax.ShapeDtypeStruct((16 * rows, cols), pieces[0].dtype)
    return pl.pallas_call(
        assemble_kernel,
        out_shape=(full, full),
        grid_spec=pltpu.PrefetchScalarGridSpec(
            num_scalar_prefetch=1,
            grid=(1,),
            in_specs=[pl.BlockSpec(memory_space=pl.ANY)] * 8,
            out_specs=[pl.BlockSpec((16 * rows, cols), lambda i, w: (0, 0))] * 2,
            scratch_shapes=[pltpu.SemaphoreType.DMA((8, 4))],
        ),
        cost_estimate=pl.CostEstimate(
            flops=0, transcendentals=0, bytes_accessed=64 * rows * cols * 2
        ),
        name="assemble",
    )(where, *pieces)


def gather(where, shard, dp_size):
    if dp_size != 16:
        full = lax.all_gather(shard, "dp", axis=0, tiled=True)
        return full, swap_mp(full)
    along_z = jnp.stack([shard] + [move(shard, moves) for moves in MOVE_Z])
    a = move(along_z, MOVE_FIRST)
    b = move(along_z, MOVE_SECOND)
    c = move(a, MOVE_SECOND)
    pieces = [along_z, a, b, c]
    pieces += [move(piece, MOVE_CORE) for piece in pieces]
    return assemble(where, pieces)


def split_kernel(where, own_ref, other_ref, keep_ref, send_ref, sem):
    rows = keep_ref.shape[3]
    z, y, core = where[0], where[1], where[2]
    copies = []
    for dcore, target in enumerate((keep_ref, send_ref)):
        for dy in range(2):
            for dm, source in enumerate((own_ref, other_ref)):
                for k in range(4):
                    block = ((lax.rem(z + k, 4) * 2 + (y ^ dy)) * 2 + (core ^ dcore)) * rows
                    copies.append(
                        pltpu.make_async_copy(
                            source.at[pl.ds(pl.multiple_of(block, 16), rows), :],
                            target.at[dy, dm, k],
                            sem.at[len(copies)],
                        )
                    )
    for copy in copies:
        copy.start()
    for copy in copies:
        copy.wait()


def split(where, own, other):
    rows, cols = own.shape[0] // 16, own.shape[1]
    part = jax.ShapeDtypeStruct((2, 2, 4, rows, cols), own.dtype)
    return pl.pallas_call(
        split_kernel,
        out_shape=(part, part),
        grid_spec=pltpu.PrefetchScalarGridSpec(
            num_scalar_prefetch=1,
            grid=(1,),
            in_specs=[pl.BlockSpec((16 * rows, cols), lambda i, w: (0, 0))] * 2,
            out_specs=[pl.BlockSpec(memory_space=pl.ANY)] * 2,
            scratch_shapes=[pltpu.SemaphoreType.DMA((32,))],
        ),
        cost_estimate=pl.CostEstimate(
            flops=0, transcendentals=0, bytes_accessed=64 * rows * cols * 2
        ),
        name="split",
    )(where, own, other)


def reduce_scatter(where, own, other, dp_size):
    if dp_size != 16:
        summed = own.astype(F32) + swap_mp(other).astype(F32)
        return lax.psum_scatter(summed, "dp", scatter_dimension=0, tiled=True)

    def add(first, second):
        return (first.astype(F32) + second.astype(F32)).astype(BF)

    keep, send = split(where, own, other)
    got = move(send, MOVE_CORE)
    send = add(keep[1], got[1])
    keep = add(keep[0], got[0])
    got = move(send, MOVE_Y)
    send = add(keep[1], got[1])
    keep = add(keep[0], got[0])
    got = move(send, MOVE_X)
    parts = [add(keep[k], got[k]) for k in range(1, 4)]
    total = keep[0].astype(F32) + got[0].astype(F32)
    for part, moves in zip(parts, MOVE_Z):
        total = total + move(part, moves).astype(F32)
    return total


def lane_mask(head, rows):
    lanes = lax.broadcasted_iota(jnp.int32, (rows, PAIR), 1)
    return (lanes < HD) if head == 0 else (lanes >= HD)


def attn_fwd_kernel(table, q_ref, k_ref, v_ref, ctx_ref, prob_ref):
    pair = pl.program_id(0)
    lanes = lax.broadcasted_iota(jnp.int32, (1, HALF), 1)
    for half in range(2):
        rows = pl.ds(half * HALF, HALF)
        query = q_ref[rows, :] * jnp.asarray(HD**-0.5, BF)
        parts = []
        for head in range(2):
            at = (pair * 2 + head) * 4
            start = (half ^ table[at]) * HALF
            flags = [table[at + 1 + n] == 1 for n in range(3)]
            key_lo = k_ref[pl.ds(pl.multiple_of(start, BLOCK), BLOCK), :]
            key_hi = k_ref[pl.ds(pl.multiple_of(start + BLOCK, BLOCK), BLOCK), :]
            masked = jnp.where(lane_mask(head, HALF), query, jnp.zeros_like(query))
            score_lo = mm(key_lo, masked, NT)
            score_hi = mm(key_hi, masked[BLOCK:], NT)
            no_lo = jnp.where(
                lanes < BLOCK,
                jnp.where(flags[0], 0.0, -1e30),
                jnp.where(flags[1], 0.0, -1e30),
            ).astype(F32)
            no_hi = jnp.where(flags[2], 0.0, -1e30).astype(F32)
            top_lo = jnp.max(score_lo, axis=0, keepdims=True) + no_lo
            top_hi = jnp.max(score_hi, axis=0, keepdims=True) + no_hi
            top = jnp.concatenate(
                [top_lo[:, :BLOCK], jnp.maximum(top_lo[:, BLOCK:], top_hi)], axis=1
            )
            ref_lo = jnp.where(no_lo < 0.0, 1e30, top)
            ref_hi = jnp.where(no_hi < 0.0, 1e30, top[:, BLOCK:])
            exp_lo = jnp.exp(score_lo - ref_lo)
            exp_hi = jnp.exp(score_hi - ref_hi)
            sum_lo = jnp.sum(exp_lo, axis=0, keepdims=True)
            sum_hi = jnp.sum(exp_hi, axis=0, keepdims=True)
            total = jnp.concatenate([sum_lo[:, :BLOCK], sum_lo[:, BLOCK:] + sum_hi], axis=1)
            scale = jnp.where(total > 0.0, 1.0 / jnp.where(total > 0.0, total, 1.0), 0.0)
            prob_lo = (exp_lo * scale).astype(BF)
            prob_hi = (exp_hi * scale[:, BLOCK:]).astype(BF)
            prob_ref[0, head, half, :, :HALF] = prob_lo
            prob_ref[0, head, half, :, HALF:] = prob_hi
            val_lo = v_ref[pl.ds(pl.multiple_of(start, BLOCK), BLOCK), :].T
            val_hi = v_ref[pl.ds(pl.multiple_of(start + BLOCK, BLOCK), BLOCK), :].T
            side = slice(head * HD, (head + 1) * HD)
            out_lo = mm(val_lo[side], prob_lo, NN)
            out_hi = mm(val_hi[side], prob_hi, NN)
            parts.append(
                jnp.concatenate([out_lo[:, :BLOCK], out_lo[:, BLOCK:] + out_hi], axis=1)
            )
        ctx_ref[rows, :] = jnp.concatenate(parts, axis=0).T.astype(BF)


def attn_fwd(table, proj):
    seq, width = proj.shape
    pairs = width // 3 // PAIR
    return pl.pallas_call(
        attn_fwd_kernel,
        out_shape=(
            jax.ShapeDtypeStruct((seq, width // 3), BF),
            jax.ShapeDtypeStruct((pairs, 2, 2, BLOCK, HALF + BLOCK), BF),
        ),
        grid_spec=pltpu.PrefetchScalarGridSpec(
            num_scalar_prefetch=1,
            grid=(pairs,),
            in_specs=[
                pl.BlockSpec((seq, PAIR), lambda p, t: (0, p)),
                pl.BlockSpec((seq, PAIR), lambda p, t: (0, p + pairs)),
                pl.BlockSpec((seq, PAIR), lambda p, t: (0, p + 2 * pairs)),
            ],
            out_specs=[
                pl.BlockSpec((seq, PAIR), lambda p, t: (0, p)),
                pl.BlockSpec((1, 2, 2, BLOCK, HALF + BLOCK), lambda p, t: (p, 0, 0, 0, 0)),
            ],
        ),
        cost_estimate=pl.CostEstimate(
            flops=pairs * 4 * 2 * 2 * 3 * BLOCK * BLOCK * PAIR,
            transcendentals=pairs * 4 * 3 * BLOCK * BLOCK,
            bytes_accessed=pairs * 4 * 3 * BLOCK * BLOCK * 2 + seq * width * 3,
        ),
        name="attn_fwd",
    )(table, proj, proj, proj)


def attn_bwd_kernel(table, q_ref, k_ref, v_ref, d_ref, prob_ref, dq_ref, dk_ref, dv_ref, k_acc, v_acc):
    pair = pl.program_id(0)
    for half in range(2):
        rows = pl.ds(half * HALF, HALF)
        query = q_ref[rows, :] * jnp.asarray(HD**-0.5, BF)
        d_ctx = d_ref[rows, :]
        parts = []
        for head in range(2):
            at = (pair * 2 + head) * 4
            start = (half ^ table[at]) * HALF
            at_lo = pl.ds(pl.multiple_of(start, BLOCK), BLOCK)
            at_hi = pl.ds(pl.multiple_of(start + BLOCK, BLOCK), BLOCK)
            keep = lane_mask(head, HALF)
            query_h = jnp.where(keep, query, jnp.zeros_like(query))
            d_ctx_h = jnp.where(keep, d_ctx, jnp.zeros_like(d_ctx))
            prob_lo = prob_ref[0, head, half, :, :HALF]
            prob_hi = prob_ref[0, head, half, :, HALF:]
            d_w_lo = mm(v_ref[at_lo, :], d_ctx_h, NT)
            d_w_hi = mm(v_ref[at_hi, :], d_ctx_h[BLOCK:], NT)
            wide_lo = prob_lo.astype(F32)
            wide_hi = prob_hi.astype(F32)
            dot_lo = jnp.sum(wide_lo * d_w_lo, axis=0, keepdims=True)
            dot_hi = jnp.sum(wide_hi * d_w_hi, axis=0, keepdims=True)
            dot = jnp.concatenate([dot_lo[:, :BLOCK], dot_lo[:, BLOCK:] + dot_hi], axis=1)
            d_s_lo = (wide_lo * (d_w_lo - dot)).astype(BF)
            d_s_hi = (wide_hi * (d_w_hi - dot[:, BLOCK:])).astype(BF)
            dk_lo = mm(d_s_lo, query_h, NN)
            dk_hi = mm(d_s_hi, query_h[BLOCK:], NN)
            dv_lo = mm(prob_lo, d_ctx_h, NN)
            dv_hi = mm(prob_hi, d_ctx_h[BLOCK:], NN)
            k_acc[head, at_lo, :] = dk_lo
            k_acc[head, at_hi, :] = dk_hi
            v_acc[head, at_lo, :] = dv_lo
            v_acc[head, at_hi, :] = dv_hi
            key_lo = k_ref[at_lo, :].T
            key_hi = k_ref[at_hi, :].T
            side = slice(head * HD, (head + 1) * HD)
            dq_lo = mm(key_lo[side], d_s_lo, NN)
            dq_hi = mm(key_hi[side], d_s_hi, NN)
            parts.append(jnp.concatenate([dq_lo[:, :BLOCK], dq_lo[:, BLOCK:] + dq_hi], axis=1))
        dq_ref[rows, :] = (jnp.concatenate(parts, axis=0).T * HD**-0.5).astype(BF)
    dk_ref[...] = (k_acc[0] + k_acc[1]).astype(BF)
    dv_ref[...] = (v_acc[0] + v_acc[1]).astype(BF)


def attn_bwd(table, proj, d_context, probs):
    seq, width = proj.shape
    pairs = width // 3 // PAIR
    part = jax.ShapeDtypeStruct((seq, width // 3), BF)
    column = pl.BlockSpec((seq, PAIR), lambda p, t: (0, p))
    return pl.pallas_call(
        attn_bwd_kernel,
        out_shape=(part, part, part),
        grid_spec=pltpu.PrefetchScalarGridSpec(
            num_scalar_prefetch=1,
            grid=(pairs,),
            in_specs=[
                column,
                pl.BlockSpec((seq, PAIR), lambda p, t: (0, p + pairs)),
                pl.BlockSpec((seq, PAIR), lambda p, t: (0, p + 2 * pairs)),
                column,
                pl.BlockSpec((1, 2, 2, BLOCK, HALF + BLOCK), lambda p, t: (p, 0, 0, 0, 0)),
            ],
            out_specs=[column] * 3,
            scratch_shapes=[pltpu.VMEM((2, seq, PAIR), F32)] * 2,
        ),
        cost_estimate=pl.CostEstimate(
            flops=pairs * 4 * 4 * 2 * 3 * BLOCK * BLOCK * PAIR,
            transcendentals=0,
            bytes_accessed=pairs * 4 * 3 * BLOCK * BLOCK * 2 + seq * width * 5,
        ),
        name="attn_bwd",
    )(table, proj, proj, proj, d_context, probs)


def norm_parts(values):
    centered = values - jnp.mean(values, axis=-1, keepdims=True)
    inverse = lax.rsqrt(jnp.mean(centered * centered, axis=-1, keepdims=True) + NORM_EPS)
    return centered * inverse, inverse


def norm_back(d_normed, z, inverse, gain):
    dz = d_normed * gain
    return (
        dz - jnp.mean(dz, axis=-1, keepdims=True) - z * jnp.mean(dz * z, axis=-1, keepdims=True)
    ) * inverse


def gelu_both(values):
    half = 0.5 * (1.0 + lax.erf(values * (0.5**0.5)))
    slope = half + values * jnp.exp(-0.5 * values * values) * 0.3989422804014327
    return values * half, slope


def body(
    dp_size,
    tokens,
    grad_out,
    head_perm,
    block_mask,
    w_qkv,
    b_qv,
    w_out,
    b_out,
    gain_one,
    shift_one,
    w_up,
    b_up,
    w_down,
    b_down,
    gain_two,
    shift_two,
):
    seq = tokens.shape[0] // head_perm.shape[0]
    rows = w_qkv.shape[0]
    width = w_qkv.shape[2]
    d_model = tokens.shape[1]
    dp_at = lax.axis_index("dp")
    mp_at = lax.axis_index("mp")
    where = jnp.stack([dp_at // 4, (dp_at // 2) % 2, dp_at % 2]).astype(jnp.int32)

    own_tokens = lax.dynamic_slice_in_dim(tokens, mp_at * seq, seq, 0)
    own_grad = lax.dynamic_slice_in_dim(grad_out, mp_at * seq, seq, 0)
    table = jnp.concatenate([head_perm[:, :, None], block_mask], axis=2).astype(jnp.int32)
    table = table.reshape(2, -1)
    table_own = lax.dynamic_index_in_dim(table, mp_at, 0, keepdims=False)
    table_other = swap_mp(lax.dynamic_index_in_dim(table, 1 - mp_at, 0, keepdims=False))

    small = jnp.stack(
        [
            b_out,
            gain_one,
            shift_one,
            b_down,
            gain_two,
            shift_two,
            b_up[:rows],
            b_up[rows:],
            b_qv.reshape(-1),
        ],
        axis=1,
    )
    small = jnp.pad(small, ((0, 0), (0, SMALL - small.shape[1])))
    shard_qkv = jnp.concatenate([w_qkv.reshape(rows, 3 * width), small], axis=1)
    qkv_own, qkv_other = gather(where, shard_qkv, dp_size)
    shard_up = jnp.concatenate([w_out.T, w_up], axis=1)
    up_own, up_other = gather(where, shard_up, dp_size)
    down_own, down_other = gather(where, w_down.T, dp_size)

    small_own = qkv_own[:, 3 * width :].astype(F32)
    small_other = qkv_other[:, 3 * width :].astype(F32)
    vectors = small_own.T
    b_out_f, gain_one_f, shift_one_f, b_down_f, gain_two_f, shift_two_f = (
        vectors[n][None] for n in range(6)
    )

    def up_bias(columns):
        return columns[:, 6:8].reshape(dp_size, rows, 2).transpose(0, 2, 1).reshape(1, -1)

    def qkv_bias(columns):
        parts = columns[:, 8].reshape(dp_size, 2, rows // 2).transpose(1, 0, 2).reshape(2, -1)
        return jnp.concatenate([parts[0], jnp.zeros_like(parts[0]), parts[1]])[None]

    wq = (qkv_own[:, : 3 * width], qkv_other[:, : 3 * width])
    wo = (up_own[:, :width], up_other[:, :width])
    wu = (up_own[:, width:], up_other[:, width:])
    wd = (down_own, down_other)

    proj = tuple(
        (mm(own_tokens, w, NN) + qkv_bias(s)).astype(BF)
        for w, s in zip(wq, (small_own, small_other))
    )
    tables = (table_own, table_other)
    ctx, probs = zip(*(attn_fwd(t, p) for t, p in zip(tables, proj)))
    attn_out = mm(ctx[0], wo[0], NT) + mm(ctx[1], wo[1], NT)
    resid_one = own_tokens.astype(F32) + attn_out + b_out_f
    z_one, inv_one = norm_parts(resid_one)
    normed_one = z_one * gain_one_f + shift_one_f
    normed_low = normed_one.astype(BF)
    hidden, slope = [], []
    for w, s in zip(wu, (small_own, small_other)):
        pre = mm(normed_low, w, NN) + up_bias(s)
        gelu, grad = gelu_both(pre)
        hidden.append(gelu.astype(BF))
        slope.append(grad.astype(BF))
    ffn_out = mm(hidden[0], wd[0], NT) + mm(hidden[1], wd[1], NT)
    resid_two = normed_one + ffn_out + b_down_f
    z_two, inv_two = norm_parts(resid_two)
    out_own = (z_two * gain_two_f + shift_two_f).astype(BF)
    out_other = swap_mp(out_own)

    cot = own_grad.astype(F32)
    g_gain_two = jnp.sum(cot * z_two, axis=0)
    g_shift_two = jnp.sum(cot, axis=0)
    d_two = norm_back(cot, z_two, inv_two, gain_two_f)
    d_two_low = d_two.astype(BF)
    g_b_down = jnp.sum(d_two, axis=0)
    g_down = [mm(d_two_low, h, TN).astype(BF) for h in hidden]
    s_down = reduce_scatter(where, *g_down, dp_size)
    d_pre = [(mm(d_two_low, w, NN) * s.astype(F32)).astype(BF) for w, s in zip(wd, slope)]
    g_b_up = [jnp.sum(d, axis=0, dtype=F32) for d in d_pre]
    g_up = [mm(normed_low, d, TN).astype(BF) for d in d_pre]
    d_normed = mm(d_pre[0], wu[0], NT) + mm(d_pre[1], wu[1], NT) + d_two
    g_gain_one = jnp.sum(d_normed * z_one, axis=0)
    g_shift_one = jnp.sum(d_normed, axis=0)
    d_one = norm_back(d_normed, z_one, inv_one, gain_one_f)
    d_one_low = d_one.astype(BF)
    g_b_out = jnp.sum(d_one, axis=0)
    g_out = [mm(d_one_low, c, TN).astype(BF) for c in ctx]
    s_up = reduce_scatter(
        where, *(jnp.concatenate([o, u], axis=1) for o, u in zip(g_out, g_up)), dp_size
    )
    d_ctx = [mm(d_one_low, w, NN).astype(BF) for w in wo]
    d_proj = [
        jnp.concatenate(attn_bwd(t, p, d, pr), axis=1)
        for t, p, d, pr in zip(tables, proj, d_ctx, probs)
    ]
    d_input = mm(d_proj[0], wq[0], NT) + mm(d_proj[1], wq[1], NT) + d_one
    in_other = swap_mp(d_input.astype(BF)).astype(F32)
    g_qkv = [mm(own_tokens, d, TN).astype(BF) for d in d_proj]

    shared = jnp.stack([g_b_out, g_gain_one, g_shift_one, g_b_down, g_gain_two, g_shift_two])

    def small_grads(g_up_bias, d):
        sums = jnp.sum(d, axis=0, dtype=F32)
        qv = jnp.stack([sums[:width], sums[2 * width :]]).reshape(2, dp_size, rows // 2)
        per_up = g_up_bias.reshape(dp_size, 2, rows).transpose(1, 0, 2).reshape(2, d_model)
        stacked = jnp.concatenate(
            [shared, per_up, qv.transpose(1, 0, 2).reshape(1, d_model)], axis=0
        )
        return jnp.pad(stacked, ((0, SMALL - stacked.shape[0]), (0, 0))).T.astype(BF)

    s_qkv = reduce_scatter(
        where,
        *(
            jnp.concatenate([g, small_grads(b, d)], axis=1)
            for g, b, d in zip(g_qkv, g_b_up, d_proj)
        ),
        dp_size,
    )

    def place(own, other):
        whole = jnp.zeros((2 * seq, d_model), own.dtype)
        whole = lax.dynamic_update_slice_in_dim(whole, own, mp_at * seq, 0)
        return lax.dynamic_update_slice_in_dim(whole, other, (1 - mp_at) * seq, 0)

    cols = s_qkv[:, 3 * width :].T
    return (
        place(out_own, out_other),
        place(d_input, in_other),
        s_qkv[:, : 3 * width].reshape(rows, 3, width),
        cols[8].reshape(2, rows // 2),
        s_up[:, :width].T,
        cols[0],
        cols[1],
        cols[2],
        s_up[:, width:],
        cols[6:8].reshape(-1),
        s_down.T,
        cols[3],
        cols[4],
        cols[5],
    )


def solution(mesh):
    placed = (
        P("dp", None),
        P("dp", None),
        P("dp", "mp"),
        P("dp", "mp", None),
        P("dp", None, "mp"),
        P(None, ("mp", "dp")),
        P("mp", "dp"),
        P("dp"),
        P("dp"),
        P("dp"),
        P("dp", "mp"),
        P(("mp", "dp")),
        P("mp", "dp"),
        P("dp"),
        P("dp"),
        P("dp"),
    )
    return jax.shard_map(
        functools.partial(body, mesh.shape["dp"]),
        mesh=mesh,
        in_specs=placed,
        out_specs=(
            P("dp", None),
            P("dp", None),
            P("dp", None, "mp"),
            P(None, ("mp", "dp")),
            P("mp", "dp"),
            P("dp"),
            P("dp"),
            P("dp"),
            P("dp", "mp"),
            P(("mp", "dp")),
            P("mp", "dp"),
            P("dp"),
            P("dp"),
            P("dp"),
        ),
        check_vma=False,
    )
```

```python
import functools

import jax
import jax.numpy as jnp
from jax import lax
from jax.experimental import pallas as pl
from jax.experimental.pallas import tpu as pltpu
from jax.sharding import PartitionSpec as P

HD = 64
PAIR = 2 * HD
BLOCK = 256
HALF = 2 * BLOCK
NORM_EPS = 1e-05
BF = jnp.bfloat16
F32 = jnp.float32
AXES = ("dp", "mp")
NN = (((1,), (0,)), ((), ()))
NT = (((1,), (1,)), ((), ()))
TN = (((0,), (0,)), ((), ()))
SMALL = 128


def mm(first, second, dims):
    return lax.dot_general(first, second, dims, preferred_element_type=F32)


def pairs_of(step):
    moves = []
    for d in range(16):
        for m in range(2):
            d2, m2 = step(d, m)
            moves.append((2 * d + m, 2 * d2 + m2))
    return moves


MOVE_X = pairs_of(lambda d, m: (d, 1 - m))
MOVE_Y = pairs_of(lambda d, m: (d ^ 2, m))
MOVE_CORE = pairs_of(lambda d, m: (d ^ 1, m))
MOVE_Z = [pairs_of(lambda d, m, k=k: ((d + 4 * k) % 16, m)) for k in (1, 2, 3)]
MOVE_FIRST = pairs_of(lambda d, m: (d ^ 2, m) if d & 1 else (d, 1 - m))
MOVE_SECOND = pairs_of(lambda d, m: (d, 1 - m) if d & 1 else (d ^ 2, m))


MOVE_REDUCE = MOVE_SECOND, MOVE_FIRST


def move(values, moves):
    return lax.ppermute(values, AXES, moves)


def swap_mp(values):
    return lax.ppermute(values, "mp", [(0, 1), (1, 0)])


def piece_copies(where, pieces, target, sem):
    if len(pieces) == 2:
        waits = [pltpu.make_async_copy(p, target.at[n], sem.at[n, 0]) for n, p in enumerate(pieces)]
        for copy in waits:
            copy.start()
        return waits
    rows = pieces[0].shape[1]
    z, y, core = where[0], where[1], where[2]
    z0, a0, b0, c0, z1, a1, b1, c1 = pieces
    first = core == 0

    def copies(ref, half, dy, dcore, slot):
        out = []
        for k in range(4):
            block = ((lax.rem(z + 4 - k, 4) * 2 + (y ^ dy)) * 2 + (core ^ dcore)) * rows
            block = pl.multiple_of(block, 16)
            out.append(
                pltpu.make_async_copy(
                    ref.at[k], target.at[half, pl.ds(block, rows), :], sem.at[slot, k]
                )
            )
        return out

    waits = []
    for slot, (ref, half, dy, dcore) in enumerate(
        ((z0, 0, 0, 0), (c0, 1, 1, 0), (z1, 0, 0, 1), (c1, 1, 1, 1))
    ):
        waits += copies(ref, half, dy, dcore, slot)
    for copy in waits:
        copy.start()
    for slot, (ref_if, ref_else, half, dy, dcore) in enumerate(
        ((b0, a0, 0, 1, 0), (a0, b0, 1, 0, 0), (a1, b1, 0, 1, 1), (b1, a1, 1, 0, 1)), 4
    ):
        @pl.when(first)
        def _(ref=ref_if, half=half, dy=dy, dcore=dcore, slot=slot):
            for copy in copies(ref, half, dy, dcore, slot):
                copy.start()

        @pl.when(jnp.logical_not(first))
        def _(ref=ref_else, half=half, dy=dy, dcore=dcore, slot=slot):
            for copy in copies(ref, half, dy, dcore, slot):
                copy.start()

        waits += copies(ref_if, half, dy, dcore, slot)
    return waits


def assemble_kernel(count, where, *refs):
    pieces, (own_ref, other_ref, target, sem) = refs[:count], refs[count:]
    for copy in piece_copies(where, pieces, target, sem):
        copy.wait()
    own_ref[...] = target[0]
    other_ref[...] = target[1]


def assemble(where, pieces):
    rows, cols = pieces[0].shape[1:]
    full = jax.ShapeDtypeStruct((16 * rows, cols), pieces[0].dtype)
    return pl.pallas_call(
        functools.partial(assemble_kernel, len(pieces)),
        out_shape=(full, full),
        grid_spec=pltpu.PrefetchScalarGridSpec(
            num_scalar_prefetch=1,
            grid=(1,),
            in_specs=[pl.BlockSpec(memory_space=pl.ANY)] * len(pieces),
            out_specs=[pl.BlockSpec((16 * rows, cols), lambda i, w: (0, 0))] * 2,
            scratch_shapes=[
                pltpu.VMEM((2, 16 * rows, cols), BF),
                pltpu.SemaphoreType.DMA((8, 4)),
            ],
        ),
        cost_estimate=pl.CostEstimate(
            flops=0, transcendentals=0, bytes_accessed=64 * rows * cols * 2
        ),
        name="assemble",
    )(where, *pieces)


def part_copies(where, result, half, keep_ref, send_ref, sem, staged):
    if not staged:
        return [pltpu.make_async_copy(result.at[half], keep_ref.at[half], sem.at[half, 0])]
    rows = keep_ref.shape[-2]
    z, y, core = where[0], where[1], where[2]
    out = []
    for dcore, target in enumerate((keep_ref, send_ref)):
        for dy in range(2):
            for k in range(4):
                block = ((lax.rem(z + k, 4) * 2 + (y ^ dy)) * 2 + (core ^ dcore)) * rows
                block = pl.multiple_of(block, 16)
                if target.shape[2] == 1:
                    place = target.at[dy, k, 0]
                else:
                    by_y = (core ^ dcore) == 0
                    place = target.at[jnp.where(by_y, dy, half), jnp.where(by_y, half, dy), k]
                out.append(
                    pltpu.make_async_copy(
                        result.at[half, pl.ds(block, rows), :], place, sem.at[half, len(out)]
                    )
                )
    return out


def part_shapes(staged, halves, d_model, cols):
    if not staged:
        whole = jax.ShapeDtypeStruct((halves, d_model, cols), BF)
        return whole, jax.ShapeDtypeStruct((8, 128), BF)
    rows = d_model // 16
    dims = (2, 4, 1, rows, cols) if halves == 1 else (2, 2, 4, rows, cols)
    return (jax.ShapeDtypeStruct(dims, BF),) * 2


def after(value, *others):
    return lax.optimization_barrier((value, *others))[0]


def grads_kernel(staged, halves, widths, where, *refs):
    count = len(widths)
    lhs_refs, refs = refs[:count], refs[count:]
    rhs_refs, refs = refs[: count * halves], refs[count * halves :]
    extra_ref, keep_ref, send_ref, result, turned, sem = refs
    for lhs, out in zip(lhs_refs, range(count)):
        for at in range(0, lhs.shape[0], BLOCK):
            turned[out, :, at : at + BLOCK] = lhs[at : at + BLOCK, :].T
    for half in range(halves):
        first = 0
        for n in range(count):
            rhs = rhs_refs[n * halves + half]
            rhs = rhs.at[half] if len(rhs.shape) == 3 else rhs
            width = rhs.shape[1]
            for at in range(0, width, 384):
                result[half, :, first + at : first + at + 384] = mm(
                    turned[n], rhs[:, at : at + 384], NN
                ).astype(BF)
            first += width
        result[half, :, first:] = extra_ref[half]
        for copy in part_copies(where, result, half, keep_ref, send_ref, sem, staged):
            copy.start()
    for half in range(halves):
        for copy in part_copies(where, result, half, keep_ref, send_ref, sem, staged):
            copy.wait()


def whole_spec(array):
    return pl.BlockSpec(array.shape, lambda i, w, n=array.ndim: (0,) * n)


def grads(where, staged, lhs, rhs, extra):
    seq, d_model = lhs[0].shape
    halves = extra.shape[0]
    widths = [r[0].shape[-1] for r in rhs]
    cols = sum(widths) + extra.shape[2]
    operands = [*lhs, *(r for pair in rhs for r in pair), extra]
    return pl.pallas_call(
        functools.partial(grads_kernel, staged, halves, widths),
        out_shape=part_shapes(staged, halves, d_model, cols),
        grid_spec=pltpu.PrefetchScalarGridSpec(
            num_scalar_prefetch=1,
            grid=(1,),
            in_specs=[whole_spec(o) for o in operands],
            out_specs=[pl.BlockSpec(memory_space=pl.ANY)] * 2,
            scratch_shapes=[
                pltpu.VMEM((halves, d_model, cols), BF),
                pltpu.VMEM((len(lhs), d_model, seq), BF),
                pltpu.SemaphoreType.DMA((halves, 16)),
            ],
        ),
        cost_estimate=pl.CostEstimate(
            flops=2 * seq * d_model * halves * sum(widths),
            transcendentals=0,
            bytes_accessed=halves * (seq + d_model) * cols * 2,
        ),
        name="grads",
    )(where, *operands)


def row_norm(values):
    centered = values - jnp.mean(values, axis=-1, keepdims=True)
    inverse = lax.rsqrt(jnp.mean(centered * centered, axis=-1, keepdims=True) + NORM_EPS)
    return centered * inverse, inverse


def row_norm_back(d_normed, z, inverse, gain):
    dz = d_normed * gain
    return (
        dz - jnp.mean(dz, axis=-1, keepdims=True) - z * jnp.mean(dz * z, axis=-1, keepdims=True)
    ) * inverse


def column_sum(values):
    return jnp.sum(values, axis=0, keepdims=True)


def first_kernel(n_up, where, tok_ref, ctx0_ref, ctx1_ref, vec_ref, bias_ref, *refs):
    pieces = refs[:n_up]
    z_ref, inv_ref, hid_ref, slope_ref, weights, sem = refs[n_up:]
    width = ctx0_ref.shape[1]

    @pl.when(pl.program_id(0) == 0)
    def _():
        for copy in piece_copies(where, pieces, weights, sem):
            copy.wait()

    resid = (
        tok_ref[...].astype(F32)
        + mm(ctx0_ref[...], weights[0, :, :width], NT)
        + mm(ctx1_ref[...], weights[1, :, :width], NT)
        + vec_ref[0:1]
    )
    z, inverse = row_norm(resid)
    z_ref[...] = z
    inv_ref[...] = jnp.broadcast_to(inverse, inv_ref.shape)
    low = (z * vec_ref[1:2] + vec_ref[2:3]).astype(BF)
    ff = hid_ref.shape[2]
    for half in range(2):
        for at in range(0, ff, 512):
            pre = mm(low, weights[half, :, width + at : width + at + 512], NN)
            gelu, slope = gelu_both(pre + bias_ref[half, :, at : at + 512])
            hid_ref[half, :, at : at + 512] = gelu.astype(BF)
            slope_ref[half, :, at : at + 512] = slope.astype(BF)


def row_tile(tile, width):
    return pl.BlockSpec((tile, width), lambda i, w: (i, 0))


def halves_tile(tile, width):
    return pl.BlockSpec((2, tile, width), lambda i, w: (0, i, 0))


ANYWHERE = pl.BlockSpec(memory_space=pl.ANY)


def first_part(where, tokens, ctx, vectors, bias, pieces, tile=256):
    seq, d_model = tokens.shape
    width, ff = ctx[0].shape[1], bias.shape[2]
    return pl.pallas_call(
        functools.partial(first_kernel, len(pieces)),
        out_shape=(
            jax.ShapeDtypeStruct((seq, d_model), F32),
            jax.ShapeDtypeStruct((seq, 128), F32),
            jax.ShapeDtypeStruct((2, seq, ff), BF),
            jax.ShapeDtypeStruct((2, seq, ff), BF),
        ),
        grid_spec=pltpu.PrefetchScalarGridSpec(
            num_scalar_prefetch=1,
            grid=(seq // tile,),
            in_specs=[
                row_tile(tile, d_model),
                row_tile(tile, width),
                row_tile(tile, width),
                whole_spec(vectors),
                whole_spec(bias),
            ]
            + [ANYWHERE] * len(pieces),
            out_specs=[
                row_tile(tile, d_model),
                row_tile(tile, 128),
                halves_tile(tile, ff),
                halves_tile(tile, ff),
            ],
            scratch_shapes=[
                pltpu.VMEM((2, d_model, width + ff), BF),
                pltpu.SemaphoreType.DMA((8, 4)),
            ],
        ),
        cost_estimate=pl.CostEstimate(
            flops=2 * seq * d_model * 2 * (width + ff),
            transcendentals=seq * 2 * ff * 2,
            bytes_accessed=seq * (d_model * 8 + ff * 8) + d_model * 4 * (width + ff),
        ),
        name="first_part",
    )(where, tokens, *ctx, vectors, bias, *pieces)


def second_kernel(staged, n_down, where, hid_ref, z_ref, cot_ref, vec_ref, *refs):
    pieces = refs[:n_down]
    out_ref, d_ref, sum_ref, keep_ref, send_ref, weights, turned, kept, result, sem, out_sem = refs[
        n_down:
    ]
    step = pl.program_id(0)
    tile, ff = hid_ref.shape[1:]

    @pl.when(step == 0)
    def _():
        for copy in piece_copies(where, pieces, weights, sem):
            copy.wait()
        sum_ref[...] = jnp.zeros_like(sum_ref)

    ffn = mm(hid_ref[0], weights[0], NT) + mm(hid_ref[1], weights[1], NT)
    resid = z_ref[...] * vec_ref[1:2] + vec_ref[2:3] + ffn + vec_ref[3:4]
    z, inverse = row_norm(resid)
    out_ref[...] = (z * vec_ref[4:5] + vec_ref[5:6]).astype(BF)
    cot = cot_ref[...].astype(F32)
    d_two = row_norm_back(cot, z, inverse, vec_ref[4:5])
    d_ref[...] = d_two
    sum_ref[0:1] += column_sum(cot * z)
    sum_ref[1:2] += column_sum(cot)
    sum_ref[2:3] += column_sum(d_two)
    rows = pl.ds(pl.multiple_of(step * tile, tile), tile)
    turned[:, rows] = d_two.astype(BF).T
    kept[:, rows, :] = hid_ref[...]

    @pl.when(step == pl.num_programs(0) - 1)
    def _():
        for half in range(2):
            for at in range(0, ff, 512):
                result[half, :, at : at + 512] = mm(
                    turned[...], kept[half, :, at : at + 512], NN
                ).astype(BF)
            for copy in part_copies(where, result, half, keep_ref, send_ref, out_sem, staged):
                copy.start()
        for half in range(2):
            for copy in part_copies(where, result, half, keep_ref, send_ref, out_sem, staged):
                copy.wait()


def second_part(where, staged, hidden, z_one, cot, vectors, pieces, tile=256):
    _, seq, ff = hidden.shape
    d_model = z_one.shape[1]
    return pl.pallas_call(
        functools.partial(second_kernel, staged, len(pieces)),
        out_shape=(
            jax.ShapeDtypeStruct((seq, d_model), BF),
            jax.ShapeDtypeStruct((seq, d_model), F32),
            jax.ShapeDtypeStruct((8, d_model), F32),
            *part_shapes(staged, 2, d_model, ff),
        ),
        grid_spec=pltpu.PrefetchScalarGridSpec(
            num_scalar_prefetch=1,
            grid=(seq // tile,),
            in_specs=[
                halves_tile(tile, ff),
                row_tile(tile, d_model),
                row_tile(tile, d_model),
                whole_spec(vectors),
            ]
            + [ANYWHERE] * len(pieces),
            out_specs=[
                row_tile(tile, d_model),
                row_tile(tile, d_model),
                pl.BlockSpec((8, d_model), lambda i, w: (0, 0)),
                ANYWHERE,
                ANYWHERE,
            ],
            scratch_shapes=[
                pltpu.VMEM((2, d_model, ff), BF),
                pltpu.VMEM((d_model, seq), BF),
                pltpu.VMEM((2, seq, ff), BF),
                pltpu.VMEM((2, d_model, ff), BF),
                pltpu.SemaphoreType.DMA((8, 4)),
                pltpu.SemaphoreType.DMA((2, 16)),
            ],
        ),
        cost_estimate=pl.CostEstimate(
            flops=2 * seq * d_model * 4 * ff,
            transcendentals=seq,
            bytes_accessed=seq * (d_model * 12 + ff * 4) + d_model * 8 * ff,
        ),
        name="second_part",
    )(where, hidden, z_one, cot, vectors, *pieces)


def third_kernel(n_up, where, d_ref, slope_ref, z_ref, inv_ref, vec_ref, *refs):
    up_pieces, down_pieces = refs[:n_up], refs[n_up : 2 * n_up]
    pre_ref, low_ref, one_ref, ctx_ref, sum_ref, bias_ref, up, down, sem, down_sem = refs[2 * n_up :]
    step = pl.program_id(0)
    ff = slope_ref.shape[2]
    width = ctx_ref.shape[2]

    @pl.when(step == 0)
    def _():
        waits = piece_copies(where, down_pieces, down, down_sem)
        waits += piece_copies(where, up_pieces, up, sem)
        for copy in waits:
            copy.wait()
        sum_ref[...] = jnp.zeros_like(sum_ref)
        bias_ref[...] = jnp.zeros_like(bias_ref)

    d_two = d_ref[...]
    d_two_low = d_two.astype(BF)
    d_normed = d_two
    for half in range(2):
        for at in range(0, ff, 512):
            span = slice(at, at + 512)
            d_pre = mm(d_two_low, down[half, :, span], NN) * slope_ref[half, :, span].astype(F32)
            d_pre = d_pre.astype(BF)
            pre_ref[half, :, span] = d_pre
            bias_ref[half, 0:1, span] += column_sum(d_pre.astype(F32))
            d_normed = d_normed + mm(d_pre, up[half, :, width + at : width + at + 512], NT)
    z = z_ref[...]
    low_ref[...] = (z * vec_ref[1:2] + vec_ref[2:3]).astype(BF)
    d_one = row_norm_back(d_normed, z, inv_ref[:, 0:1], vec_ref[1:2])
    one_ref[...] = d_one
    sum_ref[0:1] += column_sum(d_normed * z)
    sum_ref[1:2] += column_sum(d_normed)
    sum_ref[2:3] += column_sum(d_one)
    d_one_low = d_one.astype(BF)
    for half in range(2):
        ctx_ref[half] = mm(d_one_low, up[half, :, :width], NN).astype(BF)


def third_part(where, d_two, slope, z_one, inv_one, vectors, up_pieces, down_pieces, width, tile=256):
    seq, d_model = d_two.shape
    ff = slope.shape[2]
    return pl.pallas_call(
        functools.partial(third_kernel, len(up_pieces)),
        out_shape=(
            jax.ShapeDtypeStruct((2, seq, ff), BF),
            jax.ShapeDtypeStruct((seq, d_model), BF),
            jax.ShapeDtypeStruct((seq, d_model), F32),
            jax.ShapeDtypeStruct((2, seq, width), BF),
            jax.ShapeDtypeStruct((8, d_model), F32),
            jax.ShapeDtypeStruct((2, 8, ff), F32),
        ),
        grid_spec=pltpu.PrefetchScalarGridSpec(
            num_scalar_prefetch=1,
            grid=(seq // tile,),
            in_specs=[
                row_tile(tile, d_model),
                halves_tile(tile, ff),
                row_tile(tile, d_model),
                row_tile(tile, 128),
                whole_spec(vectors),
            ]
            + [ANYWHERE] * (2 * len(up_pieces)),
            out_specs=[
                halves_tile(tile, ff),
                row_tile(tile, d_model),
                row_tile(tile, d_model),
                halves_tile(tile, width),
                pl.BlockSpec((8, d_model), lambda i, w: (0, 0)),
                pl.BlockSpec((2, 8, ff), lambda i, w: (0, 0, 0)),
            ],
            scratch_shapes=[
                pltpu.VMEM((2, d_model, width + ff), BF),
                pltpu.VMEM((2, d_model, ff), BF),
                pltpu.SemaphoreType.DMA((8, 4)),
                pltpu.SemaphoreType.DMA((8, 4)),
            ],
        ),
        cost_estimate=pl.CostEstimate(
            flops=2 * seq * d_model * 2 * (2 * ff + width),
            transcendentals=0,
            bytes_accessed=seq * (d_model * 14 + ff * 8) + d_model * 4 * (2 * ff + width),
        ),
        name="third_part",
    )(where, d_two, slope, z_one, inv_one, vectors, *up_pieces, *down_pieces)


def add(first, second):
    return (first.astype(F32) + second.astype(F32)).astype(BF)


def core_stage(keep, send):
    return move(send, MOVE_CORE), keep


def flip_stage(moves, got, keep):
    return move(add(keep[1], got[1]), moves), add(keep[0], got[0])


def z_stage(got, keep):
    parts = [move(add(keep[k], got[k]), moves) for k, moves in zip((1, 2, 3), MOVE_Z)]
    return parts, keep[0].astype(F32) + got[0].astype(F32)


def z_sum(parts, keep):
    return keep + parts[0].astype(F32) + parts[1].astype(F32) + parts[2].astype(F32)


def lane_mask(head, rows):
    lanes = lax.broadcasted_iota(jnp.int32, (rows, PAIR), 1)
    return (lanes < HD) if head == 0 else (lanes >= HD)


def attn_fwd_kernel(table, qkv_ref, ctx_ref, prob_ref):
    pair = pl.program_id(0)
    q_ref, k_ref, v_ref = (qkv_ref.at[:, n * PAIR : (n + 1) * PAIR] for n in range(3))
    lanes = lax.broadcasted_iota(jnp.int32, (1, HALF), 1)
    for half in range(2):
        rows = pl.ds(half * HALF, HALF)
        query = q_ref[rows, :] * jnp.asarray(HD**-0.5, BF)
        parts = []
        for head in range(2):
            at = (pair * 2 + head) * 4
            start = (half ^ table[at]) * HALF
            flags = [table[at + 1 + n] == 1 for n in range(3)]
            key_lo = k_ref[pl.ds(pl.multiple_of(start, BLOCK), BLOCK), :]
            key_hi = k_ref[pl.ds(pl.multiple_of(start + BLOCK, BLOCK), BLOCK), :]
            masked = jnp.where(lane_mask(head, HALF), query, jnp.zeros_like(query))
            score_lo = mm(key_lo, masked, NT)
            score_hi = mm(key_hi, masked[BLOCK:], NT)
            no_lo = jnp.where(
                lanes < BLOCK,
                jnp.where(flags[0], 0.0, -1e30),
                jnp.where(flags[1], 0.0, -1e30),
            ).astype(F32)
            no_hi = jnp.where(flags[2], 0.0, -1e30).astype(F32)
            top_lo = jnp.max(score_lo, axis=0, keepdims=True) + no_lo
            top_hi = jnp.max(score_hi, axis=0, keepdims=True) + no_hi
            top = jnp.concatenate(
                [top_lo[:, :BLOCK], jnp.maximum(top_lo[:, BLOCK:], top_hi)], axis=1
            )
            ref_lo = jnp.where(no_lo < 0.0, 1e30, top)
            ref_hi = jnp.where(no_hi < 0.0, 1e30, top[:, BLOCK:])
            exp_lo = jnp.exp(score_lo - ref_lo)
            exp_hi = jnp.exp(score_hi - ref_hi)
            sum_lo = jnp.sum(exp_lo, axis=0, keepdims=True)
            sum_hi = jnp.sum(exp_hi, axis=0, keepdims=True)
            total = jnp.concatenate([sum_lo[:, :BLOCK], sum_lo[:, BLOCK:] + sum_hi], axis=1)
            scale = jnp.where(total > 0.0, 1.0 / jnp.where(total > 0.0, total, 1.0), 0.0)
            prob_lo = (exp_lo * scale).astype(BF)
            prob_hi = (exp_hi * scale[:, BLOCK:]).astype(BF)
            prob_ref[0, head, half, :, :HALF] = prob_lo
            prob_ref[0, head, half, :, HALF:] = prob_hi
            val_lo = v_ref[pl.ds(pl.multiple_of(start, BLOCK), BLOCK), :].T
            val_hi = v_ref[pl.ds(pl.multiple_of(start + BLOCK, BLOCK), BLOCK), :].T
            side = slice(head * HD, (head + 1) * HD)
            out_lo = mm(val_lo[side], prob_lo, NN)
            out_hi = mm(val_hi[side], prob_hi, NN)
            parts.append(
                jnp.concatenate([out_lo[:, :BLOCK], out_lo[:, BLOCK:] + out_hi], axis=1)
            )
        ctx_ref[rows, :] = jnp.concatenate(parts, axis=0).T.astype(BF)


def attn_fwd(table, proj):
    seq, width = proj.shape
    pairs = width // 3 // PAIR
    return pl.pallas_call(
        attn_fwd_kernel,
        out_shape=(
            jax.ShapeDtypeStruct((seq, width // 3), BF),
            jax.ShapeDtypeStruct((pairs, 2, 2, BLOCK, HALF + BLOCK), BF),
        ),
        grid_spec=pltpu.PrefetchScalarGridSpec(
            num_scalar_prefetch=1,
            grid=(pairs,),
            in_specs=[pl.BlockSpec((seq, 3 * PAIR), lambda p, t: (0, p))],
            out_specs=[
                pl.BlockSpec((seq, PAIR), lambda p, t: (0, p)),
                pl.BlockSpec((1, 2, 2, BLOCK, HALF + BLOCK), lambda p, t: (p, 0, 0, 0, 0)),
            ],
        ),
        cost_estimate=pl.CostEstimate(
            flops=pairs * 4 * 2 * 2 * 3 * BLOCK * BLOCK * PAIR,
            transcendentals=pairs * 4 * 3 * BLOCK * BLOCK,
            bytes_accessed=pairs * 4 * 3 * BLOCK * BLOCK * 2 + seq * width * 3,
        ),
        name="attn_fwd",
    )(table, proj)


def attn_bwd_kernel(table, qkv_ref, d_ref, prob_ref, out_ref, sum_ref, k_acc, v_acc):
    pair = pl.program_id(0)
    q_ref, k_ref, v_ref = (qkv_ref.at[:, n * PAIR : (n + 1) * PAIR] for n in range(3))
    for half in range(2):
        rows = pl.ds(half * HALF, HALF)
        query = q_ref[rows, :] * jnp.asarray(HD**-0.5, BF)
        d_ctx = d_ref[rows, :]
        parts = []
        for head in range(2):
            at = (pair * 2 + head) * 4
            start = (half ^ table[at]) * HALF
            at_lo = pl.ds(pl.multiple_of(start, BLOCK), BLOCK)
            at_hi = pl.ds(pl.multiple_of(start + BLOCK, BLOCK), BLOCK)
            keep = lane_mask(head, HALF)
            query_h = jnp.where(keep, query, jnp.zeros_like(query))
            d_ctx_h = jnp.where(keep, d_ctx, jnp.zeros_like(d_ctx))
            prob_lo = prob_ref[0, head, half, :, :HALF]
            prob_hi = prob_ref[0, head, half, :, HALF:]
            d_w_lo = mm(v_ref[at_lo, :], d_ctx_h, NT)
            d_w_hi = mm(v_ref[at_hi, :], d_ctx_h[BLOCK:], NT)
            wide_lo = prob_lo.astype(F32)
            wide_hi = prob_hi.astype(F32)
            dot_lo = jnp.sum(wide_lo * d_w_lo, axis=0, keepdims=True)
            dot_hi = jnp.sum(wide_hi * d_w_hi, axis=0, keepdims=True)
            dot = jnp.concatenate([dot_lo[:, :BLOCK], dot_lo[:, BLOCK:] + dot_hi], axis=1)
            d_s_lo = (wide_lo * (d_w_lo - dot)).astype(BF)
            d_s_hi = (wide_hi * (d_w_hi - dot[:, BLOCK:])).astype(BF)
            dk_lo = mm(d_s_lo, query_h, NN)
            dk_hi = mm(d_s_hi, query_h[BLOCK:], NN)
            dv_lo = mm(prob_lo, d_ctx_h, NN)
            dv_hi = mm(prob_hi, d_ctx_h[BLOCK:], NN)
            k_acc[head, at_lo, :] = dk_lo
            k_acc[head, at_hi, :] = dk_hi
            v_acc[head, at_lo, :] = dv_lo
            v_acc[head, at_hi, :] = dv_hi
            key_lo = k_ref[at_lo, :].T
            key_hi = k_ref[at_hi, :].T
            side = slice(head * HD, (head + 1) * HD)
            dq_lo = mm(key_lo[side], d_s_lo, NN)
            dq_hi = mm(key_hi[side], d_s_hi, NN)
            parts.append(jnp.concatenate([dq_lo[:, :BLOCK], dq_lo[:, BLOCK:] + dq_hi], axis=1))
        out_ref[rows, :PAIR] = (jnp.concatenate(parts, axis=0).T * HD**-0.5).astype(BF)
    out_ref[:, PAIR : 2 * PAIR] = (k_acc[0] + k_acc[1]).astype(BF)
    out_ref[:, 2 * PAIR :] = (v_acc[0] + v_acc[1]).astype(BF)
    sums = jnp.sum(out_ref[...].astype(F32), axis=0, keepdims=True)
    sum_ref[0] = jnp.broadcast_to(sums, sum_ref.shape[1:])


def attn_bwd(table, proj, d_context, probs):
    seq, width = proj.shape
    pairs = width // 3 // PAIR
    return pl.pallas_call(
        attn_bwd_kernel,
        out_shape=(
            jax.ShapeDtypeStruct((seq, width), BF),
            jax.ShapeDtypeStruct((pairs, 8, 3 * PAIR), F32),
        ),
        grid_spec=pltpu.PrefetchScalarGridSpec(
            num_scalar_prefetch=1,
            grid=(pairs,),
            in_specs=[
                pl.BlockSpec((seq, 3 * PAIR), lambda p, t: (0, p)),
                pl.BlockSpec((seq, PAIR), lambda p, t: (0, p)),
                pl.BlockSpec((1, 2, 2, BLOCK, HALF + BLOCK), lambda p, t: (p, 0, 0, 0, 0)),
            ],
            out_specs=[
                pl.BlockSpec((seq, 3 * PAIR), lambda p, t: (0, p)),
                pl.BlockSpec((1, 8, 3 * PAIR), lambda p, t: (p, 0, 0)),
            ],
            scratch_shapes=[pltpu.VMEM((2, seq, PAIR), F32)] * 2,
        ),
        cost_estimate=pl.CostEstimate(
            flops=pairs * 4 * 4 * 2 * 3 * BLOCK * BLOCK * PAIR,
            transcendentals=0,
            bytes_accessed=pairs * 4 * 3 * BLOCK * BLOCK * 2 + seq * width * 5,
        ),
        name="attn_bwd",
    )(table, proj, d_context, probs)


def gelu_both(values):
    half = 0.5 * (1.0 + lax.erf(values * (0.5**0.5)))
    slope = half + values * jnp.exp(-0.5 * values * values) * 0.3989422804014327
    return values * half, slope


def body(
    dp_size,
    tokens,
    grad_out,
    head_perm,
    block_mask,
    w_qkv,
    b_qv,
    w_out,
    b_out,
    gain_one,
    shift_one,
    w_up,
    b_up,
    w_down,
    b_down,
    gain_two,
    shift_two,
):
    seq = tokens.shape[0] // head_perm.shape[0]
    rows = w_qkv.shape[0]
    width = w_qkv.shape[2]
    d_model = tokens.shape[1]
    dp_at = lax.axis_index("dp")
    mp_at = lax.axis_index("mp")
    where = jnp.stack([dp_at // 4, (dp_at // 2) % 2, dp_at % 2]).astype(jnp.int32)

    own_tokens = lax.dynamic_slice_in_dim(tokens, mp_at * seq, seq, 0)
    own_grad = lax.dynamic_slice_in_dim(grad_out, mp_at * seq, seq, 0)
    table = jnp.concatenate([head_perm[:, :, None], block_mask], axis=2).astype(jnp.int32)
    table = table.reshape(2, -1)
    table_own = lax.dynamic_index_in_dim(table, mp_at, 0, keepdims=False)
    table_other = swap_mp(lax.dynamic_index_in_dim(table, 1 - mp_at, 0, keepdims=False))

    small = jnp.stack(
        [
            b_out,
            gain_one,
            shift_one,
            b_down,
            gain_two,
            shift_two,
            b_up[:rows],
            b_up[rows:],
            b_qv.reshape(-1),
        ],
        axis=1,
    )
    small = jnp.pad(small, ((0, 0), (0, SMALL - small.shape[1])))
    pairs = width // PAIR
    by_pair = w_qkv.reshape(rows, 3, pairs, PAIR).transpose(0, 2, 1, 3).reshape(rows, 3 * width)
    shard_qkv = jnp.concatenate([by_pair, small], axis=1)
    shard_up = jnp.concatenate([w_out.T, w_up], axis=1)
    shard_down = w_down.T
    staged = dp_size == 16

    def plain_gather(shard):
        full = lax.all_gather(shard, "dp", axis=0, tiled=True)
        return full, swap_mp(full)

    def gather_z(shard):
        return jnp.stack([shard] + [move(shard, moves) for moves in MOVE_Z])

    def gather_core(*pieces):
        return (*pieces, *(move(piece, MOVE_CORE) for piece in pieces))

    if staged:
        qkv_z = gather_z(shard_qkv)
        qkv_a = move(qkv_z, MOVE_FIRST)
        up_z = gather_z(after(shard_up, qkv_z))
        qkv_b, qkv_c = move(qkv_z, MOVE_SECOND), move(qkv_a, MOVE_SECOND)
        up_z, down_in = lax.optimization_barrier((up_z, shard_down))
        down_z = gather_z(down_in)
        up_a = move(after(up_z, qkv_b, qkv_c), MOVE_FIRST)
        qkv_own, qkv_other = assemble(where, gather_core(qkv_z, qkv_a, qkv_b, qkv_c))
    else:
        qkv_own, qkv_other = plain_gather(shard_qkv)

    small_own = qkv_own[:, 3 * width :].astype(F32)
    small_other = qkv_other[:, 3 * width :].astype(F32)
    vectors = small_own.T[:8]

    def up_bias(columns):
        return columns[:, 6:8].reshape(dp_size, rows, 2).transpose(0, 2, 1).reshape(1, -1)

    def qkv_bias(columns):
        parts = columns[:, 8].reshape(dp_size, 2, rows // 2).transpose(1, 0, 2)
        parts = parts.reshape(2, pairs, PAIR)
        return jnp.stack([parts[0], jnp.zeros_like(parts[0]), parts[1]], axis=1).reshape(1, -1)

    wq = (qkv_own[:, : 3 * width], qkv_other[:, : 3 * width])
    bias_up = jnp.stack([up_bias(small_own), up_bias(small_other)])

    def project(w, s):
        return (mm(own_tokens, w, NN) + qkv_bias(s)).astype(BF)

    proj_own = project(wq[0], small_own)
    if staged:
        table_own, up_a = lax.optimization_barrier((table_own, up_a))
        up_b, up_c = move(up_z, MOVE_SECOND), move(up_a, MOVE_SECOND)
    ctx_own, probs_own = attn_fwd(table_own, proj_own)
    proj_other = project(after(wq[1], ctx_own), small_other)
    if staged:
        table_other, up_b, up_c, down_z, proj_other = lax.optimization_barrier(
            (table_other, up_b, up_c, down_z, proj_other)
        )
        down_a = move(down_z, MOVE_FIRST)
        up_pieces = gather_core(up_z, up_a, up_b, up_c)
    else:
        up_pieces = plain_gather(shard_up)
    ctx_other, probs_other = attn_fwd(table_other, proj_other)
    tables, proj = (table_own, table_other), (proj_own, proj_other)
    probs = (probs_own, probs_other)
    if staged:
        down_a, ctx_other = lax.optimization_barrier((down_a, ctx_other))
        down_b, down_c = move(down_z, MOVE_SECOND), move(down_a, MOVE_SECOND)
    ctx = (ctx_own, ctx_other)
    z_one, inv_one, hidden, slope = first_part(where, own_tokens, ctx, vectors, bias_up, up_pieces)
    if staged:
        hidden, down_b, down_c = lax.optimization_barrier((hidden, down_b, down_c))
        down_pieces = gather_core(down_z, down_a, down_b, down_c)
    else:
        down_pieces = plain_gather(shard_down)

    out_own, d_two, sums_two, *down_parts = second_part(
        where, staged, hidden, z_one, own_grad, vectors, down_pieces
    )
    out_other = swap_mp(out_own)

    def plain_scatter(whole):
        own, other = (whole[0], whole[1]) if isinstance(whole, tuple) else whole
        summed = own.astype(F32) + swap_mp(other).astype(F32)
        return lax.psum_scatter(summed, "dp", scatter_dimension=0, tiled=True)

    if staged:
        down_got, down_keep = core_stage(*down_parts)
        d_two, down_got = lax.optimization_barrier((d_two, down_got))
        down_got, down_keep = flip_stage(MOVE_REDUCE[0], down_got, down_keep)
    else:
        s_down = plain_scatter(down_parts[0])
    d_pre, normed_low, d_one, d_ctx, sums_one, sums_up = third_part(
        where, d_two, slope, z_one, inv_one, vectors, up_pieces, down_pieces, width
    )
    d_one_low = d_one.astype(BF)
    shared = jnp.concatenate(
        [sums_one[2:3], sums_one[0:2], sums_two[2:3], sums_two[0:2]], axis=0
    )

    def columns(stacked):
        return jnp.pad(stacked, ((0, SMALL - stacked.shape[0]), (0, 0))).T.astype(BF)

    def vector_grads(g_up_bias):
        per_up = g_up_bias.reshape(dp_size, 2, rows).transpose(1, 0, 2).reshape(2, d_model)
        return columns(jnp.concatenate([shared, per_up], axis=0))

    def qv_grads(sums):
        sums = sums[:, 0].reshape(pairs, 3, PAIR).transpose(1, 0, 2).reshape(3, width)
        qv = jnp.stack([sums[0], sums[2]]).reshape(2, dp_size, rows // 2)
        return columns(qv.transpose(1, 0, 2).reshape(1, d_model))

    small_up = jnp.stack([vector_grads(sums_up[n, 0]) for n in range(2)])
    up_parts = grads(
        where, staged, [normed_low, d_one_low], [(d_pre, d_pre), ctx], small_up
    )
    if staged:
        up_got, up_keep = core_stage(*up_parts)
        table_other, down_got, up_keep = lax.optimization_barrier((tables[1], down_got, up_keep))
        down_got, down_keep = flip_stage(MOVE_REDUCE[1], down_got, down_keep)
        tables = (tables[0], table_other)
    else:
        s_up = plain_scatter(up_parts[0])
    d_proj_other, sums_other = attn_bwd(tables[1], proj[1], d_ctx[1], probs[1])
    small_qkv_other = qv_grads(sums_other)
    other_parts = grads(where, staged, [own_tokens], [(d_proj_other,)], small_qkv_other[None])
    if staged:
        qo_got, qo_keep = core_stage(*other_parts)
        table_own, up_got, down_got, qo_keep = lax.optimization_barrier(
            (tables[0], up_got, down_got, qo_keep)
        )
        down_parts, down_keep = z_stage(down_got, down_keep)
        up_got, up_keep = flip_stage(MOVE_REDUCE[0], up_got, up_keep)
        tables = (table_own, tables[1])
    d_proj_own, sums_own = attn_bwd(tables[0], proj[0], d_ctx[0], probs[0])
    small_qkv_own = qv_grads(sums_own)
    if staged:
        d_proj_own, qo_got, up_got = lax.optimization_barrier((d_proj_own, qo_got, up_got))
        up_got, up_keep = flip_stage(MOVE_REDUCE[1], up_got, up_keep)
        qo_got, qo_keep = flip_stage(MOVE_Y, qo_got, qo_keep)
    d_input = mm(d_proj_own, wq[0], NT) + mm(d_proj_other, wq[1], NT) + d_one
    in_low = d_input.astype(BF)
    tokens_in = own_tokens
    if staged:
        in_low, tokens_in = lax.optimization_barrier((in_low, own_tokens))
    in_other = swap_mp(in_low).astype(F32)
    own_parts = grads(where, staged, [tokens_in], [(d_proj_own,)], small_qkv_own[None])
    if staged:
        qs_got, qs_keep = core_stage(*own_parts)
        s_down = z_sum(down_parts, down_keep)
        up_parts, up_keep = z_stage(up_got, up_keep)
        qs_got, qs_keep = flip_stage(MOVE_Y, qs_got, qs_keep)
        qo_parts, qo_keep = z_stage(qo_got, qo_keep)
        s_up = z_sum(up_parts, up_keep)
        qo_sum = move(z_sum(qo_parts, qo_keep).astype(BF), MOVE_X)
        qs_parts, qs_keep = z_stage(qs_got, qs_keep)
        s_qkv = (z_sum(qs_parts, qs_keep) + qo_sum.astype(F32))[0]
    else:
        s_qkv = plain_scatter((own_parts[0][0], other_parts[0][0]))

    def place(own, other):
        whole = jnp.zeros((2 * seq, d_model), own.dtype)
        whole = lax.dynamic_update_slice_in_dim(whole, own, mp_at * seq, 0)
        return lax.dynamic_update_slice_in_dim(whole, other, (1 - mp_at) * seq, 0)

    ff = w_up.shape[1]
    cols = s_up[:, ff + width :].T
    g_w_qkv = s_qkv[:, : 3 * width].reshape(rows, pairs, 3, PAIR).transpose(0, 2, 1, 3)
    return (
        place(out_own, out_other),
        place(d_input, in_other),
        g_w_qkv.reshape(rows, 3, width),
        s_qkv[:, 3 * width].reshape(2, rows // 2),
        s_up[:, ff : ff + width].T,
        cols[0],
        cols[1],
        cols[2],
        s_up[:, :ff],
        cols[6:8].reshape(-1),
        s_down.T,
        cols[3],
        cols[4],
        cols[5],
    )


def solution(mesh):
    placed = (
        P("dp", None),
        P("dp", None),
        P("dp", "mp"),
        P("dp", "mp", None),
        P("dp", None, "mp"),
        P(None, ("mp", "dp")),
        P("mp", "dp"),
        P("dp"),
        P("dp"),
        P("dp"),
        P("dp", "mp"),
        P(("mp", "dp")),
        P("mp", "dp"),
        P("dp"),
        P("dp"),
        P("dp"),
    )
    return jax.shard_map(
        functools.partial(body, mesh.shape["dp"]),
        mesh=mesh,
        in_specs=placed,
        out_specs=(
            P("dp", None),
            P("dp", None),
            P("dp", None, "mp"),
            P(None, ("mp", "dp")),
            P("mp", "dp"),
            P("dp"),
            P("dp"),
            P("dp"),
            P("dp", "mp"),
            P(("mp", "dp")),
            P("mp", "dp"),
            P("dp"),
            P("dp"),
            P("dp"),
        ),
        check_vma=False,
    )
```

```python
import functools

import jax
import jax.numpy as jnp
from jax import lax
from jax.experimental import pallas as pl
from jax.experimental.pallas import tpu as pltpu
from jax.sharding import PartitionSpec as P

HD = 64
PAIR = 2 * HD
BLOCK = 256
HALF = 2 * BLOCK
NORM_EPS = 1e-05
BF = jnp.bfloat16
F32 = jnp.float32
AXES = ("dp", "mp")
NN = (((1,), (0,)), ((), ()))
NT = (((1,), (1,)), ((), ()))
TN = (((0,), (0,)), ((), ()))
SMALL = 128


def mm(first, second, dims):
    return lax.dot_general(first, second, dims, preferred_element_type=F32)


def cost(microseconds):
    return pl.CostEstimate(
        flops=int(microseconds * 4 * 1e9),
        transcendentals=0,
        bytes_accessed=int(microseconds * 4 * 3e6),
    )


def pairs_of(step):
    moves = []
    for d in range(16):
        for m in range(2):
            d2, m2 = step(d, m)
            moves.append((2 * d + m, 2 * d2 + m2))
    return moves


MOVE_X = pairs_of(lambda d, m: (d, 1 - m))
MOVE_Y = pairs_of(lambda d, m: (d ^ 2, m))
MOVE_CORE = pairs_of(lambda d, m: (d ^ 1, m))
MOVE_Z = [pairs_of(lambda d, m, k=k: ((d + 4 * k) % 16, m)) for k in (1, 2, 3)]
MOVE_FIRST = pairs_of(lambda d, m: (d ^ 2, m) if d & 1 else (d, 1 - m))
MOVE_SECOND = pairs_of(lambda d, m: (d, 1 - m) if d & 1 else (d ^ 2, m))


MOVE_REDUCE = MOVE_SECOND, MOVE_FIRST


def move(values, moves):
    return lax.ppermute(values, AXES, moves)


def swap_mp(values):
    return lax.ppermute(values, "mp", [(0, 1), (1, 0)])


def started(copies):
    for copy in copies:
        copy.start()
    return copies


def piece_copies(where, pieces, target, sem, by_core=False):
    if len(pieces[0].shape) == 4:
        (whole,) = pieces
        count, _, rows, _ = whole.shape
        return started(
            [
                pltpu.make_async_copy(
                    whole.at[d, where[3] ^ half],
                    target.at[half, pl.ds(d * rows, rows), :],
                    sem.at[(half * count + d) // 4, d % 4],
                )
                for half in range(2)
                for d in range(count)
            ]
        )
    if len(pieces[0].shape) == 2:
        return started(
            [pltpu.make_async_copy(p, target.at[n], sem.at[n, 0]) for n, p in enumerate(pieces)]
        )
    rows = pieces[0].shape[1]
    z, y, core = where[0], where[1], where[2]

    def copies(ref, half, dy, dcore, slot):
        out = []
        for k in range(4):
            block = ((lax.rem(z + 4 - k, 4) * 2 + (y ^ dy)) * 2 + (core ^ dcore)) * rows
            block = pl.multiple_of(block, 16)
            out.append(
                pltpu.make_async_copy(
                    ref.at[k], target.at[half, pl.ds(block, rows), :], sem.at[slot, k]
                )
            )
        return out

    waits = []
    if not by_core:
        for slot, ref in enumerate(pieces):
            waits += copies(ref, slot // 4, slot % 2, slot % 4 // 2, slot)
        return started(waits)

    z0, a0, b0, c0, z1, a1, b1, c1 = pieces
    first = core == 0
    for slot, (ref, half, dy, dcore) in enumerate(
        ((z0, 0, 0, 0), (c0, 1, 1, 0), (z1, 0, 0, 1), (c1, 1, 1, 1))
    ):
        waits += copies(ref, half, dy, dcore, slot)
    started(waits)
    for slot, (ref_if, ref_else, half, dy, dcore) in enumerate(
        ((b0, a0, 0, 1, 0), (a0, b0, 1, 0, 0), (a1, b1, 0, 1, 1), (b1, a1, 1, 0, 1)), 4
    ):
        @pl.when(first)
        def _(ref=ref_if, half=half, dy=dy, dcore=dcore, slot=slot):
            started(copies(ref, half, dy, dcore, slot))

        @pl.when(jnp.logical_not(first))
        def _(ref=ref_else, half=half, dy=dy, dcore=dcore, slot=slot):
            started(copies(ref, half, dy, dcore, slot))

        waits += copies(ref_if, half, dy, dcore, slot)
    return waits


def device_of(rows, half, d_model):
    row = lax.broadcasted_iota(jnp.int32, (d_model, 1), 0)
    device = lax.div(row, jnp.int32(rows))
    return device, row - device * rows


def one_hot(target, cols):
    lane = lax.broadcasted_iota(jnp.int32, (target.shape[0], cols), 1)
    return jnp.where(lane == target, 1.0, 0.0).astype(BF)


def qv_places(rows, d_model):
    device, at = device_of(rows, rows // 2, d_model)
    value = (at >= rows // 2).astype(jnp.int32)
    target = value * (d_model // 2) + device * (rows // 2) + at - value * (rows // 2)
    return one_hot(target, d_model)


def up_places(rows, d_model, part, ff):
    device, at = device_of(rows, rows, d_model)
    return one_hot(device * (2 * rows) + part * rows + at, ff)


def project_kernel(rows, n_qkv, where, tok_ref, *refs):
    pieces = refs[:n_qkv]
    proj_ref, vec_ref, up_ref, weights, bias, sem = refs[n_qkv:]
    d_model = tok_ref.shape[1]
    span = proj_ref.shape[1]

    @pl.when(pl.program_id(0) == 0)
    def _():
        for copy in piece_copies(where, pieces, weights, sem):
            copy.wait()
        bias[...] = jnp.zeros_like(bias)
        qv = qv_places(rows, d_model)
        up = [up_places(rows, d_model, part, up_ref.shape[1]) for part in range(2)]
        turned = weights[0, :, span:].T[:16]
        vec_ref[...] = turned[:8].astype(F32)
        row = mm(turned, qv, NN)[8:9]
        for pair in range(span // (3 * PAIR)):
            at = pair * 3 * PAIR
            bias[0:1, at : at + PAIR] = row[:, pair * PAIR : (pair + 1) * PAIR]
            first = d_model // 2 + pair * PAIR
            bias[0:1, at + 2 * PAIR : at + 3 * PAIR] = row[:, first : first + PAIR]
        up_ref[...] = mm(turned, up[0], NN)[6:7] + mm(turned, up[1], NN)[7:8]

    tokens = tok_ref[...]
    for at in range(0, span, 384):
        proj_ref[:, at : at + 384] = (
            mm(tokens, weights[0, :, at : at + 384], NN) + bias[0:1, at : at + 384]
        ).astype(BF)


def project(where, tokens, pieces, rows, seq, span, ff, tile=512):
    d_model = tokens.shape[1]
    return pl.pallas_call(
        functools.partial(project_kernel, rows, len(pieces)),
        out_shape=(
            jax.ShapeDtypeStruct((seq, span), BF),
            jax.ShapeDtypeStruct((8, d_model), F32),
            jax.ShapeDtypeStruct((1, ff), F32),
        ),
        grid_spec=pltpu.PrefetchScalarGridSpec(
            num_scalar_prefetch=1,
            grid=(seq // tile,),
            in_specs=[own_tile(tile, d_model, seq)] + [ANYWHERE] * len(pieces),
            out_specs=[
                row_tile(tile, span),
                pl.BlockSpec((8, d_model), lambda i, w: (0, 0)),
                pl.BlockSpec((1, ff), lambda i, w: (0, 0)),
            ],
            scratch_shapes=[
                pltpu.VMEM((1, d_model, span + SMALL), BF),
                pltpu.VMEM((8, span), F32),
                pltpu.SemaphoreType.DMA((8, 4)),
            ],
        ),
        cost_estimate=cost(8.7),
        name="project",
    )(where, tokens, *pieces)


def last_kernel(n_qkv, where, own_ref, other_ref, one_ref, *refs):
    pieces = refs[:n_qkv]
    whole_ref, low_ref, weights, sem = refs[n_qkv:]
    span = own_ref.shape[1]

    @pl.when(pl.program_id(0) == 0)
    def _():
        for copy in piece_copies(where, pieces, weights, sem):
            copy.wait()

    total = (
        mm(own_ref[...], weights[0, :, :span], NT)
        + mm(other_ref[...], weights[1, :, :span], NT)
        + one_ref[...]
    )
    whole_ref[...] = total
    low_ref[...] = total.astype(BF)


def last_part(where, d_proj, d_one, pieces, tile=512):
    seq, span = d_proj[0].shape
    d_model = d_one.shape[1]
    return pl.pallas_call(
        functools.partial(last_kernel, len(pieces)),
        out_shape=(
            jax.ShapeDtypeStruct((2 * seq, d_model), F32),
            jax.ShapeDtypeStruct((seq, d_model), BF),
        ),
        grid_spec=pltpu.PrefetchScalarGridSpec(
            num_scalar_prefetch=1,
            grid=(seq // tile,),
            in_specs=[row_tile(tile, span), row_tile(tile, span), row_tile(tile, d_model)]
            + [ANYWHERE] * len(pieces),
            out_specs=[own_tile(tile, d_model, seq), row_tile(tile, d_model)],
            scratch_shapes=[
                pltpu.VMEM((2, d_model, span + SMALL), BF),
                pltpu.SemaphoreType.DMA((8, 4)),
            ],
        ),
        cost_estimate=cost(12.0),
        name="last_part",
    )(where, *d_proj, d_one, *pieces)


def part_copies(where, result, half, keep_ref, send_ref, sem, staged):
    if not staged:
        return [pltpu.make_async_copy(result.at[half], keep_ref.at[half], sem.at[half, 0])]
    if len(keep_ref.shape) == 4:
        rows = keep_ref.shape[2]
        return [
            pltpu.make_async_copy(
                result.at[half, pl.ds(d * rows, rows), :],
                keep_ref.at[d, where[3] ^ half],
                sem.at[half, d],
            )
            for d in range(keep_ref.shape[0])
        ]
    rows = keep_ref.shape[-2]
    z, y, core = where[0], where[1], where[2]
    out = []
    for dcore, target in enumerate((keep_ref, send_ref)):
        for dy in range(2):
            for k in range(4):
                block = ((lax.rem(z + k, 4) * 2 + (y ^ dy)) * 2 + (core ^ dcore)) * rows
                block = pl.multiple_of(block, 16)
                if target.shape[2] == 1:
                    place = target.at[dy, k, 0]
                else:
                    by_y = (core ^ dcore) == 0
                    place = target.at[jnp.where(by_y, dy, half), jnp.where(by_y, half, dy), k]
                out.append(
                    pltpu.make_async_copy(
                        result.at[half, pl.ds(block, rows), :], place, sem.at[half, len(out)]
                    )
                )
    return out


def part_shapes(staged, halves, d_model, cols):
    if not staged:
        whole = jax.ShapeDtypeStruct((halves, d_model, cols), BF)
        return whole, jax.ShapeDtypeStruct((8, 128), BF)
    rows = d_model // 16
    dims = (2, 4, 1, rows, cols) if halves == 1 else (2, 2, 4, rows, cols)
    return (jax.ShapeDtypeStruct(dims, BF),) * 2


def after(value, *others):
    return lax.optimization_barrier((value, *others))[0]


def grads_kernel(staged, rows, halves, widths, n_extra, where, *refs):
    count = len(widths)
    lhs_refs, refs = refs[:count], refs[count:]
    rhs_refs, refs = refs[: count * halves], refs[count * halves :]
    extra_refs, refs = refs[:n_extra], refs[n_extra:]
    keep_ref, send_ref, result, turned, sem = refs
    d_model = result.shape[1]
    for lhs, out in zip(lhs_refs, range(count)):
        for at in range(0, lhs.shape[0], BLOCK):
            turned[out, :, at : at + BLOCK] = lhs[at : at + BLOCK, :].T
    for half in range(halves):
        first = 0
        for n in range(count):
            rhs = rhs_refs[n * halves + half]
            rhs = rhs.at[half] if len(rhs.shape) == 3 else rhs
            width = rhs.shape[1]
            for at in range(0, width, 384):
                result[half, :, first + at : first + at + 384] = mm(
                    turned[n], rhs[:, at : at + 384], NN
                ).astype(BF)
            first += width
        if n_extra == 1:
            (sums,) = extra_refs
            blank = jnp.zeros((SMALL - 1, PAIR), F32)
            parts = [
                sums[pair, 0:1, n * PAIR : (n + 1) * PAIR]
                for n in (0, 2)
                for pair in range(sums.shape[0])
            ]
            line = jnp.concatenate(parts, axis=1)
            lines = jnp.concatenate([line, jnp.zeros((SMALL - 1, line.shape[1]), F32)], axis=0)
            extra = mm(qv_places(rows, d_model), lines.astype(BF), NT)
        else:
            two, one, up = extra_refs
            own = one_hot(lax.broadcasted_iota(jnp.int32, (d_model, 1), 0), d_model)
            zero = jnp.zeros((SMALL - 6, d_model), F32)
            lines = jnp.concatenate([one[2:3], one[0:2], two[2:3], two[0:2], zero], axis=0)
            extra = mm(own, lines.astype(BF), NT)
            blank = jnp.zeros((SMALL - 8, up.shape[2]), F32)
            for part in range(2):
                line = up[half, 0:1]
                before = jnp.zeros((6 + part, line.shape[1]), F32)
                behind = jnp.zeros((SMALL - 7 - part, line.shape[1]), F32)
                lines = jnp.concatenate([before, line, behind], axis=0)
                extra = extra + mm(
                    up_places(rows, d_model, part, line.shape[1]), lines.astype(BF), NT
                )
        result[half, :, first:] = extra.astype(BF)
        for copy in part_copies(where, result, half, keep_ref, send_ref, sem, staged):
            copy.start()
    for half in range(halves):
        for copy in part_copies(where, result, half, keep_ref, send_ref, sem, staged):
            copy.wait()


def whole_spec(array):
    return pl.BlockSpec(array.shape, lambda i, w, n=array.ndim: (0,) * n)


def own_tile(tile, width, seq):
    return pl.BlockSpec((tile, width), lambda i, w: (w[3] * (seq // tile) + i, 0))


def grads(where, staged, rows, lhs, rhs, extra):
    halves = len(rhs[0])
    seq = rhs[0][0].shape[-2]
    d_model = lhs[0].shape[1]
    widths = [r[0].shape[-1] for r in rhs]
    cols = sum(widths) + SMALL
    operands = [*(r for pair in rhs for r in pair), *extra]
    return pl.pallas_call(
        functools.partial(grads_kernel, staged, rows, halves, widths, len(extra)),
        out_shape=part_shapes(staged, halves, d_model, cols),
        grid_spec=pltpu.PrefetchScalarGridSpec(
            num_scalar_prefetch=1,
            grid=(1,),
            in_specs=[
                own_tile(seq, d_model, seq) if l.shape[0] > seq else whole_spec(l) for l in lhs
            ]
            + [whole_spec(o) for o in operands],
            out_specs=[ANYWHERE] * 2,
            scratch_shapes=[
                pltpu.VMEM((halves, d_model, cols), BF),
                pltpu.VMEM((len(lhs), d_model, seq), BF),
                pltpu.SemaphoreType.DMA((halves, 16)),
            ],
        ),
        cost_estimate=cost(20.0 if halves == 2 else 7.2),
        name="grads",
    )(where, *lhs, *operands)


def row_norm(values):
    centered = values - jnp.mean(values, axis=-1, keepdims=True)
    inverse = lax.rsqrt(jnp.mean(centered * centered, axis=-1, keepdims=True) + NORM_EPS)
    return centered * inverse, inverse


def row_norm_back(d_normed, z, inverse, gain):
    dz = d_normed * gain
    return (
        dz - jnp.mean(dz, axis=-1, keepdims=True) - z * jnp.mean(dz * z, axis=-1, keepdims=True)
    ) * inverse


def column_sum(values):
    return jnp.sum(values, axis=0, keepdims=True)


def first_kernel(n_up, where, tok_ref, ctx0_ref, ctx1_ref, vec_ref, bias0_ref, bias1_ref, *refs):
    pieces = refs[:n_up]
    z_ref, inv_ref, hid_ref, slope_ref, weights, sem = refs[n_up:]
    bias_refs = bias0_ref, bias1_ref
    width = ctx0_ref.shape[1]

    @pl.when(pl.program_id(0) == 0)
    def _():
        for copy in piece_copies(where, pieces, weights, sem, True):
            copy.wait()

    resid = (
        tok_ref[...].astype(F32)
        + mm(ctx0_ref[...], weights[0, :, :width], NT)
        + mm(ctx1_ref[...], weights[1, :, :width], NT)
        + vec_ref[0:1]
    )
    z, inverse = row_norm(resid)
    z_ref[...] = z
    inv_ref[...] = jnp.broadcast_to(inverse, inv_ref.shape)
    low = (z * vec_ref[1:2] + vec_ref[2:3]).astype(BF)
    ff = hid_ref.shape[2]
    for half in range(2):
        for at in range(0, ff, 512):
            pre = mm(low, weights[half, :, width + at : width + at + 512], NN)
            gelu, slope = gelu_both(pre + bias_refs[half][:, at : at + 512])
            hid_ref[half, :, at : at + 512] = gelu.astype(BF)
            slope_ref[half, :, at : at + 512] = slope.astype(BF)


def row_tile(tile, width):
    return pl.BlockSpec((tile, width), lambda i, w: (i, 0))


def halves_tile(tile, width):
    return pl.BlockSpec((2, tile, width), lambda i, w: (0, i, 0))


ANYWHERE = pl.BlockSpec(memory_space=pl.ANY)


def first_part(where, tokens, ctx, vectors, bias, pieces, tile=256):
    d_model = tokens.shape[1]
    seq = ctx[0].shape[0]
    width, ff = ctx[0].shape[1], bias[0].shape[1]
    return pl.pallas_call(
        functools.partial(first_kernel, len(pieces)),
        out_shape=(
            jax.ShapeDtypeStruct((seq, d_model), F32),
            jax.ShapeDtypeStruct((seq, 128), F32),
            jax.ShapeDtypeStruct((2, seq, ff), BF),
            jax.ShapeDtypeStruct((2, seq, ff), BF),
        ),
        grid_spec=pltpu.PrefetchScalarGridSpec(
            num_scalar_prefetch=1,
            grid=(seq // tile,),
            in_specs=[
                own_tile(tile, d_model, seq),
                row_tile(tile, width),
                row_tile(tile, width),
                whole_spec(vectors),
                whole_spec(bias[0]),
                whole_spec(bias[1]),
            ]
            + [ANYWHERE] * len(pieces),
            out_specs=[
                row_tile(tile, d_model),
                row_tile(tile, 128),
                halves_tile(tile, ff),
                halves_tile(tile, ff),
            ],
            scratch_shapes=[
                pltpu.VMEM((2, d_model, width + ff), BF),
                pltpu.SemaphoreType.DMA((8, 4)),
            ],
        ),
        cost_estimate=cost(19.4),
        name="first_part",
    )(where, tokens, *ctx, vectors, *bias, *pieces)


def second_kernel(staged, n_down, where, hid_ref, z_ref, cot_ref, vec_ref, *refs):
    pieces = refs[:n_down]
    out_ref, own_ref, d_ref, sum_ref, keep_ref, *refs = refs[n_down:]
    weights, turned, kept, result, sem, out_sem = refs
    step = pl.program_id(0)
    tile, ff = hid_ref.shape[1:]

    @pl.when(step == 0)
    def _():
        for copy in piece_copies(where, pieces, weights, sem):
            copy.wait()
        sum_ref[...] = jnp.zeros_like(sum_ref)

    ffn = mm(hid_ref[0], weights[0], NT) + mm(hid_ref[1], weights[1], NT)
    resid = z_ref[...] * vec_ref[1:2] + vec_ref[2:3] + ffn + vec_ref[3:4]
    z, inverse = row_norm(resid)
    out = (z * vec_ref[4:5] + vec_ref[5:6]).astype(BF)
    out_ref[...] = out
    own_ref[...] = out
    cot = cot_ref[...].astype(F32)
    d_two = row_norm_back(cot, z, inverse, vec_ref[4:5])
    d_ref[...] = d_two
    sum_ref[0:1] += column_sum(cot * z)
    sum_ref[1:2] += column_sum(cot)
    sum_ref[2:3] += column_sum(d_two)
    rows = pl.ds(pl.multiple_of(step * tile, tile), tile)
    turned[:, rows] = d_two.astype(BF).T
    kept[:, rows, :] = hid_ref[...]

    @pl.when(step == pl.num_programs(0) - 1)
    def _():
        for half in range(2):
            for at in range(0, ff, 512):
                result[half, :, at : at + 512] = mm(
                    turned[...], kept[half, :, at : at + 512], NN
                ).astype(BF)
            for copy in part_copies(where, result, half, keep_ref, None, out_sem, staged):
                copy.start()
        for half in range(2):
            for copy in part_copies(where, result, half, keep_ref, None, out_sem, staged):
                copy.wait()


def second_part(where, staged, hidden, z_one, cot, vectors, pieces, tile=256):
    _, seq, ff = hidden.shape
    d_model = z_one.shape[1]
    return pl.pallas_call(
        functools.partial(second_kernel, staged, len(pieces)),
        out_shape=(
            jax.ShapeDtypeStruct((2 * seq, d_model), BF),
            jax.ShapeDtypeStruct((seq, d_model), BF),
            jax.ShapeDtypeStruct((seq, d_model), F32),
            jax.ShapeDtypeStruct((8, d_model), F32),
            (
                jax.ShapeDtypeStruct((16, 2, d_model // 16, ff), BF)
                if staged
                else jax.ShapeDtypeStruct((2, d_model, ff), BF)
            ),
        ),
        grid_spec=pltpu.PrefetchScalarGridSpec(
            num_scalar_prefetch=1,
            grid=(seq // tile,),
            in_specs=[
                halves_tile(tile, ff),
                row_tile(tile, d_model),
                own_tile(tile, d_model, seq),
                whole_spec(vectors),
            ]
            + [ANYWHERE] * len(pieces),
            out_specs=[
                own_tile(tile, d_model, seq),
                row_tile(tile, d_model),
                row_tile(tile, d_model),
                pl.BlockSpec((8, d_model), lambda i, w: (0, 0)),
                ANYWHERE,
            ],
            scratch_shapes=[
                pltpu.VMEM((2, d_model, ff), BF),
                pltpu.VMEM((d_model, seq), BF),
                pltpu.VMEM((2, seq, ff), BF),
                pltpu.VMEM((2, d_model, ff), BF),
                pltpu.SemaphoreType.DMA((8, 4)),
                pltpu.SemaphoreType.DMA((2, 16)),
            ],
        ),
        cost_estimate=cost(21.8),
        name="second_part",
    )(where, hidden, z_one, cot, vectors, *pieces)


def third_kernel(n_up, n_down, where, d_ref, slope_ref, z_ref, inv_ref, vec_ref, *refs):
    up_pieces, down_pieces, refs = refs[:n_up], refs[n_up : n_up + n_down], refs[n_up + n_down :]
    pre_ref, low_ref, one_ref, one_low_ref, ctx_ref, sum_ref, bias_ref, *refs = refs
    up, down, sem, down_sem = refs
    step = pl.program_id(0)
    ff = slope_ref.shape[2]
    width = ctx_ref.shape[2]

    @pl.when(step == 0)
    def _():
        waits = piece_copies(where, down_pieces, down, down_sem)
        waits += piece_copies(where, up_pieces, up, sem, True)
        for copy in waits:
            copy.wait()
        sum_ref[...] = jnp.zeros_like(sum_ref)
        bias_ref[...] = jnp.zeros_like(bias_ref)

    d_two = d_ref[...]
    d_two_low = d_two.astype(BF)
    d_normed = d_two
    for half in range(2):
        for at in range(0, ff, 512):
            span = slice(at, at + 512)
            d_pre = mm(d_two_low, down[half, :, span], NN) * slope_ref[half, :, span].astype(F32)
            d_pre = d_pre.astype(BF)
            pre_ref[half, :, span] = d_pre
            bias_ref[half, 0:1, span] += column_sum(d_pre.astype(F32))
            d_normed = d_normed + mm(d_pre, up[half, :, width + at : width + at + 512], NT)
    z = z_ref[...]
    low_ref[...] = (z * vec_ref[1:2] + vec_ref[2:3]).astype(BF)
    d_one = row_norm_back(d_normed, z, inv_ref[:, 0:1], vec_ref[1:2])
    one_ref[...] = d_one
    sum_ref[0:1] += column_sum(d_normed * z)
    sum_ref[1:2] += column_sum(d_normed)
    sum_ref[2:3] += column_sum(d_one)
    d_one_low = d_one.astype(BF)
    one_low_ref[...] = d_one_low
    for half in range(2):
        ctx_ref[half] = mm(d_one_low, up[half, :, :width], NN).astype(BF)


def third_part(where, d_two, slope, z_one, inv_one, vectors, up_pieces, down_pieces, width, tile=256):
    seq, d_model = d_two.shape
    ff = slope.shape[2]
    return pl.pallas_call(
        functools.partial(third_kernel, len(up_pieces), len(down_pieces)),
        out_shape=(
            jax.ShapeDtypeStruct((2, seq, ff), BF),
            jax.ShapeDtypeStruct((seq, d_model), BF),
            jax.ShapeDtypeStruct((seq, d_model), F32),
            jax.ShapeDtypeStruct((seq, d_model), BF),
            jax.ShapeDtypeStruct((2, seq, width), BF),
            jax.ShapeDtypeStruct((8, d_model), F32),
            jax.ShapeDtypeStruct((2, 8, ff), F32),
        ),
        grid_spec=pltpu.PrefetchScalarGridSpec(
            num_scalar_prefetch=1,
            grid=(seq // tile,),
            in_specs=[
                row_tile(tile, d_model),
                halves_tile(tile, ff),
                row_tile(tile, d_model),
                row_tile(tile, 128),
                whole_spec(vectors),
            ]
            + [ANYWHERE] * (len(up_pieces) + len(down_pieces)),
            out_specs=[
                halves_tile(tile, ff),
                row_tile(tile, d_model),
                row_tile(tile, d_model),
                row_tile(tile, d_model),
                halves_tile(tile, width),
                pl.BlockSpec((8, d_model), lambda i, w: (0, 0)),
                pl.BlockSpec((2, 8, ff), lambda i, w: (0, 0, 0)),
            ],
            scratch_shapes=[
                pltpu.VMEM((2, d_model, width + ff), BF),
                pltpu.VMEM((2, d_model, ff), BF),
                pltpu.SemaphoreType.DMA((8, 4)),
                pltpu.SemaphoreType.DMA((8, 4)),
            ],
        ),
        cost_estimate=cost(25.6),
        name="third_part",
    )(where, d_two, slope, z_one, inv_one, vectors, *up_pieces, *down_pieces)


def add(first, second):
    return (first.astype(F32) + second.astype(F32)).astype(BF)


def core_stage(keep, send):
    return move(send, MOVE_CORE), keep


def flip_stage(moves, got, keep):
    return move(add(keep[1], got[1]), moves), add(keep[0], got[0])


def z_stage(*terms):
    sums = [functools.reduce(jnp.add, [t[k].astype(F32) for t in terms]) for k in range(4)]
    parts = [move(part.astype(BF), moves) for part, moves in zip(sums[1:], MOVE_Z)]
    return parts, sums[0]


def z_sum(parts, keep):
    return keep + parts[0].astype(F32) + parts[1].astype(F32) + parts[2].astype(F32)


def lane_mask(head, rows):
    lanes = lax.broadcasted_iota(jnp.int32, (rows, PAIR), 1)
    return (lanes < HD) if head == 0 else (lanes >= HD)


def attn_fwd_kernel(table, qkv_ref, ctx_ref, prob_ref):
    pair = pl.program_id(0)
    q_ref, k_ref, v_ref = (qkv_ref.at[:, n * PAIR : (n + 1) * PAIR] for n in range(3))
    lanes = lax.broadcasted_iota(jnp.int32, (1, HALF), 1)
    for half in range(2):
        rows = pl.ds(half * HALF, HALF)
        query = q_ref[rows, :] * jnp.asarray(HD**-0.5, BF)
        parts = []
        for head in range(2):
            at = (pair * 2 + head) * 4
            start = (half ^ table[at]) * HALF
            flags = [table[at + 1 + n] == 1 for n in range(3)]
            key_lo = k_ref[pl.ds(pl.multiple_of(start, BLOCK), BLOCK), :]
            key_hi = k_ref[pl.ds(pl.multiple_of(start + BLOCK, BLOCK), BLOCK), :]
            masked = jnp.where(lane_mask(head, HALF), query, jnp.zeros_like(query))
            score_lo = mm(key_lo, masked, NT)
            score_hi = mm(key_hi, masked[BLOCK:], NT)
            no_lo = jnp.where(
                lanes < BLOCK,
                jnp.where(flags[0], 0.0, -1e30),
                jnp.where(flags[1], 0.0, -1e30),
            ).astype(F32)
            no_hi = jnp.where(flags[2], 0.0, -1e30).astype(F32)
            top_lo = jnp.max(score_lo, axis=0, keepdims=True) + no_lo
            top_hi = jnp.max(score_hi, axis=0, keepdims=True) + no_hi
            top = jnp.concatenate(
                [top_lo[:, :BLOCK], jnp.maximum(top_lo[:, BLOCK:], top_hi)], axis=1
            )
            ref_lo = jnp.where(no_lo < 0.0, 1e30, top)
            ref_hi = jnp.where(no_hi < 0.0, 1e30, top[:, BLOCK:])
            exp_lo = jnp.exp(score_lo - ref_lo)
            exp_hi = jnp.exp(score_hi - ref_hi)
            sum_lo = jnp.sum(exp_lo, axis=0, keepdims=True)
            sum_hi = jnp.sum(exp_hi, axis=0, keepdims=True)
            total = jnp.concatenate([sum_lo[:, :BLOCK], sum_lo[:, BLOCK:] + sum_hi], axis=1)
            scale = jnp.where(total > 0.0, 1.0 / jnp.where(total > 0.0, total, 1.0), 0.0)
            prob_lo = (exp_lo * scale).astype(BF)
            prob_hi = (exp_hi * scale[:, BLOCK:]).astype(BF)
            prob_ref[0, head, half, :, :HALF] = prob_lo
            prob_ref[0, head, half, :, HALF:] = prob_hi
            val_lo = v_ref[pl.ds(pl.multiple_of(start, BLOCK), BLOCK), :].T
            val_hi = v_ref[pl.ds(pl.multiple_of(start + BLOCK, BLOCK), BLOCK), :].T
            side = slice(head * HD, (head + 1) * HD)
            out_lo = mm(val_lo[side], prob_lo, NN)
            out_hi = mm(val_hi[side], prob_hi, NN)
            parts.append(
                jnp.concatenate([out_lo[:, :BLOCK], out_lo[:, BLOCK:] + out_hi], axis=1)
            )
        ctx_ref[rows, :] = jnp.concatenate(parts, axis=0).T.astype(BF)


def attn_fwd(table, proj):
    seq, width = proj.shape
    pairs = width // 3 // PAIR
    return pl.pallas_call(
        attn_fwd_kernel,
        out_shape=(
            jax.ShapeDtypeStruct((seq, width // 3), BF),
            jax.ShapeDtypeStruct((pairs, 2, 2, BLOCK, HALF + BLOCK), BF),
        ),
        grid_spec=pltpu.PrefetchScalarGridSpec(
            num_scalar_prefetch=1,
            grid=(pairs,),
            in_specs=[pl.BlockSpec((seq, 3 * PAIR), lambda p, t: (0, p))],
            out_specs=[
                pl.BlockSpec((seq, PAIR), lambda p, t: (0, p)),
                pl.BlockSpec((1, 2, 2, BLOCK, HALF + BLOCK), lambda p, t: (p, 0, 0, 0, 0)),
            ],
        ),
        cost_estimate=cost(8.9),
        name="attn_fwd",
    )(table, proj)


def attn_bwd_kernel(table, qkv_ref, d_ref, prob_ref, out_ref, sum_ref, k_acc, v_acc):
    pair = pl.program_id(0)
    q_ref, k_ref, v_ref = (qkv_ref.at[:, n * PAIR : (n + 1) * PAIR] for n in range(3))
    for half in range(2):
        rows = pl.ds(half * HALF, HALF)
        query = q_ref[rows, :] * jnp.asarray(HD**-0.5, BF)
        d_ctx = d_ref[rows, :]
        parts = []
        for head in range(2):
            at = (pair * 2 + head) * 4
            start = (half ^ table[at]) * HALF
            at_lo = pl.ds(pl.multiple_of(start, BLOCK), BLOCK)
            at_hi = pl.ds(pl.multiple_of(start + BLOCK, BLOCK), BLOCK)
            keep = lane_mask(head, HALF)
            query_h = jnp.where(keep, query, jnp.zeros_like(query))
            d_ctx_h = jnp.where(keep, d_ctx, jnp.zeros_like(d_ctx))
            prob_lo = prob_ref[0, head, half, :, :HALF]
            prob_hi = prob_ref[0, head, half, :, HALF:]
            d_w_lo = mm(v_ref[at_lo, :], d_ctx_h, NT)
            d_w_hi = mm(v_ref[at_hi, :], d_ctx_h[BLOCK:], NT)
            wide_lo = prob_lo.astype(F32)
            wide_hi = prob_hi.astype(F32)
            dot_lo = jnp.sum(wide_lo * d_w_lo, axis=0, keepdims=True)
            dot_hi = jnp.sum(wide_hi * d_w_hi, axis=0, keepdims=True)
            dot = jnp.concatenate([dot_lo[:, :BLOCK], dot_lo[:, BLOCK:] + dot_hi], axis=1)
            d_s_lo = (wide_lo * (d_w_lo - dot)).astype(BF)
            d_s_hi = (wide_hi * (d_w_hi - dot[:, BLOCK:])).astype(BF)
            dk_lo = mm(d_s_lo, query_h, NN)
            dk_hi = mm(d_s_hi, query_h[BLOCK:], NN)
            dv_lo = mm(prob_lo, d_ctx_h, NN)
            dv_hi = mm(prob_hi, d_ctx_h[BLOCK:], NN)
            k_acc[head, at_lo, :] = dk_lo
            k_acc[head, at_hi, :] = dk_hi
            v_acc[head, at_lo, :] = dv_lo
            v_acc[head, at_hi, :] = dv_hi
            key_lo = k_ref[at_lo, :].T
            key_hi = k_ref[at_hi, :].T
            side = slice(head * HD, (head + 1) * HD)
            dq_lo = mm(key_lo[side], d_s_lo, NN)
            dq_hi = mm(key_hi[side], d_s_hi, NN)
            parts.append(jnp.concatenate([dq_lo[:, :BLOCK], dq_lo[:, BLOCK:] + dq_hi], axis=1))
        out_ref[rows, :PAIR] = (jnp.concatenate(parts, axis=0).T * HD**-0.5).astype(BF)
    out_ref[:, PAIR : 2 * PAIR] = (k_acc[0] + k_acc[1]).astype(BF)
    out_ref[:, 2 * PAIR :] = (v_acc[0] + v_acc[1]).astype(BF)
    sums = jnp.sum(out_ref[...].astype(F32), axis=0, keepdims=True)
    sum_ref[0] = jnp.broadcast_to(sums, sum_ref.shape[1:])


def attn_bwd(table, proj, d_context, half, probs):
    seq, width = proj.shape
    pairs = width // 3 // PAIR
    return pl.pallas_call(
        attn_bwd_kernel,
        out_shape=(
            jax.ShapeDtypeStruct((seq, width), BF),
            jax.ShapeDtypeStruct((pairs, 8, 3 * PAIR), F32),
        ),
        grid_spec=pltpu.PrefetchScalarGridSpec(
            num_scalar_prefetch=1,
            grid=(pairs,),
            in_specs=[
                pl.BlockSpec((seq, 3 * PAIR), lambda p, t: (0, p)),
                pl.BlockSpec((None, seq, PAIR), lambda p, t: (half, 0, p)),
                pl.BlockSpec((1, 2, 2, BLOCK, HALF + BLOCK), lambda p, t: (p, 0, 0, 0, 0)),
            ],
            out_specs=[
                pl.BlockSpec((seq, 3 * PAIR), lambda p, t: (0, p)),
                pl.BlockSpec((1, 8, 3 * PAIR), lambda p, t: (p, 0, 0)),
            ],
            scratch_shapes=[pltpu.VMEM((2, seq, PAIR), F32)] * 2,
        ),
        cost_estimate=cost(11.3),
        name="attn_bwd",
    )(table, proj, d_context, probs)


def gelu_both(values):
    half = 0.5 * (1.0 + lax.erf(values * (0.5**0.5)))
    slope = half + values * jnp.exp(-0.5 * values * values) * 0.3989422804014327
    return values * half, slope


def body(
    dp_size,
    tokens,
    grad_out,
    head_perm,
    block_mask,
    w_qkv,
    b_qv,
    w_out,
    b_out,
    gain_one,
    shift_one,
    w_up,
    b_up,
    w_down,
    b_down,
    gain_two,
    shift_two,
):
    seq = tokens.shape[0] // head_perm.shape[0]
    rows = w_qkv.shape[0]
    width = w_qkv.shape[2]
    d_model = tokens.shape[1]
    dp_at = lax.axis_index("dp")
    mp_at = lax.axis_index("mp")
    where = jnp.stack([dp_at // 4, (dp_at // 2) % 2, dp_at % 2, mp_at]).astype(jnp.int32)

    table = jnp.concatenate([head_perm[:, :, None], block_mask], axis=2).astype(jnp.int32)
    table = table.reshape(2, -1)
    table_own = lax.dynamic_index_in_dim(table, mp_at, 0, keepdims=False)
    table_other = swap_mp(lax.dynamic_index_in_dim(table, 1 - mp_at, 0, keepdims=False))

    small = jnp.stack(
        [
            b_out,
            gain_one,
            shift_one,
            b_down,
            gain_two,
            shift_two,
            b_up[:rows],
            b_up[rows:],
            b_qv.reshape(-1),
        ],
        axis=1,
    )
    small = jnp.pad(small, ((0, 0), (0, SMALL - small.shape[1])))
    pairs = width // PAIR
    by_pair = w_qkv.reshape(rows, 3, pairs, PAIR).transpose(0, 2, 1, 3).reshape(rows, 3 * width)
    shard_qkv = jnp.concatenate([by_pair, small], axis=1)
    shard_up = jnp.concatenate([w_out.T, w_up], axis=1)
    shard_down = w_down.T
    staged = dp_size == 16

    def plain_gather(shard):
        full = lax.all_gather(shard, "dp", axis=0, tiled=True)
        return full, swap_mp(full)

    def gather_z(shard):
        return jnp.stack([shard] + [move(shard, moves) for moves in MOVE_Z])

    def gather_core(*pieces):
        return (*pieces, *(move(piece, MOVE_CORE) for piece in pieces))

    if staged:
        qkv_z = gather_z(shard_qkv)
        qkv_y = move(qkv_z, MOVE_Y)
        qkv_x = move(qkv_z, MOVE_X)
        up_parts = [move(after(shard_up, qkv_z), moves) for moves in MOVE_Z]
        down_whole = lax.all_gather(after(shard_down, qkv_z), AXES)
        down_pieces = (down_whole.reshape(dp_size, 2, *shard_down.shape),)
        qkv_own = gather_core(qkv_z, qkv_y)
        qkv_xy = move(qkv_y, MOVE_X)
        tokens_in, table_other = lax.optimization_barrier((tokens, table_other))
    else:
        qkv_own, qkv_other = ((piece,) for piece in plain_gather(shard_qkv))
        up_pieces = plain_gather(shard_up)
        down_pieces = plain_gather(shard_down)
        tokens_in = tokens

    ff = w_up.shape[1]

    def project_half(values, pieces):
        return project(where, values, pieces, rows, seq, 3 * width, ff)

    proj_own, vectors, bias_own = project_half(tokens_in, qkv_own)
    if staged:
        proj_own, qkv_x, qkv_xy, *up_parts = lax.optimization_barrier(
            (proj_own, qkv_x, qkv_xy, *up_parts)
        )
        qkv_other = gather_core(qkv_x, qkv_xy)
        up_z = jnp.stack([shard_up, *up_parts])
        up_a, up_b = move(up_z, MOVE_FIRST), move(up_z, MOVE_SECOND)
    ctx_own, probs_own = attn_fwd(table_own, proj_own)
    proj_other, _, bias_other = project_half(after(tokens, ctx_own), qkv_other)
    if staged:
        proj_other, up_a = lax.optimization_barrier((proj_other, up_a))
        up_c = move(up_a, MOVE_SECOND)
        up_pieces = gather_core(up_z, up_a, up_b)
    ctx_other, probs_other = attn_fwd(table_other, proj_other)
    if staged:
        ctx_other, up_c = lax.optimization_barrier((ctx_other, up_c))
        up_pieces = (*up_pieces[:3], up_c, *up_pieces[3:], move(up_c, MOVE_CORE))
    tables, proj = (table_own, table_other), (proj_own, proj_other)
    probs = (probs_own, probs_other)
    ctx = (ctx_own, ctx_other)
    qkv_pieces = (*qkv_own, *qkv_other)
    z_one, inv_one, hidden, slope = first_part(
        where, tokens, ctx, vectors, (bias_own, bias_other), up_pieces
    )

    out_whole, out_own, d_two, sums_two, down_grad = second_part(
        where, staged, hidden, z_one, grad_out, vectors, down_pieces
    )
    out_other = swap_mp(out_own)

    def plain_scatter(own, other):
        summed = own.astype(F32) + swap_mp(other).astype(F32)
        return lax.psum_scatter(summed, "dp", scatter_dimension=0, tiled=True)

    if staged:
        down_grad = down_grad.reshape(2 * dp_size, *shard_down.shape)
        s_down = lax.psum_scatter(down_grad, AXES, scatter_dimension=0).astype(F32)
    else:
        s_down = plain_scatter(*down_grad)
    d_pre, normed_low, d_one, d_one_low, d_ctx, sums_one, sums_up = third_part(
        where, d_two, slope, z_one, inv_one, vectors, up_pieces, down_pieces, width
    )
    up_parts = grads(
        where,
        staged,
        rows,
        [normed_low, d_one_low],
        [(d_pre, d_pre), ctx],
        (sums_two, sums_one, sums_up),
    )
    d_ctx_other = d_ctx
    if staged:
        up_got, up_keep = core_stage(*up_parts)
        d_ctx_other, out_other, up_keep = lax.optimization_barrier((d_ctx, out_other, up_keep))
    else:
        s_up = plain_scatter(*up_parts[0])
    d_proj_other, sums_other = attn_bwd(tables[1], proj[1], d_ctx_other, 1, probs[1])
    if staged:
        d_proj_other, up_got = lax.optimization_barrier((d_proj_other, up_got))
        up_got, up_keep = flip_stage(MOVE_REDUCE[0], up_got, up_keep)
        d_proj_other, up_keep = lax.optimization_barrier((d_proj_other, up_keep))
    other_parts = grads(where, staged, rows, [tokens], [(d_proj_other,)], (sums_other,))
    d_ctx_own = d_ctx
    if staged:
        qo_got, qo_keep = core_stage(*other_parts)
        d_ctx_own, qo_keep = lax.optimization_barrier((d_ctx, qo_keep))
    d_proj_own, sums_own = attn_bwd(tables[0], proj[0], d_ctx_own, 0, probs[0])
    d_proj_last = d_proj_own
    if staged:
        d_proj_own, up_got, qo_got = lax.optimization_barrier((d_proj_own, up_got, qo_got))
        up_got, up_keep = flip_stage(MOVE_REDUCE[1], up_got, up_keep)
        qo_got, qo_keep = flip_stage(MOVE_Y, qo_got, qo_keep)
        d_proj_last, up_keep, qo_keep = lax.optimization_barrier((d_proj_own, up_keep, qo_keep))
    d_input, in_low = last_part(where, (d_proj_last, d_proj_other), d_one, qkv_pieces)
    tokens_in = tokens
    if staged:
        tokens_in, in_low = lax.optimization_barrier((tokens, in_low))
    in_other = swap_mp(in_low)
    own_parts = grads(where, staged, rows, [tokens_in], [(d_proj_own,)], (sums_own,))
    if staged:
        qs_got, qs_keep = core_stage(*own_parts)
        up_got, qo_got, qs_keep = lax.optimization_barrier((up_got, qo_got, qs_keep))
        qo_in = move(add(qo_keep, qo_got), MOVE_X)
        up_parts, up_keep = z_stage(up_got, up_keep)
        up_keep, qs_got = lax.optimization_barrier((up_keep, qs_got))
        qs_got, qs_keep = flip_stage(MOVE_Y, qs_got, qs_keep)
        s_up = z_sum(up_parts, up_keep)
        qs_parts, qs_keep = z_stage(qs_got, qs_keep, qo_in)
        s_qkv = z_sum(qs_parts, qs_keep)[0]
        in_other, s_qkv = lax.optimization_barrier((in_other, s_qkv))
    else:
        s_qkv = plain_scatter(own_parts[0][0], other_parts[0][0])

    def place(whole, other):
        return lax.dynamic_update_slice_in_dim(
            whole, other.astype(whole.dtype), (1 - mp_at) * seq, 0
        )

    cols = s_up[:, ff + width :].T
    g_w_qkv = s_qkv[:, : 3 * width].reshape(rows, pairs, 3, PAIR).transpose(0, 2, 1, 3)
    return (
        place(out_whole, out_other),
        place(d_input, in_other),
        g_w_qkv.reshape(rows, 3, width),
        s_qkv[:, 3 * width].reshape(2, rows // 2),
        s_up[:, ff : ff + width].T,
        cols[0],
        cols[1],
        cols[2],
        s_up[:, :ff],
        cols[6:8].reshape(-1),
        s_down.T,
        cols[3],
        cols[4],
        cols[5],
    )


def solution(mesh):
    placed = (
        P("dp", None),
        P("dp", None),
        P("dp", "mp"),
        P("dp", "mp", None),
        P("dp", None, "mp"),
        P(None, ("mp", "dp")),
        P("mp", "dp"),
        P("dp"),
        P("dp"),
        P("dp"),
        P("dp", "mp"),
        P(("mp", "dp")),
        P("mp", "dp"),
        P("dp"),
        P("dp"),
        P("dp"),
    )
    return jax.shard_map(
        functools.partial(body, mesh.shape["dp"]),
        mesh=mesh,
        in_specs=placed,
        out_specs=(
            P("dp", None),
            P("dp", None),
            P("dp", None, "mp"),
            P(None, ("mp", "dp")),
            P("mp", "dp"),
            P("dp"),
            P("dp"),
            P("dp"),
            P("dp", "mp"),
            P(("mp", "dp")),
            P("mp", "dp"),
            P("dp"),
            P("dp"),
            P("dp"),
        ),
        check_vma=False,
    )
```

```python
import functools

import jax
import jax.numpy as jnp
from jax import lax
from jax.experimental import pallas as pl
from jax.experimental.pallas import tpu as pltpu
from jax.sharding import PartitionSpec as P

HD = 64
PAIR = 2 * HD
BLOCK = 256
HALF = 2 * BLOCK
NORM_EPS = 1e-05
BF = jnp.bfloat16
F32 = jnp.float32
AXES = ("dp", "mp")
NN = (((1,), (0,)), ((), ()))
NT = (((1,), (1,)), ((), ()))
TN = (((0,), (0,)), ((), ()))
SMALL = 128


def mm(first, second, dims):
    return lax.dot_general(first, second, dims, preferred_element_type=F32)


def cost(microseconds):
    return pl.CostEstimate(
        flops=int(microseconds * 4 * 1e9),
        transcendentals=0,
        bytes_accessed=int(microseconds * 4 * 3e6),
    )


def pairs_of(step):
    moves = []
    for d in range(16):
        for m in range(2):
            d2, m2 = step(d, m)
            moves.append((2 * d + m, 2 * d2 + m2))
    return moves


MOVE_X = pairs_of(lambda d, m: (d, 1 - m))
MOVE_Y = pairs_of(lambda d, m: (d ^ 2, m))
MOVE_CORE = pairs_of(lambda d, m: (d ^ 1, m))
MOVE_Z = [pairs_of(lambda d, m, k=k: ((d + 4 * k) % 16, m)) for k in (1, 2, 3)]
MOVE_FIRST = pairs_of(lambda d, m: (d ^ 2, m) if d & 1 else (d, 1 - m))
MOVE_SECOND = pairs_of(lambda d, m: (d, 1 - m) if d & 1 else (d ^ 2, m))


MOVE_REDUCE = MOVE_SECOND, MOVE_FIRST


def move(values, moves):
    return lax.ppermute(values, AXES, moves)


def swap_mp(values):
    return lax.ppermute(values, "mp", [(0, 1), (1, 0)])


def started(copies):
    for copy in copies:
        copy.start()
    return copies


def piece_copies(where, pieces, target, sem, by_core=False):
    if len(pieces[0].shape) == 4:
        (whole,) = pieces
        count, _, rows, _ = whole.shape
        return started(
            [
                pltpu.make_async_copy(
                    whole.at[d, where[3] ^ half],
                    target.at[half, pl.ds(d * rows, rows), :],
                    sem.at[(half * count + d) // 4, d % 4],
                )
                for half in range(2)
                for d in range(count)
            ]
        )
    if len(pieces[0].shape) == 2:
        return started(
            [pltpu.make_async_copy(p, target.at[n], sem.at[n, 0]) for n, p in enumerate(pieces)]
        )
    rows = pieces[0].shape[1]
    z, y, core = where[0], where[1], where[2]

    def copies(ref, half, dy, dcore, slot):
        out = []
        for k in range(4):
            block = ((lax.rem(z + 4 - k, 4) * 2 + (y ^ dy)) * 2 + (core ^ dcore)) * rows
            block = pl.multiple_of(block, 16)
            out.append(
                pltpu.make_async_copy(
                    ref.at[k], target.at[half, pl.ds(block, rows), :], sem.at[slot, k]
                )
            )
        return out

    waits = []
    if not by_core:
        for slot, ref in enumerate(pieces):
            waits += copies(ref, slot // 4, slot % 2, slot % 4 // 2, slot)
        return started(waits)

    z0, a0, b0, c0, z1, a1, b1, c1 = pieces
    first = core == 0
    for slot, (ref, half, dy, dcore) in enumerate(
        ((z0, 0, 0, 0), (c0, 1, 1, 0), (z1, 0, 0, 1), (c1, 1, 1, 1))
    ):
        waits += copies(ref, half, dy, dcore, slot)
    started(waits)
    for slot, (ref_if, ref_else, half, dy, dcore) in enumerate(
        ((b0, a0, 0, 1, 0), (a0, b0, 1, 0, 0), (a1, b1, 0, 1, 1), (b1, a1, 1, 0, 1)), 4
    ):
        @pl.when(first)
        def _(ref=ref_if, half=half, dy=dy, dcore=dcore, slot=slot):
            started(copies(ref, half, dy, dcore, slot))

        @pl.when(jnp.logical_not(first))
        def _(ref=ref_else, half=half, dy=dy, dcore=dcore, slot=slot):
            started(copies(ref, half, dy, dcore, slot))

        waits += copies(ref_if, half, dy, dcore, slot)
    return waits


def device_of(rows, half, d_model):
    row = lax.broadcasted_iota(jnp.int32, (d_model, 1), 0)
    device = lax.div(row, jnp.int32(rows))
    return device, row - device * rows


def one_hot(target, cols):
    lane = lax.broadcasted_iota(jnp.int32, (target.shape[0], cols), 1)
    return jnp.where(lane == target, 1.0, 0.0).astype(BF)


def qv_places(rows, d_model):
    device, at = device_of(rows, rows // 2, d_model)
    value = (at >= rows // 2).astype(jnp.int32)
    target = value * (d_model // 2) + device * (rows // 2) + at - value * (rows // 2)
    return one_hot(target, d_model)


def up_places(rows, d_model, part, ff):
    device, at = device_of(rows, rows, d_model)
    return one_hot(device * (2 * rows) + part * rows + at, ff)


def project_kernel(rows, n_qkv, where, tok_ref, *refs):
    pieces = refs[:n_qkv]
    proj_ref, vec_ref, up_ref, weights, bias, sem = refs[n_qkv:]
    d_model = tok_ref.shape[1]
    span = proj_ref.shape[1]

    @pl.when(pl.program_id(0) == 0)
    def _():
        for copy in piece_copies(where, pieces, weights, sem):
            copy.wait()
        bias[...] = jnp.zeros_like(bias)
        qv = qv_places(rows, d_model)
        up = [up_places(rows, d_model, part, up_ref.shape[1]) for part in range(2)]
        turned = weights[0, :, span:].T[:16]
        vec_ref[...] = turned[:8].astype(F32)
        row = mm(turned, qv, NN)[8:9]
        for pair in range(span // (3 * PAIR)):
            at = pair * 3 * PAIR
            bias[0:1, at : at + PAIR] = row[:, pair * PAIR : (pair + 1) * PAIR]
            first = d_model // 2 + pair * PAIR
            bias[0:1, at + 2 * PAIR : at + 3 * PAIR] = row[:, first : first + PAIR]
        up_ref[...] = mm(turned, up[0], NN)[6:7] + mm(turned, up[1], NN)[7:8]

    tokens = tok_ref[...]
    for at in range(0, span, 384):
        proj_ref[:, at : at + 384] = (
            mm(tokens, weights[0, :, at : at + 384], NN) + bias[0:1, at : at + 384]
        ).astype(BF)


def project(where, tokens, pieces, rows, seq, span, ff, tile=512):
    d_model = tokens.shape[1]
    return pl.pallas_call(
        functools.partial(project_kernel, rows, len(pieces)),
        out_shape=(
            jax.ShapeDtypeStruct((seq, span), BF),
            jax.ShapeDtypeStruct((8, d_model), F32),
            jax.ShapeDtypeStruct((1, ff), F32),
        ),
        grid_spec=pltpu.PrefetchScalarGridSpec(
            num_scalar_prefetch=1,
            grid=(seq // tile,),
            in_specs=[own_tile(tile, d_model, seq)] + [ANYWHERE] * len(pieces),
            out_specs=[
                row_tile(tile, span),
                pl.BlockSpec((8, d_model), lambda i, w: (0, 0)),
                pl.BlockSpec((1, ff), lambda i, w: (0, 0)),
            ],
            scratch_shapes=[
                pltpu.VMEM((1, d_model, span + SMALL), BF),
                pltpu.VMEM((8, span), F32),
                pltpu.SemaphoreType.DMA((8, 4)),
            ],
        ),
        cost_estimate=cost(8.7),
        name="project",
    )(where, tokens, *pieces)


def last_kernel(n_qkv, where, own_ref, other_ref, one_ref, *refs):
    pieces = refs[:n_qkv]
    whole_ref, low_ref, weights, sem = refs[n_qkv:]
    span = own_ref.shape[1]

    @pl.when(pl.program_id(0) == 0)
    def _():
        for copy in piece_copies(where, pieces, weights, sem):
            copy.wait()

    total = (
        mm(own_ref[...], weights[0, :, :span], NT)
        + mm(other_ref[...], weights[1, :, :span], NT)
        + one_ref[...]
    )
    whole_ref[...] = total
    low_ref[...] = total.astype(BF)


def last_part(where, d_proj, d_one, pieces, tile=512):
    seq, span = d_proj[0].shape
    d_model = d_one.shape[1]
    return pl.pallas_call(
        functools.partial(last_kernel, len(pieces)),
        out_shape=(
            jax.ShapeDtypeStruct((2 * seq, d_model), F32),
            jax.ShapeDtypeStruct((seq, d_model), BF),
        ),
        grid_spec=pltpu.PrefetchScalarGridSpec(
            num_scalar_prefetch=1,
            grid=(seq // tile,),
            in_specs=[row_tile(tile, span), row_tile(tile, span), row_tile(tile, d_model)]
            + [ANYWHERE] * len(pieces),
            out_specs=[own_tile(tile, d_model, seq), row_tile(tile, d_model)],
            scratch_shapes=[
                pltpu.VMEM((2, d_model, span + SMALL), BF),
                pltpu.SemaphoreType.DMA((8, 4)),
            ],
        ),
        cost_estimate=cost(12.0),
        name="last_part",
    )(where, *d_proj, d_one, *pieces)


def part_copies(where, result, half, keep_ref, send_ref, sem, staged):
    if not staged:
        return [pltpu.make_async_copy(result.at[half], keep_ref.at[half], sem.at[half, 0])]
    if len(keep_ref.shape) == 4:
        rows = keep_ref.shape[2]
        return [
            pltpu.make_async_copy(
                result.at[half, pl.ds(d * rows, rows), :],
                keep_ref.at[d, where[3] ^ half],
                sem.at[half, d],
            )
            for d in range(keep_ref.shape[0])
        ]
    rows = keep_ref.shape[-2]
    z, y, core = where[0], where[1], where[2]
    out = []
    for dcore, target in enumerate((keep_ref, send_ref)):
        for dy in range(2):
            for k in range(4):
                block = ((lax.rem(z + k, 4) * 2 + (y ^ dy)) * 2 + (core ^ dcore)) * rows
                block = pl.multiple_of(block, 16)
                if target.shape[2] == 1:
                    place = target.at[dy, k, 0]
                else:
                    by_y = (core ^ dcore) == 0
                    place = target.at[jnp.where(by_y, dy, half), jnp.where(by_y, half, dy), k]
                out.append(
                    pltpu.make_async_copy(
                        result.at[half, pl.ds(block, rows), :], place, sem.at[half, len(out)]
                    )
                )
    return out


def part_shapes(staged, halves, d_model, cols):
    if not staged:
        whole = jax.ShapeDtypeStruct((halves, d_model, cols), BF)
        return whole, jax.ShapeDtypeStruct((8, 128), BF)
    rows = d_model // 16
    dims = (2, 4, 1, rows, cols) if halves == 1 else (2, 2, 4, rows, cols)
    return (jax.ShapeDtypeStruct(dims, BF),) * 2


def after(value, *others):
    return lax.optimization_barrier((value, *others))[0]


def grads_kernel(staged, rows, halves, widths, n_extra, where, *refs):
    count = len(widths)
    lhs_refs, refs = refs[:count], refs[count:]
    rhs_refs, refs = refs[: count * halves], refs[count * halves :]
    extra_refs, refs = refs[:n_extra], refs[n_extra:]
    keep_ref, send_ref, result, turned, sem = refs
    d_model = result.shape[1]
    for lhs, out in zip(lhs_refs, range(count)):
        for at in range(0, lhs.shape[0], BLOCK):
            turned[out, :, at : at + BLOCK] = lhs[at : at + BLOCK, :].T
    for half in range(halves):
        first = 0
        for n in range(count):
            rhs = rhs_refs[n * halves + half]
            rhs = rhs.at[half] if len(rhs.shape) == 3 else rhs
            width = rhs.shape[1]
            for at in range(0, width, 384):
                result[half, :, first + at : first + at + 384] = mm(
                    turned[n], rhs[:, at : at + 384], NN
                ).astype(BF)
            first += width
        if n_extra == 1:
            (sums,) = extra_refs
            blank = jnp.zeros((SMALL - 1, PAIR), F32)
            parts = [
                sums[pair, 0:1, n * PAIR : (n + 1) * PAIR]
                for n in (0, 2)
                for pair in range(sums.shape[0])
            ]
            line = jnp.concatenate(parts, axis=1)
            lines = jnp.concatenate([line, jnp.zeros((SMALL - 1, line.shape[1]), F32)], axis=0)
            extra = mm(qv_places(rows, d_model), lines.astype(BF), NT)
        else:
            two, one, up = extra_refs
            own = one_hot(lax.broadcasted_iota(jnp.int32, (d_model, 1), 0), d_model)
            zero = jnp.zeros((SMALL - 6, d_model), F32)
            lines = jnp.concatenate([one[2:3], one[0:2], two[2:3], two[0:2], zero], axis=0)
            extra = mm(own, lines.astype(BF), NT)
            blank = jnp.zeros((SMALL - 8, up.shape[2]), F32)
            for part in range(2):
                line = up[half, 0:1]
                before = jnp.zeros((6 + part, line.shape[1]), F32)
                behind = jnp.zeros((SMALL - 7 - part, line.shape[1]), F32)
                lines = jnp.concatenate([before, line, behind], axis=0)
                extra = extra + mm(
                    up_places(rows, d_model, part, line.shape[1]), lines.astype(BF), NT
                )
        result[half, :, first:] = extra.astype(BF)
        for copy in part_copies(where, result, half, keep_ref, send_ref, sem, staged):
            copy.start()
    for half in range(halves):
        for copy in part_copies(where, result, half, keep_ref, send_ref, sem, staged):
            copy.wait()


def whole_spec(array):
    return pl.BlockSpec(array.shape, lambda i, w, n=array.ndim: (0,) * n)


def own_tile(tile, width, seq):
    return pl.BlockSpec((tile, width), lambda i, w: (w[3] * (seq // tile) + i, 0))


def grads(where, staged, rows, lhs, rhs, extra):
    halves = len(rhs[0])
    seq = rhs[0][0].shape[-2]
    d_model = lhs[0].shape[1]
    widths = [r[0].shape[-1] for r in rhs]
    cols = sum(widths) + SMALL
    operands = [*(r for pair in rhs for r in pair), *extra]
    return pl.pallas_call(
        functools.partial(grads_kernel, staged, rows, halves, widths, len(extra)),
        out_shape=part_shapes(staged, halves, d_model, cols),
        grid_spec=pltpu.PrefetchScalarGridSpec(
            num_scalar_prefetch=1,
            grid=(1,),
            in_specs=[
                own_tile(seq, d_model, seq) if l.shape[0] > seq else whole_spec(l) for l in lhs
            ]
            + [whole_spec(o) for o in operands],
            out_specs=[ANYWHERE] * 2,
            scratch_shapes=[
                pltpu.VMEM((halves, d_model, cols), BF),
                pltpu.VMEM((len(lhs), d_model, seq), BF),
                pltpu.SemaphoreType.DMA((halves, 16)),
            ],
        ),
        cost_estimate=cost(20.0 if halves == 2 else 7.2),
        name="grads",
    )(where, *lhs, *operands)


def row_norm(values):
    centered = values - jnp.mean(values, axis=-1, keepdims=True)
    inverse = lax.rsqrt(jnp.mean(centered * centered, axis=-1, keepdims=True) + NORM_EPS)
    return centered * inverse, inverse


def row_norm_back(d_normed, z, inverse, gain):
    dz = d_normed * gain
    return (
        dz - jnp.mean(dz, axis=-1, keepdims=True) - z * jnp.mean(dz * z, axis=-1, keepdims=True)
    ) * inverse


def column_sum(values):
    return jnp.sum(values, axis=0, keepdims=True)


def first_kernel(n_up, where, tok_ref, ctx0_ref, ctx1_ref, vec_ref, bias0_ref, bias1_ref, *refs):
    pieces = refs[:n_up]
    z_ref, inv_ref, hid_ref, slope_ref, weights, sem = refs[n_up:]
    bias_refs = bias0_ref, bias1_ref
    width = ctx0_ref.shape[1]

    @pl.when(pl.program_id(0) == 0)
    def _():
        for copy in piece_copies(where, pieces, weights, sem, True):
            copy.wait()

    resid = (
        tok_ref[...].astype(F32)
        + mm(ctx0_ref[...], weights[0, :, :width], NT)
        + mm(ctx1_ref[...], weights[1, :, :width], NT)
        + vec_ref[0:1]
    )
    z, inverse = row_norm(resid)
    z_ref[...] = z
    inv_ref[...] = jnp.broadcast_to(inverse, inv_ref.shape)
    low = (z * vec_ref[1:2] + vec_ref[2:3]).astype(BF)
    ff = hid_ref.shape[2]
    for half in range(2):
        for at in range(0, ff, 512):
            pre = mm(low, weights[half, :, width + at : width + at + 512], NN)
            gelu, slope = gelu_both(pre + bias_refs[half][:, at : at + 512])
            hid_ref[half, :, at : at + 512] = gelu.astype(BF)
            slope_ref[half, :, at : at + 512] = slope.astype(BF)


def row_tile(tile, width):
    return pl.BlockSpec((tile, width), lambda i, w: (i, 0))


def halves_tile(tile, width):
    return pl.BlockSpec((2, tile, width), lambda i, w: (0, i, 0))


ANYWHERE = pl.BlockSpec(memory_space=pl.ANY)


def first_part(where, tokens, ctx, vectors, bias, pieces, tile=256):
    d_model = tokens.shape[1]
    seq = ctx[0].shape[0]
    width, ff = ctx[0].shape[1], bias[0].shape[1]
    return pl.pallas_call(
        functools.partial(first_kernel, len(pieces)),
        out_shape=(
            jax.ShapeDtypeStruct((seq, d_model), F32),
            jax.ShapeDtypeStruct((seq, 128), F32),
            jax.ShapeDtypeStruct((2, seq, ff), BF),
            jax.ShapeDtypeStruct((2, seq, ff), BF),
        ),
        grid_spec=pltpu.PrefetchScalarGridSpec(
            num_scalar_prefetch=1,
            grid=(seq // tile,),
            in_specs=[
                own_tile(tile, d_model, seq),
                row_tile(tile, width),
                row_tile(tile, width),
                whole_spec(vectors),
                whole_spec(bias[0]),
                whole_spec(bias[1]),
            ]
            + [ANYWHERE] * len(pieces),
            out_specs=[
                row_tile(tile, d_model),
                row_tile(tile, 128),
                halves_tile(tile, ff),
                halves_tile(tile, ff),
            ],
            scratch_shapes=[
                pltpu.VMEM((2, d_model, width + ff), BF),
                pltpu.SemaphoreType.DMA((8, 4)),
            ],
        ),
        cost_estimate=cost(19.4),
        name="first_part",
    )(where, tokens, *ctx, vectors, *bias, *pieces)


def second_kernel(staged, n_down, where, hid_ref, z_ref, cot_ref, vec_ref, *refs):
    pieces = refs[:n_down]
    out_ref, own_ref, d_ref, sum_ref, keep_ref, *refs = refs[n_down:]
    weights, turned, kept, result, sem, out_sem = refs
    step = pl.program_id(0)
    tile, ff = hid_ref.shape[1:]

    @pl.when(step == 0)
    def _():
        for copy in piece_copies(where, pieces, weights, sem):
            copy.wait()
        sum_ref[...] = jnp.zeros_like(sum_ref)

    ffn = mm(hid_ref[0], weights[0], NT) + mm(hid_ref[1], weights[1], NT)
    resid = z_ref[...] * vec_ref[1:2] + vec_ref[2:3] + ffn + vec_ref[3:4]
    z, inverse = row_norm(resid)
    out = (z * vec_ref[4:5] + vec_ref[5:6]).astype(BF)
    out_ref[...] = out
    own_ref[...] = out
    cot = cot_ref[...].astype(F32)
    d_two = row_norm_back(cot, z, inverse, vec_ref[4:5])
    d_ref[...] = d_two
    sum_ref[0:1] += column_sum(cot * z)
    sum_ref[1:2] += column_sum(cot)
    sum_ref[2:3] += column_sum(d_two)
    rows = pl.ds(pl.multiple_of(step * tile, tile), tile)
    turned[:, rows] = d_two.astype(BF).T
    kept[:, rows, :] = hid_ref[...]

    @pl.when(step == pl.num_programs(0) - 1)
    def _():
        for half in range(2):
            for at in range(0, ff, 512):
                result[half, :, at : at + 512] = mm(
                    turned[...], kept[half, :, at : at + 512], NN
                ).astype(BF)
            for copy in part_copies(where, result, half, keep_ref, None, out_sem, staged):
                copy.start()
        for half in range(2):
            for copy in part_copies(where, result, half, keep_ref, None, out_sem, staged):
                copy.wait()


def second_part(where, staged, hidden, z_one, cot, vectors, pieces, tile=256):
    _, seq, ff = hidden.shape
    d_model = z_one.shape[1]
    return pl.pallas_call(
        functools.partial(second_kernel, staged, len(pieces)),
        out_shape=(
            jax.ShapeDtypeStruct((2 * seq, d_model), BF),
            jax.ShapeDtypeStruct((seq, d_model), BF),
            jax.ShapeDtypeStruct((seq, d_model), F32),
            jax.ShapeDtypeStruct((8, d_model), F32),
            (
                jax.ShapeDtypeStruct((16, 2, d_model // 16, ff), BF)
                if staged
                else jax.ShapeDtypeStruct((2, d_model, ff), BF)
            ),
        ),
        grid_spec=pltpu.PrefetchScalarGridSpec(
            num_scalar_prefetch=1,
            grid=(seq // tile,),
            in_specs=[
                halves_tile(tile, ff),
                row_tile(tile, d_model),
                own_tile(tile, d_model, seq),
                whole_spec(vectors),
            ]
            + [ANYWHERE] * len(pieces),
            out_specs=[
                own_tile(tile, d_model, seq),
                row_tile(tile, d_model),
                row_tile(tile, d_model),
                pl.BlockSpec((8, d_model), lambda i, w: (0, 0)),
                ANYWHERE,
            ],
            scratch_shapes=[
                pltpu.VMEM((2, d_model, ff), BF),
                pltpu.VMEM((d_model, seq), BF),
                pltpu.VMEM((2, seq, ff), BF),
                pltpu.VMEM((2, d_model, ff), BF),
                pltpu.SemaphoreType.DMA((8, 4)),
                pltpu.SemaphoreType.DMA((2, 16)),
            ],
        ),
        cost_estimate=cost(21.8),
        name="second_part",
    )(where, hidden, z_one, cot, vectors, *pieces)


def third_kernel(n_up, n_down, where, d_ref, slope_ref, z_ref, inv_ref, vec_ref, *refs):
    up_pieces, down_pieces, refs = refs[:n_up], refs[n_up : n_up + n_down], refs[n_up + n_down :]
    pre_ref, low_ref, one_ref, one_low_ref, ctx_ref, sum_ref, bias_ref, *refs = refs
    up, down, sem, down_sem = refs
    step = pl.program_id(0)
    ff = slope_ref.shape[2]
    width = ctx_ref.shape[2]

    @pl.when(step == 0)
    def _():
        waits = piece_copies(where, down_pieces, down, down_sem)
        waits += piece_copies(where, up_pieces, up, sem, True)
        for copy in waits:
            copy.wait()
        sum_ref[...] = jnp.zeros_like(sum_ref)
        bias_ref[...] = jnp.zeros_like(bias_ref)

    d_two = d_ref[...]
    d_two_low = d_two.astype(BF)
    d_normed = d_two
    for half in range(2):
        for at in range(0, ff, 512):
            span = slice(at, at + 512)
            d_pre = mm(d_two_low, down[half, :, span], NN) * slope_ref[half, :, span].astype(F32)
            d_pre = d_pre.astype(BF)
            pre_ref[half, :, span] = d_pre
            bias_ref[half, 0:1, span] += column_sum(d_pre.astype(F32))
            d_normed = d_normed + mm(d_pre, up[half, :, width + at : width + at + 512], NT)
    z = z_ref[...]
    low_ref[...] = (z * vec_ref[1:2] + vec_ref[2:3]).astype(BF)
    d_one = row_norm_back(d_normed, z, inv_ref[:, 0:1], vec_ref[1:2])
    one_ref[...] = d_one
    sum_ref[0:1] += column_sum(d_normed * z)
    sum_ref[1:2] += column_sum(d_normed)
    sum_ref[2:3] += column_sum(d_one)
    d_one_low = d_one.astype(BF)
    one_low_ref[...] = d_one_low
    for half in range(2):
        ctx_ref[half] = mm(d_one_low, up[half, :, :width], NN).astype(BF)


def third_part(where, d_two, slope, z_one, inv_one, vectors, up_pieces, down_pieces, width, tile=256):
    seq, d_model = d_two.shape
    ff = slope.shape[2]
    return pl.pallas_call(
        functools.partial(third_kernel, len(up_pieces), len(down_pieces)),
        out_shape=(
            jax.ShapeDtypeStruct((2, seq, ff), BF),
            jax.ShapeDtypeStruct((seq, d_model), BF),
            jax.ShapeDtypeStruct((seq, d_model), F32),
            jax.ShapeDtypeStruct((seq, d_model), BF),
            jax.ShapeDtypeStruct((2, seq, width), BF),
            jax.ShapeDtypeStruct((8, d_model), F32),
            jax.ShapeDtypeStruct((2, 8, ff), F32),
        ),
        grid_spec=pltpu.PrefetchScalarGridSpec(
            num_scalar_prefetch=1,
            grid=(seq // tile,),
            in_specs=[
                row_tile(tile, d_model),
                halves_tile(tile, ff),
                row_tile(tile, d_model),
                row_tile(tile, 128),
                whole_spec(vectors),
            ]
            + [ANYWHERE] * (len(up_pieces) + len(down_pieces)),
            out_specs=[
                halves_tile(tile, ff),
                row_tile(tile, d_model),
                row_tile(tile, d_model),
                row_tile(tile, d_model),
                halves_tile(tile, width),
                pl.BlockSpec((8, d_model), lambda i, w: (0, 0)),
                pl.BlockSpec((2, 8, ff), lambda i, w: (0, 0, 0)),
            ],
            scratch_shapes=[
                pltpu.VMEM((2, d_model, width + ff), BF),
                pltpu.VMEM((2, d_model, ff), BF),
                pltpu.SemaphoreType.DMA((8, 4)),
                pltpu.SemaphoreType.DMA((8, 4)),
            ],
        ),
        cost_estimate=cost(25.6),
        name="third_part",
    )(where, d_two, slope, z_one, inv_one, vectors, *up_pieces, *down_pieces)


def add(first, second):
    return (first.astype(F32) + second.astype(F32)).astype(BF)


def core_stage(keep, send):
    return move(send, MOVE_CORE), keep


def flip_stage(moves, got, keep):
    return move(add(keep[1], got[1]), moves), add(keep[0], got[0])


def z_stage(*terms):
    sums = [functools.reduce(jnp.add, [t[k].astype(F32) for t in terms]) for k in range(4)]
    parts = [move(part.astype(BF), moves) for part, moves in zip(sums[1:], MOVE_Z)]
    return parts, sums[0]


def z_sum(parts, keep):
    return keep + parts[0].astype(F32) + parts[1].astype(F32) + parts[2].astype(F32)


def lane_mask(head, rows):
    lanes = lax.broadcasted_iota(jnp.int32, (rows, PAIR), 1)
    return (lanes < HD) if head == 0 else (lanes >= HD)


def attn_fwd_kernel(table, qkv_ref, ctx_ref, prob_ref):
    pair = pl.program_id(0)
    q_ref, k_ref, v_ref = (qkv_ref.at[:, n * PAIR : (n + 1) * PAIR] for n in range(3))
    lanes = lax.broadcasted_iota(jnp.int32, (1, HALF), 1)
    for half in range(2):
        rows = pl.ds(half * HALF, HALF)
        query = q_ref[rows, :] * jnp.asarray(HD**-0.5, BF)
        parts = []
        for head in range(2):
            at = (pair * 2 + head) * 4
            start = (half ^ table[at]) * HALF
            flags = [table[at + 1 + n] == 1 for n in range(3)]
            key_lo = k_ref[pl.ds(pl.multiple_of(start, BLOCK), BLOCK), :]
            key_hi = k_ref[pl.ds(pl.multiple_of(start + BLOCK, BLOCK), BLOCK), :]
            masked = jnp.where(lane_mask(head, HALF), query, jnp.zeros_like(query))
            score_lo = mm(key_lo, masked, NT)
            score_hi = mm(key_hi, masked[BLOCK:], NT)
            no_lo = jnp.where(
                lanes < BLOCK,
                jnp.where(flags[0], 0.0, -1e30),
                jnp.where(flags[1], 0.0, -1e30),
            ).astype(F32)
            no_hi = jnp.where(flags[2], 0.0, -1e30).astype(F32)
            top_lo = jnp.max(score_lo, axis=0, keepdims=True) + no_lo
            top_hi = jnp.max(score_hi, axis=0, keepdims=True) + no_hi
            top = jnp.concatenate(
                [top_lo[:, :BLOCK], jnp.maximum(top_lo[:, BLOCK:], top_hi)], axis=1
            )
            ref_lo = jnp.where(no_lo < 0.0, 1e30, top)
            ref_hi = jnp.where(no_hi < 0.0, 1e30, top[:, BLOCK:])
            exp_lo = jnp.exp(score_lo - ref_lo)
            exp_hi = jnp.exp(score_hi - ref_hi)
            sum_lo = jnp.sum(exp_lo, axis=0, keepdims=True)
            sum_hi = jnp.sum(exp_hi, axis=0, keepdims=True)
            total = jnp.concatenate([sum_lo[:, :BLOCK], sum_lo[:, BLOCK:] + sum_hi], axis=1)
            scale = jnp.where(total > 0.0, 1.0 / jnp.where(total > 0.0, total, 1.0), 0.0)
            prob_lo = (exp_lo * scale).astype(BF)
            prob_hi = (exp_hi * scale[:, BLOCK:]).astype(BF)
            prob_ref[0, head, half, :, :HALF] = prob_lo
            prob_ref[0, head, half, :, HALF:] = prob_hi
            val_lo = v_ref[pl.ds(pl.multiple_of(start, BLOCK), BLOCK), :].T
            val_hi = v_ref[pl.ds(pl.multiple_of(start + BLOCK, BLOCK), BLOCK), :].T
            side = slice(head * HD, (head + 1) * HD)
            out_lo = mm(val_lo[side], prob_lo, NN)
            out_hi = mm(val_hi[side], prob_hi, NN)
            parts.append(
                jnp.concatenate([out_lo[:, :BLOCK], out_lo[:, BLOCK:] + out_hi], axis=1)
            )
        ctx_ref[rows, :] = jnp.concatenate(parts, axis=0).T.astype(BF)


def attn_fwd(table, proj):
    seq, width = proj.shape
    pairs = width // 3 // PAIR
    return pl.pallas_call(
        attn_fwd_kernel,
        out_shape=(
            jax.ShapeDtypeStruct((seq, width // 3), BF),
            jax.ShapeDtypeStruct((pairs, 2, 2, BLOCK, HALF + BLOCK), BF),
        ),
        grid_spec=pltpu.PrefetchScalarGridSpec(
            num_scalar_prefetch=1,
            grid=(pairs,),
            in_specs=[pl.BlockSpec((seq, 3 * PAIR), lambda p, t: (0, p))],
            out_specs=[
                pl.BlockSpec((seq, PAIR), lambda p, t: (0, p)),
                pl.BlockSpec((1, 2, 2, BLOCK, HALF + BLOCK), lambda p, t: (p, 0, 0, 0, 0)),
            ],
        ),
        cost_estimate=cost(0.5),
        name="attn_fwd",
    )(table, proj)


def attn_bwd_kernel(table, qkv_ref, d_ref, prob_ref, out_ref, sum_ref, k_acc, v_acc):
    pair = pl.program_id(0)
    q_ref, k_ref, v_ref = (qkv_ref.at[:, n * PAIR : (n + 1) * PAIR] for n in range(3))
    for half in range(2):
        rows = pl.ds(half * HALF, HALF)
        query = q_ref[rows, :] * jnp.asarray(HD**-0.5, BF)
        d_ctx = d_ref[rows, :]
        parts = []
        for head in range(2):
            at = (pair * 2 + head) * 4
            start = (half ^ table[at]) * HALF
            at_lo = pl.ds(pl.multiple_of(start, BLOCK), BLOCK)
            at_hi = pl.ds(pl.multiple_of(start + BLOCK, BLOCK), BLOCK)
            keep = lane_mask(head, HALF)
            query_h = jnp.where(keep, query, jnp.zeros_like(query))
            d_ctx_h = jnp.where(keep, d_ctx, jnp.zeros_like(d_ctx))
            prob_lo = prob_ref[0, head, half, :, :HALF]
            prob_hi = prob_ref[0, head, half, :, HALF:]
            d_w_lo = mm(v_ref[at_lo, :], d_ctx_h, NT)
            d_w_hi = mm(v_ref[at_hi, :], d_ctx_h[BLOCK:], NT)
            wide_lo = prob_lo.astype(F32)
            wide_hi = prob_hi.astype(F32)
            dot_lo = jnp.sum(wide_lo * d_w_lo, axis=0, keepdims=True)
            dot_hi = jnp.sum(wide_hi * d_w_hi, axis=0, keepdims=True)
            dot = jnp.concatenate([dot_lo[:, :BLOCK], dot_lo[:, BLOCK:] + dot_hi], axis=1)
            d_s_lo = (wide_lo * (d_w_lo - dot)).astype(BF)
            d_s_hi = (wide_hi * (d_w_hi - dot[:, BLOCK:])).astype(BF)
            dk_lo = mm(d_s_lo, query_h, NN)
            dk_hi = mm(d_s_hi, query_h[BLOCK:], NN)
            dv_lo = mm(prob_lo, d_ctx_h, NN)
            dv_hi = mm(prob_hi, d_ctx_h[BLOCK:], NN)
            k_acc[head, at_lo, :] = dk_lo
            k_acc[head, at_hi, :] = dk_hi
            v_acc[head, at_lo, :] = dv_lo
            v_acc[head, at_hi, :] = dv_hi
            key_lo = k_ref[at_lo, :].T
            key_hi = k_ref[at_hi, :].T
            side = slice(head * HD, (head + 1) * HD)
            dq_lo = mm(key_lo[side], d_s_lo, NN)
            dq_hi = mm(key_hi[side], d_s_hi, NN)
            parts.append(jnp.concatenate([dq_lo[:, :BLOCK], dq_lo[:, BLOCK:] + dq_hi], axis=1))
        out_ref[rows, :PAIR] = (jnp.concatenate(parts, axis=0).T * HD**-0.5).astype(BF)
    out_ref[:, PAIR : 2 * PAIR] = (k_acc[0] + k_acc[1]).astype(BF)
    out_ref[:, 2 * PAIR :] = (v_acc[0] + v_acc[1]).astype(BF)
    sums = jnp.sum(out_ref[...].astype(F32), axis=0, keepdims=True)
    sum_ref[0] = jnp.broadcast_to(sums, sum_ref.shape[1:])


def attn_bwd(table, proj, d_context, half, probs):
    seq, width = proj.shape
    pairs = width // 3 // PAIR
    return pl.pallas_call(
        attn_bwd_kernel,
        out_shape=(
            jax.ShapeDtypeStruct((seq, width), BF),
            jax.ShapeDtypeStruct((pairs, 8, 3 * PAIR), F32),
        ),
        grid_spec=pltpu.PrefetchScalarGridSpec(
            num_scalar_prefetch=1,
            grid=(pairs,),
            in_specs=[
                pl.BlockSpec((seq, 3 * PAIR), lambda p, t: (0, p)),
                pl.BlockSpec((None, seq, PAIR), lambda p, t: (half, 0, p)),
                pl.BlockSpec((1, 2, 2, BLOCK, HALF + BLOCK), lambda p, t: (p, 0, 0, 0, 0)),
            ],
            out_specs=[
                pl.BlockSpec((seq, 3 * PAIR), lambda p, t: (0, p)),
                pl.BlockSpec((1, 8, 3 * PAIR), lambda p, t: (p, 0, 0)),
            ],
            scratch_shapes=[pltpu.VMEM((2, seq, PAIR), F32)] * 2,
        ),
        cost_estimate=cost(11.3),
        name="attn_bwd",
    )(table, proj, d_context, probs)


def gelu_both(values):
    half = 0.5 * (1.0 + lax.erf(values * (0.5**0.5)))
    slope = half + values * jnp.exp(-0.5 * values * values) * 0.3989422804014327
    return values * half, slope


def body(
    dp_size,
    tokens,
    grad_out,
    head_perm,
    block_mask,
    w_qkv,
    b_qv,
    w_out,
    b_out,
    gain_one,
    shift_one,
    w_up,
    b_up,
    w_down,
    b_down,
    gain_two,
    shift_two,
):
    seq = tokens.shape[0] // head_perm.shape[0]
    rows = w_qkv.shape[0]
    width = w_qkv.shape[2]
    d_model = tokens.shape[1]
    dp_at = lax.axis_index("dp")
    mp_at = lax.axis_index("mp")
    where = jnp.stack([dp_at // 4, (dp_at // 2) % 2, dp_at % 2, mp_at]).astype(jnp.int32)

    table = jnp.concatenate([head_perm[:, :, None], block_mask], axis=2).astype(jnp.int32)
    table = table.reshape(2, -1)
    table_own = lax.dynamic_index_in_dim(table, mp_at, 0, keepdims=False)
    table_other = swap_mp(lax.dynamic_index_in_dim(table, 1 - mp_at, 0, keepdims=False))

    small = jnp.stack(
        [
            b_out,
            gain_one,
            shift_one,
            b_down,
            gain_two,
            shift_two,
            b_up[:rows],
            b_up[rows:],
            b_qv.reshape(-1),
        ],
        axis=1,
    )
    small = jnp.pad(small, ((0, 0), (0, SMALL - small.shape[1])))
    pairs = width // PAIR
    by_pair = w_qkv.reshape(rows, 3, pairs, PAIR).transpose(0, 2, 1, 3).reshape(rows, 3 * width)
    shard_qkv = jnp.concatenate([by_pair, small], axis=1)
    shard_up = jnp.concatenate([w_out.T, w_up], axis=1)
    shard_down = w_down.T
    staged = dp_size == 16

    def plain_gather(shard):
        full = lax.all_gather(shard, "dp", axis=0, tiled=True)
        return full, swap_mp(full)

    def gather_z(shard):
        return jnp.stack([shard] + [move(shard, moves) for moves in MOVE_Z])

    def gather_core(*pieces):
        return (*pieces, *(move(piece, MOVE_CORE) for piece in pieces))

    if staged:
        qkv_z = gather_z(shard_qkv)
        qkv_y = move(qkv_z, MOVE_Y)
        qkv_x = move(qkv_z, MOVE_X)
        up_parts = [move(after(shard_up, qkv_z), moves) for moves in MOVE_Z]
        down_whole = lax.all_gather(after(shard_down, qkv_z), AXES)
        down_pieces = (down_whole.reshape(dp_size, 2, *shard_down.shape),)
        qkv_y, *up_parts = lax.optimization_barrier((qkv_y, *up_parts))
        qkv_own = gather_core(qkv_z, qkv_y)
        qkv_xy = move(qkv_y, MOVE_X)
        up_z = jnp.stack([shard_up, *up_parts])
        tokens_in, table_other, qkv_x, up_z = lax.optimization_barrier(
            (tokens, table_other, qkv_x, up_z)
        )
        up_a, up_b = move(up_z, MOVE_FIRST), move(up_z, MOVE_SECOND)
    else:
        qkv_own, qkv_other = ((piece,) for piece in plain_gather(shard_qkv))
        up_pieces = plain_gather(shard_up)
        down_pieces = plain_gather(shard_down)
        tokens_in = tokens

    ff = w_up.shape[1]

    def project_half(values, pieces):
        return project(where, values, pieces, rows, seq, 3 * width, ff)

    proj_own, vectors, bias_own = project_half(tokens_in, qkv_own)
    if staged:
        proj_own, qkv_xy = lax.optimization_barrier((proj_own, qkv_xy))
        qkv_other = gather_core(qkv_x, qkv_xy)
    ctx_own, probs_own = attn_fwd(table_own, proj_own)
    if staged:
        ctx_own, up_a = lax.optimization_barrier((ctx_own, up_a))
    proj_other, _, bias_other = project_half(after(tokens, ctx_own), qkv_other)
    if staged:
        proj_other, up_a = lax.optimization_barrier((proj_other, up_a))
        up_c = move(up_a, MOVE_SECOND)
        up_pieces = gather_core(up_z, up_a, up_b)
    ctx_other, probs_other = attn_fwd(table_other, proj_other)
    if staged:
        ctx_other, up_c = lax.optimization_barrier((ctx_other, up_c))
        up_pieces = (*up_pieces[:3], up_c, *up_pieces[3:], move(up_c, MOVE_CORE))
    tables, proj = (table_own, table_other), (proj_own, proj_other)
    probs = (probs_own, probs_other)
    ctx = (ctx_own, ctx_other)
    qkv_pieces = (*qkv_own, *qkv_other)
    z_one, inv_one, hidden, slope = first_part(
        where, tokens, ctx, vectors, (bias_own, bias_other), up_pieces
    )

    def place(whole, other):
        return lax.dynamic_update_slice_in_dim(
            whole, other.astype(whole.dtype), (1 - mp_at) * seq, 0
        )

    out_whole, out_own, d_two, sums_two, down_grad = second_part(
        where, staged, hidden, z_one, grad_out, vectors, down_pieces
    )
    out_other = swap_mp(out_own)

    def plain_scatter(own, other):
        summed = own.astype(F32) + swap_mp(other).astype(F32)
        return lax.psum_scatter(summed, "dp", scatter_dimension=0, tiled=True)

    if staged:
        down_grad = down_grad.reshape(2 * dp_size, *shard_down.shape)
        s_down = lax.psum_scatter(down_grad, AXES, scatter_dimension=0).astype(F32)
    else:
        s_down = plain_scatter(*down_grad)
    d_pre, normed_low, d_one, d_one_low, d_ctx, sums_one, sums_up = third_part(
        where, d_two, slope, z_one, inv_one, vectors, up_pieces, down_pieces, width
    )
    up_parts = grads(
        where,
        staged,
        rows,
        [normed_low, d_one_low],
        [(d_pre, d_pre), ctx],
        (sums_two, sums_one, sums_up),
    )
    d_ctx_other = d_ctx
    if staged:
        up_got, up_keep = core_stage(*up_parts)
        d_ctx_other, out_other, up_keep = lax.optimization_barrier((d_ctx, out_other, up_keep))
    else:
        s_up = plain_scatter(*up_parts[0])
    d_proj_other, sums_other = attn_bwd(tables[1], proj[1], d_ctx_other, 1, probs[1])
    if staged:
        d_proj_other, up_got = lax.optimization_barrier((d_proj_other, up_got))
        up_got, up_keep = flip_stage(MOVE_REDUCE[0], up_got, up_keep)
        d_proj_other, up_keep = lax.optimization_barrier((d_proj_other, up_keep))
    other_parts = grads(where, staged, rows, [tokens], [(d_proj_other,)], (sums_other,))
    d_ctx_own = d_ctx
    if staged:
        qo_got, qo_keep = core_stage(*other_parts)
        d_ctx_own, qo_keep = lax.optimization_barrier((d_ctx, qo_keep))
    d_proj_own, sums_own = attn_bwd(tables[0], proj[0], d_ctx_own, 0, probs[0])
    d_proj_last = d_proj_own
    if staged:
        d_proj_own, up_got, qo_got = lax.optimization_barrier((d_proj_own, up_got, qo_got))
        up_got, up_keep = flip_stage(MOVE_REDUCE[1], up_got, up_keep)
        qo_got, qo_keep = flip_stage(MOVE_Y, qo_got, qo_keep)
        d_proj_last, up_keep, qo_keep = lax.optimization_barrier((d_proj_own, up_keep, qo_keep))
    d_input, in_low = last_part(where, (d_proj_last, d_proj_other), d_one, qkv_pieces)
    tokens_in = tokens
    if staged:
        in_both = lax.all_gather(in_low, "mp")
        tokens_in, in_low, up_got, qo_got = lax.optimization_barrier(
            (tokens, in_low, up_got, qo_got)
        )
        qo_in = move(add(qo_keep, qo_got), MOVE_X)
        up_parts, up_keep = z_stage(up_got, up_keep)
        tokens_in, up_keep = lax.optimization_barrier((tokens_in, up_keep))
    else:
        in_other = swap_mp(in_low)
    own_parts = grads(where, staged, rows, [tokens_in], [(d_proj_own,)], (sums_own,))
    if staged:
        qs_got, qs_keep = core_stage(*own_parts)
        qs_keep, *up_parts = lax.optimization_barrier((qs_keep, *up_parts))
        qs_got, qs_keep = flip_stage(MOVE_Y, qs_got, qs_keep)
        s_up = z_sum(up_parts, up_keep)
        qs_parts, qs_keep = z_stage(qs_got, qs_keep, qo_in)
        s_qkv = z_sum(qs_parts, qs_keep)[0]
        in_both, s_qkv = lax.optimization_barrier((in_both, s_qkv))
        in_other = lax.dynamic_index_in_dim(in_both, 1 - mp_at, 0, keepdims=False)
        d_input = place(d_input, in_other)
    else:
        d_input = place(d_input, in_other)
        s_qkv = plain_scatter(own_parts[0][0], other_parts[0][0])

    cols = s_up[:, ff + width :].T
    g_w_qkv = s_qkv[:, : 3 * width].reshape(rows, pairs, 3, PAIR).transpose(0, 2, 1, 3)
    return (
        place(out_whole, out_other),
        d_input,
        g_w_qkv.reshape(rows, 3, width),
        s_qkv[:, 3 * width].reshape(2, rows // 2),
        s_up[:, ff : ff + width].T,
        cols[0],
        cols[1],
        cols[2],
        s_up[:, :ff],
        cols[6:8].reshape(-1),
        s_down.T,
        cols[3],
        cols[4],
        cols[5],
    )


def solution(mesh):
    placed = (
        P("dp", None),
        P("dp", None),
        P("dp", "mp"),
        P("dp", "mp", None),
        P("dp", None, "mp"),
        P(None, ("mp", "dp")),
        P("mp", "dp"),
        P("dp"),
        P("dp"),
        P("dp"),
        P("dp", "mp"),
        P(("mp", "dp")),
        P("mp", "dp"),
        P("dp"),
        P("dp"),
        P("dp"),
    )
    return jax.shard_map(
        functools.partial(body, mesh.shape["dp"]),
        mesh=mesh,
        in_specs=placed,
        out_specs=(
            P("dp", None),
            P("dp", None),
            P("dp", None, "mp"),
            P(None, ("mp", "dp")),
            P("mp", "dp"),
            P("dp"),
            P("dp"),
            P("dp"),
            P("dp", "mp"),
            P(("mp", "dp")),
            P("mp", "dp"),
            P("dp"),
            P("dp"),
            P("dp"),
        ),
        check_vma=False,
    )
```

```python
import functools

import jax
import jax.numpy as jnp
from jax import lax
from jax.experimental import pallas as pl
from jax.experimental.pallas import tpu as pltpu
from jax.sharding import PartitionSpec as P

HD = 64
PAIR = 2 * HD
BLOCK = 256
HALF = 2 * BLOCK
NORM_EPS = 1e-05
BF = jnp.bfloat16
F32 = jnp.float32
AXES = ("dp", "mp")
NN = (((1,), (0,)), ((), ()))
NT = (((1,), (1,)), ((), ()))
TN = (((0,), (0,)), ((), ()))
SMALL = 128


def mm(first, second, dims):
    return lax.dot_general(first, second, dims, preferred_element_type=F32)


def cost(microseconds):
    return pl.CostEstimate(
        flops=int(microseconds * 4 * 1e9),
        transcendentals=0,
        bytes_accessed=int(microseconds * 4 * 3e6),
    )


def pairs_of(step):
    moves = []
    for d in range(16):
        for m in range(2):
            d2, m2 = step(d, m)
            moves.append((2 * d + m, 2 * d2 + m2))
    return moves


MOVE_X = pairs_of(lambda d, m: (d, 1 - m))
MOVE_Y = pairs_of(lambda d, m: (d ^ 2, m))
MOVE_CORE = pairs_of(lambda d, m: (d ^ 1, m))
MOVE_Z = [pairs_of(lambda d, m, k=k: ((d + 4 * k) % 16, m)) for k in (1, 2, 3)]
MOVE_FIRST = pairs_of(lambda d, m: (d ^ 2, m) if d & 1 else (d, 1 - m))
MOVE_SECOND = pairs_of(lambda d, m: (d, 1 - m) if d & 1 else (d ^ 2, m))


MOVE_REDUCE = MOVE_SECOND, MOVE_FIRST


def move(values, moves):
    return lax.ppermute(values, AXES, moves)


def swap_mp(values):
    return lax.ppermute(values, "mp", [(0, 1), (1, 0)])


def started(copies):
    for copy in copies:
        copy.start()
    return copies


def piece_copies(where, pieces, target, sem, by_core=False):
    if len(pieces[0].shape) == 4:
        (whole,) = pieces
        count, _, rows, _ = whole.shape
        return started(
            [
                pltpu.make_async_copy(
                    whole.at[d, where[3] ^ half],
                    target.at[half, pl.ds(d * rows, rows), :],
                    sem.at[(half * count + d) // 4, d % 4],
                )
                for half in range(2)
                for d in range(count)
            ]
        )
    if len(pieces[0].shape) == 2:
        return started(
            [pltpu.make_async_copy(p, target.at[n], sem.at[n, 0]) for n, p in enumerate(pieces)]
        )
    rows = pieces[0].shape[1]
    z, y, core = where[0], where[1], where[2]

    def copies(ref, half, dy, dcore, slot):
        out = []
        for k in range(4):
            block = ((lax.rem(z + 4 - k, 4) * 2 + (y ^ dy)) * 2 + (core ^ dcore)) * rows
            block = pl.multiple_of(block, 16)
            out.append(
                pltpu.make_async_copy(
                    ref.at[k], target.at[half, pl.ds(block, rows), :], sem.at[slot, k]
                )
            )
        return out

    waits = []
    if not by_core:
        for slot, ref in enumerate(pieces):
            waits += copies(ref, slot // 4, slot % 2, slot % 4 // 2, slot)
        return started(waits)

    z0, a0, b0, c0, z1, a1, b1, c1 = pieces
    first = core == 0
    for slot, (ref, half, dy, dcore) in enumerate(
        ((z0, 0, 0, 0), (c0, 1, 1, 0), (z1, 0, 0, 1), (c1, 1, 1, 1))
    ):
        waits += copies(ref, half, dy, dcore, slot)
    started(waits)
    for slot, (ref_if, ref_else, half, dy, dcore) in enumerate(
        ((b0, a0, 0, 1, 0), (a0, b0, 1, 0, 0), (a1, b1, 0, 1, 1), (b1, a1, 1, 0, 1)), 4
    ):
        @pl.when(first)
        def _(ref=ref_if, half=half, dy=dy, dcore=dcore, slot=slot):
            started(copies(ref, half, dy, dcore, slot))

        @pl.when(jnp.logical_not(first))
        def _(ref=ref_else, half=half, dy=dy, dcore=dcore, slot=slot):
            started(copies(ref, half, dy, dcore, slot))

        waits += copies(ref_if, half, dy, dcore, slot)
    return waits


def device_of(rows, half, d_model):
    row = lax.broadcasted_iota(jnp.int32, (d_model, 1), 0)
    device = lax.div(row, jnp.int32(rows))
    return device, row - device * rows


def one_hot(target, cols):
    lane = lax.broadcasted_iota(jnp.int32, (target.shape[0], cols), 1)
    return jnp.where(lane == target, 1.0, 0.0).astype(BF)


def qv_places(rows, d_model):
    device, at = device_of(rows, rows // 2, d_model)
    value = (at >= rows // 2).astype(jnp.int32)
    target = value * (d_model // 2) + device * (rows // 2) + at - value * (rows // 2)
    return one_hot(target, d_model)


def up_places(rows, d_model, part, ff):
    device, at = device_of(rows, rows, d_model)
    return one_hot(device * (2 * rows) + part * rows + at, ff)


def project_kernel(rows, n_qkv, where, tok_ref, *refs):
    pieces = refs[:n_qkv]
    proj_ref, vec_ref, up_ref, weights, bias, sem = refs[n_qkv:]
    d_model = tok_ref.shape[1]
    span = proj_ref.shape[1]

    @pl.when(pl.program_id(0) == 0)
    def _():
        for copy in piece_copies(where, pieces, weights, sem):
            copy.wait()
        bias[...] = jnp.zeros_like(bias)
        qv = qv_places(rows, d_model)
        up = [up_places(rows, d_model, part, up_ref.shape[1]) for part in range(2)]
        turned = weights[0, :, span:].T[:16]
        vec_ref[...] = turned[:8].astype(F32)
        row = mm(turned, qv, NN)[8:9]
        for pair in range(span // (3 * PAIR)):
            at = pair * 3 * PAIR
            bias[0:1, at : at + PAIR] = row[:, pair * PAIR : (pair + 1) * PAIR]
            first = d_model // 2 + pair * PAIR
            bias[0:1, at + 2 * PAIR : at + 3 * PAIR] = row[:, first : first + PAIR]
        up_ref[...] = mm(turned, up[0], NN)[6:7] + mm(turned, up[1], NN)[7:8]

    tokens = tok_ref[...]
    for at in range(0, span, 384):
        proj_ref[:, at : at + 384] = (
            mm(tokens, weights[0, :, at : at + 384], NN) + bias[0:1, at : at + 384]
        ).astype(BF)


def project(where, tokens, pieces, rows, seq, span, ff, tile=512):
    d_model = tokens.shape[1]
    return pl.pallas_call(
        functools.partial(project_kernel, rows, len(pieces)),
        out_shape=(
            jax.ShapeDtypeStruct((seq, span), BF),
            jax.ShapeDtypeStruct((8, d_model), F32),
            jax.ShapeDtypeStruct((1, ff), F32),
        ),
        grid_spec=pltpu.PrefetchScalarGridSpec(
            num_scalar_prefetch=1,
            grid=(seq // tile,),
            in_specs=[own_tile(tile, d_model, seq)] + [ANYWHERE] * len(pieces),
            out_specs=[
                row_tile(tile, span),
                pl.BlockSpec((8, d_model), lambda i, w: (0, 0)),
                pl.BlockSpec((1, ff), lambda i, w: (0, 0)),
            ],
            scratch_shapes=[
                pltpu.VMEM((1, d_model, span + SMALL), BF),
                pltpu.VMEM((8, span), F32),
                pltpu.SemaphoreType.DMA((8, 4)),
            ],
        ),
        cost_estimate=cost(8.7),
        name="project",
    )(where, tokens, *pieces)


def last_kernel(n_qkv, where, own_ref, other_ref, one_ref, *refs):
    pieces = refs[:n_qkv]
    whole_ref, low_ref, weights, sem = refs[n_qkv:]
    span = own_ref.shape[1]

    @pl.when(pl.program_id(0) == 0)
    def _():
        for copy in piece_copies(where, pieces, weights, sem):
            copy.wait()

    total = (
        mm(own_ref[...], weights[0, :, :span], NT)
        + mm(other_ref[...], weights[1, :, :span], NT)
        + one_ref[...]
    )
    whole_ref[...] = total
    low_ref[...] = total.astype(BF)


def last_part(where, d_proj, d_one, pieces, tile=512):
    seq, span = d_proj[0].shape
    d_model = d_one.shape[1]
    return pl.pallas_call(
        functools.partial(last_kernel, len(pieces)),
        out_shape=(
            jax.ShapeDtypeStruct((2 * seq, d_model), F32),
            jax.ShapeDtypeStruct((seq, d_model), BF),
        ),
        grid_spec=pltpu.PrefetchScalarGridSpec(
            num_scalar_prefetch=1,
            grid=(seq // tile,),
            in_specs=[row_tile(tile, span), row_tile(tile, span), row_tile(tile, d_model)]
            + [ANYWHERE] * len(pieces),
            out_specs=[own_tile(tile, d_model, seq), row_tile(tile, d_model)],
            scratch_shapes=[
                pltpu.VMEM((2, d_model, span + SMALL), BF),
                pltpu.SemaphoreType.DMA((8, 4)),
            ],
        ),
        cost_estimate=cost(12.0),
        name="last_part",
    )(where, *d_proj, d_one, *pieces)


def part_copies(where, result, half, keep_ref, send_ref, sem, staged):
    if not staged:
        return [pltpu.make_async_copy(result.at[half], keep_ref.at[half], sem.at[half, 0])]
    if len(keep_ref.shape) == 4:
        rows = keep_ref.shape[2]
        return [
            pltpu.make_async_copy(
                result.at[half, pl.ds(d * rows, rows), :],
                keep_ref.at[d, where[3] ^ half],
                sem.at[half, d],
            )
            for d in range(keep_ref.shape[0])
        ]
    rows = keep_ref.shape[-2]
    z, y, core = where[0], where[1], where[2]
    out = []
    for dcore, target in enumerate((keep_ref, send_ref)):
        for dy in range(2):
            for k in range(4):
                block = ((lax.rem(z + k, 4) * 2 + (y ^ dy)) * 2 + (core ^ dcore)) * rows
                block = pl.multiple_of(block, 16)
                if target.shape[2] == 1:
                    place = target.at[dy, k, 0]
                else:
                    by_y = (core ^ dcore) == 0
                    place = target.at[jnp.where(by_y, dy, half), jnp.where(by_y, half, dy), k]
                out.append(
                    pltpu.make_async_copy(
                        result.at[half, pl.ds(block, rows), :], place, sem.at[half, len(out)]
                    )
                )
    return out


def part_shapes(staged, halves, d_model, cols):
    if not staged:
        whole = jax.ShapeDtypeStruct((halves, d_model, cols), BF)
        return whole, jax.ShapeDtypeStruct((8, 128), BF)
    rows = d_model // 16
    dims = (2, 4, 1, rows, cols) if halves == 1 else (2, 2, 4, rows, cols)
    return (jax.ShapeDtypeStruct(dims, BF),) * 2


def after(value, *others):
    return lax.optimization_barrier((value, *others))[0]


def grads_kernel(staged, rows, halves, widths, n_extra, where, *refs):
    count = len(widths)
    lhs_refs, refs = refs[:count], refs[count:]
    rhs_refs, refs = refs[: count * halves], refs[count * halves :]
    extra_refs, refs = refs[:n_extra], refs[n_extra:]
    keep_ref, send_ref, result, turned, sem = refs
    d_model = result.shape[1]
    for lhs, out in zip(lhs_refs, range(count)):
        for at in range(0, lhs.shape[0], BLOCK):
            turned[out, :, at : at + BLOCK] = lhs[at : at + BLOCK, :].T
    for half in range(halves):
        first = 0
        for n in range(count):
            rhs = rhs_refs[n * halves + half]
            rhs = rhs.at[half] if len(rhs.shape) == 3 else rhs
            width = rhs.shape[1]
            for at in range(0, width, 384):
                result[half, :, first + at : first + at + 384] = mm(
                    turned[n], rhs[:, at : at + 384], NN
                ).astype(BF)
            first += width
        if n_extra == 1:
            (sums,) = extra_refs
            blank = jnp.zeros((SMALL - 1, PAIR), F32)
            parts = [
                sums[pair, 0:1, n * PAIR : (n + 1) * PAIR]
                for n in (0, 2)
                for pair in range(sums.shape[0])
            ]
            line = jnp.concatenate(parts, axis=1)
            lines = jnp.concatenate([line, jnp.zeros((SMALL - 1, line.shape[1]), F32)], axis=0)
            extra = mm(qv_places(rows, d_model), lines.astype(BF), NT)
        else:
            two, one, up = extra_refs
            own = one_hot(lax.broadcasted_iota(jnp.int32, (d_model, 1), 0), d_model)
            zero = jnp.zeros((SMALL - 6, d_model), F32)
            lines = jnp.concatenate([one[2:3], one[0:2], two[2:3], two[0:2], zero], axis=0)
            extra = mm(own, lines.astype(BF), NT)
            blank = jnp.zeros((SMALL - 8, up.shape[2]), F32)
            for part in range(2):
                line = up[half, 0:1]
                before = jnp.zeros((6 + part, line.shape[1]), F32)
                behind = jnp.zeros((SMALL - 7 - part, line.shape[1]), F32)
                lines = jnp.concatenate([before, line, behind], axis=0)
                extra = extra + mm(
                    up_places(rows, d_model, part, line.shape[1]), lines.astype(BF), NT
                )
        result[half, :, first:] = extra.astype(BF)
        for copy in part_copies(where, result, half, keep_ref, send_ref, sem, staged):
            copy.start()
    for half in range(halves):
        for copy in part_copies(where, result, half, keep_ref, send_ref, sem, staged):
            copy.wait()


def whole_spec(array):
    return pl.BlockSpec(array.shape, lambda i, w, n=array.ndim: (0,) * n)


def own_tile(tile, width, seq):
    return pl.BlockSpec((tile, width), lambda i, w: (w[3] * (seq // tile) + i, 0))


def grads(where, staged, rows, lhs, rhs, extra):
    halves = len(rhs[0])
    seq = rhs[0][0].shape[-2]
    d_model = lhs[0].shape[1]
    widths = [r[0].shape[-1] for r in rhs]
    cols = sum(widths) + SMALL
    operands = [*(r for pair in rhs for r in pair), *extra]
    return pl.pallas_call(
        functools.partial(grads_kernel, staged, rows, halves, widths, len(extra)),
        out_shape=part_shapes(staged, halves, d_model, cols),
        grid_spec=pltpu.PrefetchScalarGridSpec(
            num_scalar_prefetch=1,
            grid=(1,),
            in_specs=[
                own_tile(seq, d_model, seq) if l.shape[0] > seq else whole_spec(l) for l in lhs
            ]
            + [whole_spec(o) for o in operands],
            out_specs=[ANYWHERE] * 2,
            scratch_shapes=[
                pltpu.VMEM((halves, d_model, cols), BF),
                pltpu.VMEM((len(lhs), d_model, seq), BF),
                pltpu.SemaphoreType.DMA((halves, 16)),
            ],
        ),
        cost_estimate=cost(20.0 if halves == 2 else 7.2),
        name="grads",
    )(where, *lhs, *operands)


def row_norm(values):
    centered = values - jnp.mean(values, axis=-1, keepdims=True)
    inverse = lax.rsqrt(jnp.mean(centered * centered, axis=-1, keepdims=True) + NORM_EPS)
    return centered * inverse, inverse


def row_norm_back(d_normed, z, inverse, gain):
    dz = d_normed * gain
    return (
        dz - jnp.mean(dz, axis=-1, keepdims=True) - z * jnp.mean(dz * z, axis=-1, keepdims=True)
    ) * inverse


def column_sum(values):
    return jnp.sum(values, axis=0, keepdims=True)


def first_kernel(n_up, where, tok_ref, ctx0_ref, ctx1_ref, vec_ref, bias0_ref, bias1_ref, *refs):
    pieces = refs[:n_up]
    z_ref, inv_ref, hid_ref, slope_ref, weights, sem = refs[n_up:]
    bias_refs = bias0_ref, bias1_ref
    width = ctx0_ref.shape[1]

    @pl.when(pl.program_id(0) == 0)
    def _():
        for copy in piece_copies(where, pieces, weights, sem, True):
            copy.wait()

    resid = (
        tok_ref[...].astype(F32)
        + mm(ctx0_ref[...], weights[0, :, :width], NT)
        + mm(ctx1_ref[...], weights[1, :, :width], NT)
        + vec_ref[0:1]
    )
    z, inverse = row_norm(resid)
    z_ref[...] = z
    inv_ref[...] = jnp.broadcast_to(inverse, inv_ref.shape)
    low = (z * vec_ref[1:2] + vec_ref[2:3]).astype(BF)
    ff = hid_ref.shape[2]
    for half in range(2):
        for at in range(0, ff, 512):
            pre = mm(low, weights[half, :, width + at : width + at + 512], NN)
            gelu, slope = gelu_both(pre + bias_refs[half][:, at : at + 512])
            hid_ref[half, :, at : at + 512] = gelu.astype(BF)
            slope_ref[half, :, at : at + 512] = slope.astype(BF)


def row_tile(tile, width):
    return pl.BlockSpec((tile, width), lambda i, w: (i, 0))


def halves_tile(tile, width):
    return pl.BlockSpec((2, tile, width), lambda i, w: (0, i, 0))


ANYWHERE = pl.BlockSpec(memory_space=pl.ANY)


def first_part(where, tokens, ctx, vectors, bias, pieces, tile=256):
    d_model = tokens.shape[1]
    seq = ctx[0].shape[0]
    width, ff = ctx[0].shape[1], bias[0].shape[1]
    return pl.pallas_call(
        functools.partial(first_kernel, len(pieces)),
        out_shape=(
            jax.ShapeDtypeStruct((seq, d_model), F32),
            jax.ShapeDtypeStruct((seq, 128), F32),
            jax.ShapeDtypeStruct((2, seq, ff), BF),
            jax.ShapeDtypeStruct((2, seq, ff), BF),
        ),
        grid_spec=pltpu.PrefetchScalarGridSpec(
            num_scalar_prefetch=1,
            grid=(seq // tile,),
            in_specs=[
                own_tile(tile, d_model, seq),
                row_tile(tile, width),
                row_tile(tile, width),
                whole_spec(vectors),
                whole_spec(bias[0]),
                whole_spec(bias[1]),
            ]
            + [ANYWHERE] * len(pieces),
            out_specs=[
                row_tile(tile, d_model),
                row_tile(tile, 128),
                halves_tile(tile, ff),
                halves_tile(tile, ff),
            ],
            scratch_shapes=[
                pltpu.VMEM((2, d_model, width + ff), BF),
                pltpu.SemaphoreType.DMA((8, 4)),
            ],
        ),
        cost_estimate=cost(19.4),
        name="first_part",
    )(where, tokens, *ctx, vectors, *bias, *pieces)


def second_kernel(staged, n_down, where, hid_ref, z_ref, cot_ref, vec_ref, *refs):
    pieces = refs[:n_down]
    out_ref, own_ref, d_ref, sum_ref, keep_ref, *refs = refs[n_down:]
    weights, turned, kept, result, sem, out_sem = refs
    step = pl.program_id(0)
    tile, ff = hid_ref.shape[1:]

    @pl.when(step == 0)
    def _():
        for copy in piece_copies(where, pieces, weights, sem):
            copy.wait()
        sum_ref[...] = jnp.zeros_like(sum_ref)

    ffn = mm(hid_ref[0], weights[0], NT) + mm(hid_ref[1], weights[1], NT)
    resid = z_ref[...] * vec_ref[1:2] + vec_ref[2:3] + ffn + vec_ref[3:4]
    z, inverse = row_norm(resid)
    out = (z * vec_ref[4:5] + vec_ref[5:6]).astype(BF)
    out_ref[...] = out
    own_ref[...] = out
    cot = cot_ref[...].astype(F32)
    d_two = row_norm_back(cot, z, inverse, vec_ref[4:5])
    d_ref[...] = d_two
    sum_ref[0:1] += column_sum(cot * z)
    sum_ref[1:2] += column_sum(cot)
    sum_ref[2:3] += column_sum(d_two)
    rows = pl.ds(pl.multiple_of(step * tile, tile), tile)
    turned[:, rows] = d_two.astype(BF).T
    kept[:, rows, :] = hid_ref[...]

    @pl.when(step == pl.num_programs(0) - 1)
    def _():
        for half in range(2):
            for at in range(0, ff, 512):
                result[half, :, at : at + 512] = mm(
                    turned[...], kept[half, :, at : at + 512], NN
                ).astype(BF)
            for copy in part_copies(where, result, half, keep_ref, None, out_sem, staged):
                copy.start()
        for half in range(2):
            for copy in part_copies(where, result, half, keep_ref, None, out_sem, staged):
                copy.wait()


def second_part(where, staged, hidden, z_one, cot, vectors, pieces, tile=256):
    _, seq, ff = hidden.shape
    d_model = z_one.shape[1]
    return pl.pallas_call(
        functools.partial(second_kernel, staged, len(pieces)),
        out_shape=(
            jax.ShapeDtypeStruct((2 * seq, d_model), BF),
            jax.ShapeDtypeStruct((seq, d_model), BF),
            jax.ShapeDtypeStruct((seq, d_model), F32),
            jax.ShapeDtypeStruct((8, d_model), F32),
            (
                jax.ShapeDtypeStruct((16, 2, d_model // 16, ff), BF)
                if staged
                else jax.ShapeDtypeStruct((2, d_model, ff), BF)
            ),
        ),
        grid_spec=pltpu.PrefetchScalarGridSpec(
            num_scalar_prefetch=1,
            grid=(seq // tile,),
            in_specs=[
                halves_tile(tile, ff),
                row_tile(tile, d_model),
                own_tile(tile, d_model, seq),
                whole_spec(vectors),
            ]
            + [ANYWHERE] * len(pieces),
            out_specs=[
                own_tile(tile, d_model, seq),
                row_tile(tile, d_model),
                row_tile(tile, d_model),
                pl.BlockSpec((8, d_model), lambda i, w: (0, 0)),
                ANYWHERE,
            ],
            scratch_shapes=[
                pltpu.VMEM((2, d_model, ff), BF),
                pltpu.VMEM((d_model, seq), BF),
                pltpu.VMEM((2, seq, ff), BF),
                pltpu.VMEM((2, d_model, ff), BF),
                pltpu.SemaphoreType.DMA((8, 4)),
                pltpu.SemaphoreType.DMA((2, 16)),
            ],
        ),
        cost_estimate=cost(21.8),
        name="second_part",
    )(where, hidden, z_one, cot, vectors, *pieces)


def third_kernel(n_up, n_down, where, d_ref, slope_ref, z_ref, inv_ref, vec_ref, *refs):
    up_pieces, down_pieces, refs = refs[:n_up], refs[n_up : n_up + n_down], refs[n_up + n_down :]
    pre_ref, low_ref, one_ref, one_low_ref, ctx_ref, sum_ref, bias_ref, *refs = refs
    up, down, sem, down_sem = refs
    step = pl.program_id(0)
    ff = slope_ref.shape[2]
    width = ctx_ref.shape[2]

    @pl.when(step == 0)
    def _():
        waits = piece_copies(where, down_pieces, down, down_sem)
        waits += piece_copies(where, up_pieces, up, sem, True)
        for copy in waits:
            copy.wait()
        sum_ref[...] = jnp.zeros_like(sum_ref)
        bias_ref[...] = jnp.zeros_like(bias_ref)

    d_two = d_ref[...]
    d_two_low = d_two.astype(BF)
    d_normed = d_two
    for half in range(2):
        for at in range(0, ff, 512):
            span = slice(at, at + 512)
            d_pre = mm(d_two_low, down[half, :, span], NN) * slope_ref[half, :, span].astype(F32)
            d_pre = d_pre.astype(BF)
            pre_ref[half, :, span] = d_pre
            bias_ref[half, 0:1, span] += column_sum(d_pre.astype(F32))
            d_normed = d_normed + mm(d_pre, up[half, :, width + at : width + at + 512], NT)
    z = z_ref[...]
    low_ref[...] = (z * vec_ref[1:2] + vec_ref[2:3]).astype(BF)
    d_one = row_norm_back(d_normed, z, inv_ref[:, 0:1], vec_ref[1:2])
    one_ref[...] = d_one
    sum_ref[0:1] += column_sum(d_normed * z)
    sum_ref[1:2] += column_sum(d_normed)
    sum_ref[2:3] += column_sum(d_one)
    d_one_low = d_one.astype(BF)
    one_low_ref[...] = d_one_low
    for half in range(2):
        ctx_ref[half] = mm(d_one_low, up[half, :, :width], NN).astype(BF)


def third_part(where, d_two, slope, z_one, inv_one, vectors, up_pieces, down_pieces, width, tile=256):
    seq, d_model = d_two.shape
    ff = slope.shape[2]
    return pl.pallas_call(
        functools.partial(third_kernel, len(up_pieces), len(down_pieces)),
        out_shape=(
            jax.ShapeDtypeStruct((2, seq, ff), BF),
            jax.ShapeDtypeStruct((seq, d_model), BF),
            jax.ShapeDtypeStruct((seq, d_model), F32),
            jax.ShapeDtypeStruct((seq, d_model), BF),
            jax.ShapeDtypeStruct((2, seq, width), BF),
            jax.ShapeDtypeStruct((8, d_model), F32),
            jax.ShapeDtypeStruct((2, 8, ff), F32),
        ),
        grid_spec=pltpu.PrefetchScalarGridSpec(
            num_scalar_prefetch=1,
            grid=(seq // tile,),
            in_specs=[
                row_tile(tile, d_model),
                halves_tile(tile, ff),
                row_tile(tile, d_model),
                row_tile(tile, 128),
                whole_spec(vectors),
            ]
            + [ANYWHERE] * (len(up_pieces) + len(down_pieces)),
            out_specs=[
                halves_tile(tile, ff),
                row_tile(tile, d_model),
                row_tile(tile, d_model),
                row_tile(tile, d_model),
                halves_tile(tile, width),
                pl.BlockSpec((8, d_model), lambda i, w: (0, 0)),
                pl.BlockSpec((2, 8, ff), lambda i, w: (0, 0, 0)),
            ],
            scratch_shapes=[
                pltpu.VMEM((2, d_model, width + ff), BF),
                pltpu.VMEM((2, d_model, ff), BF),
                pltpu.SemaphoreType.DMA((8, 4)),
                pltpu.SemaphoreType.DMA((8, 4)),
            ],
        ),
        cost_estimate=cost(25.6),
        name="third_part",
    )(where, d_two, slope, z_one, inv_one, vectors, *up_pieces, *down_pieces)


def add(first, second):
    return (first.astype(F32) + second.astype(F32)).astype(BF)


def core_stage(keep, send):
    return move(send, MOVE_CORE), keep


def flip_stage(moves, got, keep):
    return move(add(keep[1], got[1]), moves), add(keep[0], got[0])


def z_stage(*terms):
    sums = [functools.reduce(jnp.add, [t[k].astype(F32) for t in terms]) for k in range(4)]
    parts = [move(part.astype(BF), moves) for part, moves in zip(sums[1:], MOVE_Z)]
    return parts, sums[0]


def z_sum(parts, keep):
    return keep + parts[0].astype(F32) + parts[1].astype(F32) + parts[2].astype(F32)


def lane_mask(head, rows):
    lanes = lax.broadcasted_iota(jnp.int32, (rows, PAIR), 1)
    return (lanes < HD) if head == 0 else (lanes >= HD)


def attn_fwd_kernel(table, qkv_ref, ctx_ref, prob_ref):
    pair = pl.program_id(0)
    q_ref, k_ref, v_ref = (qkv_ref.at[:, n * PAIR : (n + 1) * PAIR] for n in range(3))
    lanes = lax.broadcasted_iota(jnp.int32, (1, HALF), 1)
    for half in range(2):
        rows = pl.ds(half * HALF, HALF)
        query = q_ref[rows, :] * jnp.asarray(HD**-0.5, BF)
        parts = []
        for head in range(2):
            at = (pair * 2 + head) * 4
            start = (half ^ table[at]) * HALF
            flags = [table[at + 1 + n] == 1 for n in range(3)]
            key_lo = k_ref[pl.ds(pl.multiple_of(start, BLOCK), BLOCK), :]
            key_hi = k_ref[pl.ds(pl.multiple_of(start + BLOCK, BLOCK), BLOCK), :]
            masked = jnp.where(lane_mask(head, HALF), query, jnp.zeros_like(query))
            score_lo = mm(key_lo, masked, NT)
            score_hi = mm(key_hi, masked[BLOCK:], NT)
            no_lo = jnp.where(
                lanes < BLOCK,
                jnp.where(flags[0], 0.0, -1e30),
                jnp.where(flags[1], 0.0, -1e30),
            ).astype(F32)
            no_hi = jnp.where(flags[2], 0.0, -1e30).astype(F32)
            top_lo = jnp.max(score_lo, axis=0, keepdims=True) + no_lo
            top_hi = jnp.max(score_hi, axis=0, keepdims=True) + no_hi
            top = jnp.concatenate(
                [top_lo[:, :BLOCK], jnp.maximum(top_lo[:, BLOCK:], top_hi)], axis=1
            )
            ref_lo = jnp.where(no_lo < 0.0, 1e30, top)
            ref_hi = jnp.where(no_hi < 0.0, 1e30, top[:, BLOCK:])
            exp_lo = jnp.exp(score_lo - ref_lo)
            exp_hi = jnp.exp(score_hi - ref_hi)
            sum_lo = jnp.sum(exp_lo, axis=0, keepdims=True)
            sum_hi = jnp.sum(exp_hi, axis=0, keepdims=True)
            total = jnp.concatenate([sum_lo[:, :BLOCK], sum_lo[:, BLOCK:] + sum_hi], axis=1)
            scale = jnp.where(total > 0.0, 1.0 / jnp.where(total > 0.0, total, 1.0), 0.0)
            prob_lo = (exp_lo * scale).astype(BF)
            prob_hi = (exp_hi * scale[:, BLOCK:]).astype(BF)
            prob_ref[0, head, half, :, :HALF] = prob_lo
            prob_ref[0, head, half, :, HALF:] = prob_hi
            val_lo = v_ref[pl.ds(pl.multiple_of(start, BLOCK), BLOCK), :].T
            val_hi = v_ref[pl.ds(pl.multiple_of(start + BLOCK, BLOCK), BLOCK), :].T
            side = slice(head * HD, (head + 1) * HD)
            out_lo = mm(val_lo[side], prob_lo, NN)
            out_hi = mm(val_hi[side], prob_hi, NN)
            parts.append(
                jnp.concatenate([out_lo[:, :BLOCK], out_lo[:, BLOCK:] + out_hi], axis=1)
            )
        ctx_ref[rows, :] = jnp.concatenate(parts, axis=0).T.astype(BF)


def attn_fwd(table, proj):
    seq, width = proj.shape
    pairs = width // 3 // PAIR
    return pl.pallas_call(
        attn_fwd_kernel,
        out_shape=(
            jax.ShapeDtypeStruct((seq, width // 3), BF),
            jax.ShapeDtypeStruct((pairs, 2, 2, BLOCK, HALF + BLOCK), BF),
        ),
        grid_spec=pltpu.PrefetchScalarGridSpec(
            num_scalar_prefetch=1,
            grid=(pairs,),
            in_specs=[pl.BlockSpec((seq, 3 * PAIR), lambda p, t: (0, p))],
            out_specs=[
                pl.BlockSpec((seq, PAIR), lambda p, t: (0, p)),
                pl.BlockSpec((1, 2, 2, BLOCK, HALF + BLOCK), lambda p, t: (p, 0, 0, 0, 0)),
            ],
        ),
        cost_estimate=cost(0.5),
        name="attn_fwd",
    )(table, proj)


def attn_bwd_kernel(table, qkv_ref, d_ref, prob_ref, out_ref, sum_ref, k_acc, v_acc):
    pair = pl.program_id(0)
    q_ref, k_ref, v_ref = (qkv_ref.at[:, n * PAIR : (n + 1) * PAIR] for n in range(3))
    for half in range(2):
        rows = pl.ds(half * HALF, HALF)
        query = q_ref[rows, :] * jnp.asarray(HD**-0.5, BF)
        d_ctx = d_ref[rows, :]
        parts = []
        for head in range(2):
            at = (pair * 2 + head) * 4
            start = (half ^ table[at]) * HALF
            at_lo = pl.ds(pl.multiple_of(start, BLOCK), BLOCK)
            at_hi = pl.ds(pl.multiple_of(start + BLOCK, BLOCK), BLOCK)
            keep = lane_mask(head, HALF)
            query_h = jnp.where(keep, query, jnp.zeros_like(query))
            d_ctx_h = jnp.where(keep, d_ctx, jnp.zeros_like(d_ctx))
            prob_lo = prob_ref[0, head, half, :, :HALF]
            prob_hi = prob_ref[0, head, half, :, HALF:]
            d_w_lo = mm(v_ref[at_lo, :], d_ctx_h, NT)
            d_w_hi = mm(v_ref[at_hi, :], d_ctx_h[BLOCK:], NT)
            wide_lo = prob_lo.astype(F32)
            wide_hi = prob_hi.astype(F32)
            dot_lo = jnp.sum(wide_lo * d_w_lo, axis=0, keepdims=True)
            dot_hi = jnp.sum(wide_hi * d_w_hi, axis=0, keepdims=True)
            dot = jnp.concatenate([dot_lo[:, :BLOCK], dot_lo[:, BLOCK:] + dot_hi], axis=1)
            d_s_lo = (wide_lo * (d_w_lo - dot)).astype(BF)
            d_s_hi = (wide_hi * (d_w_hi - dot[:, BLOCK:])).astype(BF)
            dk_lo = mm(d_s_lo, query_h, NN)
            dk_hi = mm(d_s_hi, query_h[BLOCK:], NN)
            dv_lo = mm(prob_lo, d_ctx_h, NN)
            dv_hi = mm(prob_hi, d_ctx_h[BLOCK:], NN)
            k_acc[head, at_lo, :] = dk_lo
            k_acc[head, at_hi, :] = dk_hi
            v_acc[head, at_lo, :] = dv_lo
            v_acc[head, at_hi, :] = dv_hi
            key_lo = k_ref[at_lo, :].T
            key_hi = k_ref[at_hi, :].T
            side = slice(head * HD, (head + 1) * HD)
            dq_lo = mm(key_lo[side], d_s_lo, NN)
            dq_hi = mm(key_hi[side], d_s_hi, NN)
            parts.append(jnp.concatenate([dq_lo[:, :BLOCK], dq_lo[:, BLOCK:] + dq_hi], axis=1))
        out_ref[rows, :PAIR] = (jnp.concatenate(parts, axis=0).T * HD**-0.5).astype(BF)
    out_ref[:, PAIR : 2 * PAIR] = (k_acc[0] + k_acc[1]).astype(BF)
    out_ref[:, 2 * PAIR :] = (v_acc[0] + v_acc[1]).astype(BF)
    sums = jnp.sum(out_ref[...].astype(F32), axis=0, keepdims=True)
    sum_ref[0] = jnp.broadcast_to(sums, sum_ref.shape[1:])


def attn_bwd(table, proj, d_context, half, probs):
    seq, width = proj.shape
    pairs = width // 3 // PAIR
    return pl.pallas_call(
        attn_bwd_kernel,
        out_shape=(
            jax.ShapeDtypeStruct((seq, width), BF),
            jax.ShapeDtypeStruct((pairs, 8, 3 * PAIR), F32),
        ),
        grid_spec=pltpu.PrefetchScalarGridSpec(
            num_scalar_prefetch=1,
            grid=(pairs,),
            in_specs=[
                pl.BlockSpec((seq, 3 * PAIR), lambda p, t: (0, p)),
                pl.BlockSpec((None, seq, PAIR), lambda p, t: (half, 0, p)),
                pl.BlockSpec((1, 2, 2, BLOCK, HALF + BLOCK), lambda p, t: (p, 0, 0, 0, 0)),
            ],
            out_specs=[
                pl.BlockSpec((seq, 3 * PAIR), lambda p, t: (0, p)),
                pl.BlockSpec((1, 8, 3 * PAIR), lambda p, t: (p, 0, 0)),
            ],
            scratch_shapes=[pltpu.VMEM((2, seq, PAIR), F32)] * 2,
        ),
        cost_estimate=cost(11.3),
        name="attn_bwd",
    )(table, proj, d_context, probs)


def gelu_both(values):
    half = 0.5 * (1.0 + lax.erf(values * (0.5**0.5)))
    slope = half + values * jnp.exp(-0.5 * values * values) * 0.3989422804014327
    return values * half, slope


def body(
    dp_size,
    tokens,
    grad_out,
    head_perm,
    block_mask,
    w_qkv,
    b_qv,
    w_out,
    b_out,
    gain_one,
    shift_one,
    w_up,
    b_up,
    w_down,
    b_down,
    gain_two,
    shift_two,
):
    seq = tokens.shape[0] // head_perm.shape[0]
    rows = w_qkv.shape[0]
    width = w_qkv.shape[2]
    d_model = tokens.shape[1]
    dp_at = lax.axis_index("dp")
    mp_at = lax.axis_index("mp")
    where = jnp.stack([dp_at // 4, (dp_at // 2) % 2, dp_at % 2, mp_at]).astype(jnp.int32)

    table = jnp.concatenate([head_perm[:, :, None], block_mask], axis=2).astype(jnp.int32)
    table = table.reshape(2, -1)
    table_own = lax.dynamic_index_in_dim(table, mp_at, 0, keepdims=False)
    table_other = swap_mp(lax.dynamic_index_in_dim(table, 1 - mp_at, 0, keepdims=False))

    small = jnp.stack(
        [
            b_out,
            gain_one,
            shift_one,
            b_down,
            gain_two,
            shift_two,
            b_up[:rows],
            b_up[rows:],
            b_qv.reshape(-1),
        ],
        axis=1,
    )
    small = jnp.pad(small, ((0, 0), (0, SMALL - small.shape[1])))
    pairs = width // PAIR
    by_pair = w_qkv.reshape(rows, 3, pairs, PAIR).transpose(0, 2, 1, 3).reshape(rows, 3 * width)
    shard_qkv = jnp.concatenate([by_pair, small], axis=1)
    shard_up = jnp.concatenate([w_out.T, w_up], axis=1)
    shard_down = w_down.T
    staged = dp_size == 16

    def plain_gather(shard):
        full = lax.all_gather(shard, "dp", axis=0, tiled=True)
        return full, swap_mp(full)

    def gather_z(shard):
        return jnp.stack([shard] + [move(shard, moves) for moves in MOVE_Z])

    def gather_core(*pieces):
        return (*pieces, *(move(piece, MOVE_CORE) for piece in pieces))

    if staged:
        qkv_z = gather_z(shard_qkv)
        qkv_y = move(qkv_z, MOVE_Y)
        qkv_x = move(qkv_z, MOVE_X)
        up_parts = [move(after(shard_up, qkv_z), moves) for moves in MOVE_Z]
        down_whole = lax.all_gather(after(shard_down, qkv_z), AXES)
        down_pieces = (down_whole.reshape(dp_size, 2, *shard_down.shape),)
        qkv_y, *up_parts = lax.optimization_barrier((qkv_y, *up_parts))
        qkv_own = gather_core(qkv_z, qkv_y)
        qkv_xy = move(qkv_y, MOVE_X)
        up_z = jnp.stack([shard_up, *up_parts])
        tokens_in, table_other, qkv_x, up_z = lax.optimization_barrier(
            (tokens, table_other, qkv_x, up_z)
        )
        up_a, up_b = move(up_z, MOVE_FIRST), move(up_z, MOVE_SECOND)
    else:
        qkv_own, qkv_other = ((piece,) for piece in plain_gather(shard_qkv))
        up_pieces = plain_gather(shard_up)
        down_pieces = plain_gather(shard_down)
        tokens_in = tokens

    ff = w_up.shape[1]

    def project_half(values, pieces):
        return project(where, values, pieces, rows, seq, 3 * width, ff)

    proj_own, vectors, bias_own = project_half(tokens_in, qkv_own)
    if staged:
        proj_own, qkv_xy = lax.optimization_barrier((proj_own, qkv_xy))
        qkv_other = gather_core(qkv_x, qkv_xy)
    ctx_own, probs_own = attn_fwd(table_own, proj_own)
    if staged:
        ctx_own, up_a = lax.optimization_barrier((ctx_own, up_a))
    proj_other, _, bias_other = project_half(after(tokens, ctx_own), qkv_other)
    if staged:
        proj_other, up_a = lax.optimization_barrier((proj_other, up_a))
        up_c = move(up_a, MOVE_SECOND)
        up_pieces = gather_core(up_z, up_a, up_b)
    ctx_other, probs_other = attn_fwd(table_other, proj_other)
    if staged:
        ctx_other, up_c = lax.optimization_barrier((ctx_other, up_c))
        up_pieces = (*up_pieces[:3], up_c, *up_pieces[3:], move(up_c, MOVE_CORE))
    tables, proj = (table_own, table_other), (proj_own, proj_other)
    probs = (probs_own, probs_other)
    ctx = (ctx_own, ctx_other)
    qkv_pieces = (*qkv_own, *qkv_other)
    z_one, inv_one, hidden, slope = first_part(
        where, tokens, ctx, vectors, (bias_own, bias_other), up_pieces
    )

    def place(whole, other):
        return lax.dynamic_update_slice_in_dim(
            whole, other.astype(whole.dtype), (1 - mp_at) * seq, 0
        )

    out_whole, out_own, d_two, sums_two, down_grad = second_part(
        where, staged, hidden, z_one, grad_out, vectors, down_pieces
    )
    out_other = swap_mp(out_own)

    def plain_scatter(own, other):
        summed = own.astype(F32) + swap_mp(other).astype(F32)
        return lax.psum_scatter(summed, "dp", scatter_dimension=0, tiled=True)

    if staged:
        down_grad = down_grad.reshape(2 * dp_size, *shard_down.shape)
        s_down = lax.psum_scatter(down_grad, AXES, scatter_dimension=0)
    else:
        s_down = plain_scatter(*down_grad)
    d_pre, normed_low, d_one, d_one_low, d_ctx, sums_one, sums_up = third_part(
        where, d_two, slope, z_one, inv_one, vectors, up_pieces, down_pieces, width
    )
    up_parts = grads(
        where,
        staged,
        rows,
        [normed_low, d_one_low],
        [(d_pre, d_pre), ctx],
        (sums_two, sums_one, sums_up),
    )
    d_ctx_other = d_ctx
    if staged:
        up_got, up_keep = core_stage(*up_parts)
        d_ctx_other, out_other, up_keep = lax.optimization_barrier((d_ctx, out_other, up_keep))
    else:
        s_up = plain_scatter(*up_parts[0])
    d_proj_other, sums_other = attn_bwd(tables[1], proj[1], d_ctx_other, 1, probs[1])
    if staged:
        d_proj_other, up_got = lax.optimization_barrier((d_proj_other, up_got))
        up_got, up_keep = flip_stage(MOVE_REDUCE[0], up_got, up_keep)
        d_proj_other, up_keep = lax.optimization_barrier((d_proj_other, up_keep))
    other_parts = grads(where, staged, rows, [tokens], [(d_proj_other,)], (sums_other,))
    d_ctx_own = d_ctx
    if staged:
        qo_got, qo_keep = core_stage(*other_parts)
        d_ctx_own, qo_keep = lax.optimization_barrier((d_ctx, qo_keep))
    d_proj_own, sums_own = attn_bwd(tables[0], proj[0], d_ctx_own, 0, probs[0])
    d_proj_last = d_proj_own
    if staged:
        d_proj_own, up_got, qo_got = lax.optimization_barrier((d_proj_own, up_got, qo_got))
        up_got, up_keep = flip_stage(MOVE_REDUCE[1], up_got, up_keep)
        qo_got, qo_keep = flip_stage(MOVE_Y, qo_got, qo_keep)
        d_proj_last, up_keep, qo_keep = lax.optimization_barrier((d_proj_own, up_keep, qo_keep))
    d_input, in_low = last_part(where, (d_proj_last, d_proj_other), d_one, qkv_pieces)
    tokens_in = tokens
    if staged:
        in_both = lax.all_gather(in_low, "mp")
        tokens_in, in_low, up_got, qo_got = lax.optimization_barrier(
            (tokens, in_low, up_got, qo_got)
        )
        qo_in = move(add(qo_keep, qo_got), MOVE_X)
        up_parts, up_keep = z_stage(up_got, up_keep)
        tokens_in, up_keep = lax.optimization_barrier((tokens_in, up_keep))
    else:
        in_other = swap_mp(in_low)
    own_parts = grads(where, staged, rows, [tokens_in], [(d_proj_own,)], (sums_own,))
    if staged:
        qs_got, qs_keep = core_stage(*own_parts)
        qs_keep, *up_parts = lax.optimization_barrier((qs_keep, *up_parts))
        qs_got, qs_keep = flip_stage(MOVE_Y, qs_got, qs_keep)
        out_other, qs_keep, s_down = lax.optimization_barrier((out_other, qs_keep, s_down))
        s_down = s_down.astype(F32)
        out_whole = place(out_whole, out_other)
        out_whole, qs_got = lax.optimization_barrier((out_whole, qs_got))
        s_up = z_sum(up_parts, up_keep)
        qs_parts, qs_keep = z_stage(qs_got, qs_keep, qo_in)
        in_both, qs_keep = lax.optimization_barrier((in_both, qs_keep))
        in_other = lax.dynamic_index_in_dim(in_both, 1 - mp_at, 0, keepdims=False)
        d_input = place(d_input, in_other)
        d_input, qs_keep = lax.optimization_barrier((d_input, qs_keep))
        s_qkv = z_sum(qs_parts, qs_keep)[0]
    else:
        out_whole = place(out_whole, out_other)
        d_input = place(d_input, in_other)
        s_qkv = plain_scatter(own_parts[0][0], other_parts[0][0])

    cols = s_up[:, ff + width :].T
    g_w_qkv = s_qkv[:, : 3 * width].reshape(rows, pairs, 3, PAIR).transpose(0, 2, 1, 3)
    return (
        out_whole,
        d_input,
        g_w_qkv.reshape(rows, 3, width),
        s_qkv[:, 3 * width].reshape(2, rows // 2),
        s_up[:, ff : ff + width].T,
        cols[0],
        cols[1],
        cols[2],
        s_up[:, :ff],
        cols[6:8].reshape(-1),
        s_down.T,
        cols[3],
        cols[4],
        cols[5],
    )


def solution(mesh):
    placed = (
        P("dp", None),
        P("dp", None),
        P("dp", "mp"),
        P("dp", "mp", None),
        P("dp", None, "mp"),
        P(None, ("mp", "dp")),
        P("mp", "dp"),
        P("dp"),
        P("dp"),
        P("dp"),
        P("dp", "mp"),
        P(("mp", "dp")),
        P("mp", "dp"),
        P("dp"),
        P("dp"),
        P("dp"),
    )
    return jax.shard_map(
        functools.partial(body, mesh.shape["dp"]),
        mesh=mesh,
        in_specs=placed,
        out_specs=(
            P("dp", None),
            P("dp", None),
            P("dp", None, "mp"),
            P(None, ("mp", "dp")),
            P("mp", "dp"),
            P("dp"),
            P("dp"),
            P("dp"),
            P("dp", "mp"),
            P(("mp", "dp")),
            P("mp", "dp"),
            P("dp"),
            P("dp"),
            P("dp"),
        ),
        check_vma=False,
    )
```

```python
import functools

import jax
import jax.numpy as jnp
from jax import lax
from jax.experimental import pallas as pl
from jax.experimental.pallas import tpu as pltpu
from jax.sharding import PartitionSpec as P

HD = 64
PAIR = 2 * HD
BLOCK = 256
HALF = 2 * BLOCK
NORM_EPS = 1e-05
BF = jnp.bfloat16
F32 = jnp.float32
AXES = ("dp", "mp")
NN = (((1,), (0,)), ((), ()))
NT = (((1,), (1,)), ((), ()))
TN = (((0,), (0,)), ((), ()))
SMALL = 128


def mm(first, second, dims):
    return lax.dot_general(first, second, dims, preferred_element_type=F32)


def cost(microseconds):
    return pl.CostEstimate(
        flops=int(microseconds * 4 * 1e9),
        transcendentals=0,
        bytes_accessed=int(microseconds * 4 * 3e6),
    )


def pairs_of(step):
    moves = []
    for d in range(16):
        for m in range(2):
            d2, m2 = step(d, m)
            moves.append((2 * d + m, 2 * d2 + m2))
    return moves


MOVE_X = pairs_of(lambda d, m: (d, 1 - m))
MOVE_Y = pairs_of(lambda d, m: (d ^ 2, m))
MOVE_CORE = pairs_of(lambda d, m: (d ^ 1, m))
MOVE_Z = [pairs_of(lambda d, m, k=k: ((d + 4 * k) % 16, m)) for k in (1, 2, 3)]
MOVE_FIRST = pairs_of(lambda d, m: (d ^ 2, m) if d & 1 else (d, 1 - m))
MOVE_SECOND = pairs_of(lambda d, m: (d, 1 - m) if d & 1 else (d ^ 2, m))


MOVE_REDUCE = MOVE_SECOND, MOVE_FIRST


def move(values, moves):
    return lax.ppermute(values, AXES, moves)


def swap_mp(values):
    return lax.ppermute(values, "mp", [(0, 1), (1, 0)])


def started(copies):
    for copy in copies:
        copy.start()
    return copies


def piece_copies(where, pieces, target, sem, by_core=False):
    if len(pieces[0].shape) == 4:
        (whole,) = pieces
        count, _, rows, _ = whole.shape
        return started(
            [
                pltpu.make_async_copy(
                    whole.at[d, where[3] ^ half],
                    target.at[half, pl.ds(d * rows, rows), :],
                    sem.at[(half * count + d) // 4, d % 4],
                )
                for half in range(2)
                for d in range(count)
            ]
        )
    if len(pieces[0].shape) == 2:
        return started(
            [pltpu.make_async_copy(p, target.at[n], sem.at[n, 0]) for n, p in enumerate(pieces)]
        )
    rows = pieces[0].shape[1]
    z, y, core = where[0], where[1], where[2]

    def copies(ref, half, dy, dcore, slot):
        out = []
        for k in range(4):
            block = ((lax.rem(z + 4 - k, 4) * 2 + (y ^ dy)) * 2 + (core ^ dcore)) * rows
            block = pl.multiple_of(block, 16)
            out.append(
                pltpu.make_async_copy(
                    ref.at[k], target.at[half, pl.ds(block, rows), :], sem.at[slot, k]
                )
            )
        return out

    waits = []
    if not by_core:
        for slot, ref in enumerate(pieces):
            waits += copies(ref, slot // 4, slot % 2, slot % 4 // 2, slot)
        return started(waits)

    z0, a0, b0, c0, z1, a1, b1, c1 = pieces
    first = core == 0
    for slot, (ref, half, dy, dcore) in enumerate(
        ((z0, 0, 0, 0), (c0, 1, 1, 0), (z1, 0, 0, 1), (c1, 1, 1, 1))
    ):
        waits += copies(ref, half, dy, dcore, slot)
    started(waits)
    for slot, (ref_if, ref_else, half, dy, dcore) in enumerate(
        ((b0, a0, 0, 1, 0), (a0, b0, 1, 0, 0), (a1, b1, 0, 1, 1), (b1, a1, 1, 0, 1)), 4
    ):
        @pl.when(first)
        def _(ref=ref_if, half=half, dy=dy, dcore=dcore, slot=slot):
            started(copies(ref, half, dy, dcore, slot))

        @pl.when(jnp.logical_not(first))
        def _(ref=ref_else, half=half, dy=dy, dcore=dcore, slot=slot):
            started(copies(ref, half, dy, dcore, slot))

        waits += copies(ref_if, half, dy, dcore, slot)
    return waits


def device_of(rows, half, d_model):
    row = lax.broadcasted_iota(jnp.int32, (d_model, 1), 0)
    device = lax.div(row, jnp.int32(rows))
    return device, row - device * rows


def one_hot(target, cols):
    lane = lax.broadcasted_iota(jnp.int32, (target.shape[0], cols), 1)
    return jnp.where(lane == target, 1.0, 0.0).astype(BF)


def qv_places(rows, d_model):
    device, at = device_of(rows, rows // 2, d_model)
    value = (at >= rows // 2).astype(jnp.int32)
    target = value * (d_model // 2) + device * (rows // 2) + at - value * (rows // 2)
    return one_hot(target, d_model)


def up_places(rows, d_model, part, ff):
    device, at = device_of(rows, rows, d_model)
    return one_hot(device * (2 * rows) + part * rows + at, ff)


def project_kernel(rows, n_qkv, where, tok_ref, *refs):
    pieces = refs[:n_qkv]
    proj_ref, vec_ref, up_ref, weights, bias, sem = refs[n_qkv:]
    d_model = tok_ref.shape[1]
    span = proj_ref.shape[1]

    @pl.when(pl.program_id(0) == 0)
    def _():
        for copy in piece_copies(where, pieces, weights, sem):
            copy.wait()
        bias[...] = jnp.zeros_like(bias)
        qv = qv_places(rows, d_model)
        up = [up_places(rows, d_model, part, up_ref.shape[1]) for part in range(2)]
        turned = weights[0, :, span:].T[:16]
        vec_ref[...] = turned[:8].astype(F32)
        row = mm(turned, qv, NN)[8:9]
        for pair in range(span // (3 * PAIR)):
            at = pair * 3 * PAIR
            bias[0:1, at : at + PAIR] = row[:, pair * PAIR : (pair + 1) * PAIR]
            first = d_model // 2 + pair * PAIR
            bias[0:1, at + 2 * PAIR : at + 3 * PAIR] = row[:, first : first + PAIR]
        up_ref[...] = mm(turned, up[0], NN)[6:7] + mm(turned, up[1], NN)[7:8]

    tokens = tok_ref[...]
    for at in range(0, span, 512):
        end = min(at + 512, span)
        proj_ref[:, at:end] = (mm(tokens, weights[0, :, at:end], NN) + bias[0:1, at:end]).astype(BF)


def project(where, tokens, pieces, rows, seq, span, ff, tile=512):
    d_model = tokens.shape[1]
    return pl.pallas_call(
        functools.partial(project_kernel, rows, len(pieces)),
        out_shape=(
            jax.ShapeDtypeStruct((seq, span), BF),
            jax.ShapeDtypeStruct((8, d_model), F32),
            jax.ShapeDtypeStruct((1, ff), F32),
        ),
        grid_spec=pltpu.PrefetchScalarGridSpec(
            num_scalar_prefetch=1,
            grid=(seq // tile,),
            in_specs=[own_tile(tile, d_model, seq)] + [ANYWHERE] * len(pieces),
            out_specs=[
                row_tile(tile, span),
                pl.BlockSpec((8, d_model), lambda i, w: (0, 0)),
                pl.BlockSpec((1, ff), lambda i, w: (0, 0)),
            ],
            scratch_shapes=[
                pltpu.VMEM((1, d_model, span + SMALL), BF),
                pltpu.VMEM((8, span), F32),
                pltpu.SemaphoreType.DMA((8, 4)),
            ],
        ),
        cost_estimate=cost(8.7),
        name="project",
    )(where, tokens, *pieces)


def last_kernel(n_qkv, where, own_ref, other_ref, one_ref, *refs):
    pieces = refs[:n_qkv]
    whole_ref, low_ref, weights, sem = refs[n_qkv:]
    span = own_ref.shape[1]

    @pl.when(pl.program_id(0) == 0)
    def _():
        for copy in piece_copies(where, pieces, weights, sem):
            copy.wait()

    total = (
        mm(own_ref[...], weights[0, :, :span], NT)
        + mm(other_ref[...], weights[1, :, :span], NT)
        + one_ref[...]
    )
    whole_ref[...] = total
    low_ref[...] = total.astype(BF)


def last_part(where, d_proj, d_one, pieces, tile=512):
    seq, span = d_proj[0].shape
    d_model = d_one.shape[1]
    return pl.pallas_call(
        functools.partial(last_kernel, len(pieces)),
        out_shape=(
            jax.ShapeDtypeStruct((2 * seq, d_model), F32),
            jax.ShapeDtypeStruct((seq, d_model), BF),
        ),
        grid_spec=pltpu.PrefetchScalarGridSpec(
            num_scalar_prefetch=1,
            grid=(seq // tile,),
            in_specs=[row_tile(tile, span), row_tile(tile, span), row_tile(tile, d_model)]
            + [ANYWHERE] * len(pieces),
            out_specs=[own_tile(tile, d_model, seq), row_tile(tile, d_model)],
            scratch_shapes=[
                pltpu.VMEM((2, d_model, span + SMALL), BF),
                pltpu.SemaphoreType.DMA((8, 4)),
            ],
        ),
        cost_estimate=cost(12.0),
        name="last_part",
    )(where, *d_proj, d_one, *pieces)


def part_copies(where, result, half, keep_ref, send_ref, sem, staged):
    if not staged:
        return [pltpu.make_async_copy(result.at[half], keep_ref.at[half], sem.at[half, 0])]
    if len(keep_ref.shape) == 4:
        rows = keep_ref.shape[2]
        return [
            pltpu.make_async_copy(
                result.at[half, pl.ds(d * rows, rows), :],
                keep_ref.at[d, where[3] ^ half],
                sem.at[half, d],
            )
            for d in range(keep_ref.shape[0])
        ]
    rows = keep_ref.shape[-2]
    z, y, core = where[0], where[1], where[2]
    out = []
    for dcore, target in enumerate((keep_ref, send_ref)):
        for dy in range(2):
            for k in range(4):
                block = ((lax.rem(z + k, 4) * 2 + (y ^ dy)) * 2 + (core ^ dcore)) * rows
                block = pl.multiple_of(block, 16)
                if target.shape[2] == 1:
                    place = target.at[dy, k, 0]
                else:
                    by_y = (core ^ dcore) == 0
                    place = target.at[jnp.where(by_y, dy, half), jnp.where(by_y, half, dy), k]
                out.append(
                    pltpu.make_async_copy(
                        result.at[half, pl.ds(block, rows), :], place, sem.at[half, len(out)]
                    )
                )
    return out


def part_shapes(staged, halves, d_model, cols):
    if not staged:
        whole = jax.ShapeDtypeStruct((halves, d_model, cols), BF)
        return whole, jax.ShapeDtypeStruct((8, 128), BF)
    rows = d_model // 16
    dims = (2, 4, 1, rows, cols) if halves == 1 else (2, 2, 4, rows, cols)
    return (jax.ShapeDtypeStruct(dims, BF),) * 2


def after(value, *others):
    return lax.optimization_barrier((value, *others))[0]


def grads_kernel(staged, rows, halves, widths, n_extra, where, *refs):
    count = len(widths)
    lhs_refs, refs = refs[:count], refs[count:]
    rhs_refs, refs = refs[: count * halves], refs[count * halves :]
    extra_refs, refs = refs[:n_extra], refs[n_extra:]
    keep_ref, send_ref, result, turned, sem = refs
    d_model = result.shape[1]
    for lhs, out in zip(lhs_refs, range(count)):
        for at in range(0, lhs.shape[0], BLOCK):
            turned[out, :, at : at + BLOCK] = lhs[at : at + BLOCK, :].T
    for half in range(halves):
        first = 0
        for n in range(count):
            rhs = rhs_refs[n * halves + half]
            rhs = rhs.at[half] if len(rhs.shape) == 3 else rhs
            width = rhs.shape[1]
            for at in range(0, width, 512):
                end = min(at + 512, width)
                result[half, :, first + at : first + end] = mm(
                    turned[n], rhs[:, at:end], NN
                ).astype(BF)
            first += width
        if n_extra == 1:
            (sums,) = extra_refs
            blank = jnp.zeros((SMALL - 1, PAIR), F32)
            parts = [
                sums[pair, 0:1, n * PAIR : (n + 1) * PAIR]
                for n in (0, 2)
                for pair in range(sums.shape[0])
            ]
            line = jnp.concatenate(parts, axis=1)
            lines = jnp.concatenate([line, jnp.zeros((SMALL - 1, line.shape[1]), F32)], axis=0)
            extra = mm(qv_places(rows, d_model), lines.astype(BF), NT)
        else:
            two, one, up = extra_refs
            own = one_hot(lax.broadcasted_iota(jnp.int32, (d_model, 1), 0), d_model)
            zero = jnp.zeros((SMALL - 6, d_model), F32)
            lines = jnp.concatenate([one[2:3], one[0:2], two[2:3], two[0:2], zero], axis=0)
            extra = mm(own, lines.astype(BF), NT)
            blank = jnp.zeros((SMALL - 8, up.shape[2]), F32)
            for part in range(2):
                line = up[half, 0:1]
                before = jnp.zeros((6 + part, line.shape[1]), F32)
                behind = jnp.zeros((SMALL - 7 - part, line.shape[1]), F32)
                lines = jnp.concatenate([before, line, behind], axis=0)
                extra = extra + mm(
                    up_places(rows, d_model, part, line.shape[1]), lines.astype(BF), NT
                )
        result[half, :, first:] = extra.astype(BF)
        for copy in part_copies(where, result, half, keep_ref, send_ref, sem, staged):
            copy.start()
    for half in range(halves):
        for copy in part_copies(where, result, half, keep_ref, send_ref, sem, staged):
            copy.wait()


def whole_spec(array):
    return pl.BlockSpec(array.shape, lambda i, w, n=array.ndim: (0,) * n)


def own_tile(tile, width, seq):
    return pl.BlockSpec((tile, width), lambda i, w: (w[3] * (seq // tile) + i, 0))


def grads(where, staged, rows, lhs, rhs, extra):
    halves = len(rhs[0])
    seq = rhs[0][0].shape[-2]
    d_model = lhs[0].shape[1]
    widths = [r[0].shape[-1] for r in rhs]
    cols = sum(widths) + SMALL
    operands = [*(r for pair in rhs for r in pair), *extra]
    return pl.pallas_call(
        functools.partial(grads_kernel, staged, rows, halves, widths, len(extra)),
        out_shape=part_shapes(staged, halves, d_model, cols),
        grid_spec=pltpu.PrefetchScalarGridSpec(
            num_scalar_prefetch=1,
            grid=(1,),
            in_specs=[
                own_tile(seq, d_model, seq) if l.shape[0] > seq else whole_spec(l) for l in lhs
            ]
            + [whole_spec(o) for o in operands],
            out_specs=[ANYWHERE] * 2,
            scratch_shapes=[
                pltpu.VMEM((halves, d_model, cols), BF),
                pltpu.VMEM((len(lhs), d_model, seq), BF),
                pltpu.SemaphoreType.DMA((halves, 16)),
            ],
        ),
        cost_estimate=cost(20.0 if halves == 2 else 7.2),
        name="grads",
    )(where, *lhs, *operands)


def row_norm(values):
    centered = values - jnp.mean(values, axis=-1, keepdims=True)
    inverse = lax.rsqrt(jnp.mean(centered * centered, axis=-1, keepdims=True) + NORM_EPS)
    return centered * inverse, inverse


def row_norm_back(d_normed, z, inverse, gain):
    dz = d_normed * gain
    return (
        dz - jnp.mean(dz, axis=-1, keepdims=True) - z * jnp.mean(dz * z, axis=-1, keepdims=True)
    ) * inverse


def column_sum(values):
    return jnp.sum(values, axis=0, keepdims=True)


def first_kernel(n_up, where, tok_ref, ctx0_ref, ctx1_ref, vec_ref, bias0_ref, bias1_ref, *refs):
    pieces = refs[:n_up]
    z_ref, inv_ref, hid_ref, slope_ref, weights, sem = refs[n_up:]
    bias_refs = bias0_ref, bias1_ref
    width = ctx0_ref.shape[1]

    @pl.when(pl.program_id(0) == 0)
    def _():
        for copy in piece_copies(where, pieces, weights, sem, True):
            copy.wait()

    resid = (
        tok_ref[...].astype(F32)
        + mm(ctx0_ref[...], weights[0, :, :width], NT)
        + mm(ctx1_ref[...], weights[1, :, :width], NT)
        + vec_ref[0:1]
    )
    z, inverse = row_norm(resid)
    z_ref[...] = z
    inv_ref[...] = jnp.broadcast_to(inverse, inv_ref.shape)
    low = (z * vec_ref[1:2] + vec_ref[2:3]).astype(BF)
    ff = hid_ref.shape[2]
    for half in range(2):
        for at in range(0, ff, 512):
            pre = mm(low, weights[half, :, width + at : width + at + 512], NN)
            gelu, slope = gelu_both(pre + bias_refs[half][:, at : at + 512])
            hid_ref[half, :, at : at + 512] = gelu.astype(BF)
            slope_ref[half, :, at : at + 512] = slope.astype(BF)


def row_tile(tile, width):
    return pl.BlockSpec((tile, width), lambda i, w: (i, 0))


def halves_tile(tile, width):
    return pl.BlockSpec((2, tile, width), lambda i, w: (0, i, 0))


ANYWHERE = pl.BlockSpec(memory_space=pl.ANY)


def first_part(where, tokens, ctx, vectors, bias, pieces, tile=256):
    d_model = tokens.shape[1]
    seq = ctx[0].shape[0]
    width, ff = ctx[0].shape[1], bias[0].shape[1]
    return pl.pallas_call(
        functools.partial(first_kernel, len(pieces)),
        out_shape=(
            jax.ShapeDtypeStruct((seq, d_model), F32),
            jax.ShapeDtypeStruct((seq, 128), F32),
            jax.ShapeDtypeStruct((2, seq, ff), BF),
            jax.ShapeDtypeStruct((2, seq, ff), BF),
        ),
        grid_spec=pltpu.PrefetchScalarGridSpec(
            num_scalar_prefetch=1,
            grid=(seq // tile,),
            in_specs=[
                own_tile(tile, d_model, seq),
                row_tile(tile, width),
                row_tile(tile, width),
                whole_spec(vectors),
                whole_spec(bias[0]),
                whole_spec(bias[1]),
            ]
            + [ANYWHERE] * len(pieces),
            out_specs=[
                row_tile(tile, d_model),
                row_tile(tile, 128),
                halves_tile(tile, ff),
                halves_tile(tile, ff),
            ],
            scratch_shapes=[
                pltpu.VMEM((2, d_model, width + ff), BF),
                pltpu.SemaphoreType.DMA((8, 4)),
            ],
        ),
        cost_estimate=cost(19.4),
        name="first_part",
    )(where, tokens, *ctx, vectors, *bias, *pieces)


def second_kernel(staged, n_down, where, hid_ref, z_ref, cot_ref, vec_ref, *refs):
    pieces = refs[:n_down]
    out_ref, own_ref, d_ref, sum_ref, keep_ref, *refs = refs[n_down:]
    weights, turned, kept, result, sem, out_sem = refs
    step = pl.program_id(0)
    tile, ff = hid_ref.shape[1:]

    @pl.when(step == 0)
    def _():
        for copy in piece_copies(where, pieces, weights, sem):
            copy.wait()
        sum_ref[...] = jnp.zeros_like(sum_ref)

    ffn = mm(hid_ref[0], weights[0], NT) + mm(hid_ref[1], weights[1], NT)
    resid = z_ref[...] * vec_ref[1:2] + vec_ref[2:3] + ffn + vec_ref[3:4]
    z, inverse = row_norm(resid)
    out = (z * vec_ref[4:5] + vec_ref[5:6]).astype(BF)
    out_ref[...] = out
    own_ref[...] = out
    cot = cot_ref[...].astype(F32)
    d_two = row_norm_back(cot, z, inverse, vec_ref[4:5])
    d_ref[...] = d_two
    sum_ref[0:1] += column_sum(cot * z)
    sum_ref[1:2] += column_sum(cot)
    sum_ref[2:3] += column_sum(d_two)
    rows = pl.ds(pl.multiple_of(step * tile, tile), tile)
    turned[:, rows] = d_two.astype(BF).T
    kept[:, rows, :] = hid_ref[...]

    @pl.when(step == pl.num_programs(0) - 1)
    def _():
        for half in range(2):
            for at in range(0, ff, 512):
                result[half, :, at : at + 512] = mm(
                    turned[...], kept[half, :, at : at + 512], NN
                ).astype(BF)
            for copy in part_copies(where, result, half, keep_ref, None, out_sem, staged):
                copy.start()
        for half in range(2):
            for copy in part_copies(where, result, half, keep_ref, None, out_sem, staged):
                copy.wait()


def second_part(where, staged, hidden, z_one, cot, vectors, pieces, tile=256):
    _, seq, ff = hidden.shape
    d_model = z_one.shape[1]
    return pl.pallas_call(
        functools.partial(second_kernel, staged, len(pieces)),
        out_shape=(
            jax.ShapeDtypeStruct((2 * seq, d_model), BF),
            jax.ShapeDtypeStruct((seq, d_model), BF),
            jax.ShapeDtypeStruct((seq, d_model), F32),
            jax.ShapeDtypeStruct((8, d_model), F32),
            (
                jax.ShapeDtypeStruct((16, 2, d_model // 16, ff), BF)
                if staged
                else jax.ShapeDtypeStruct((2, d_model, ff), BF)
            ),
        ),
        grid_spec=pltpu.PrefetchScalarGridSpec(
            num_scalar_prefetch=1,
            grid=(seq // tile,),
            in_specs=[
                halves_tile(tile, ff),
                row_tile(tile, d_model),
                own_tile(tile, d_model, seq),
                whole_spec(vectors),
            ]
            + [ANYWHERE] * len(pieces),
            out_specs=[
                own_tile(tile, d_model, seq),
                row_tile(tile, d_model),
                row_tile(tile, d_model),
                pl.BlockSpec((8, d_model), lambda i, w: (0, 0)),
                ANYWHERE,
            ],
            scratch_shapes=[
                pltpu.VMEM((2, d_model, ff), BF),
                pltpu.VMEM((d_model, seq), BF),
                pltpu.VMEM((2, seq, ff), BF),
                pltpu.VMEM((2, d_model, ff), BF),
                pltpu.SemaphoreType.DMA((8, 4)),
                pltpu.SemaphoreType.DMA((2, 16)),
            ],
        ),
        cost_estimate=cost(21.8),
        name="second_part",
    )(where, hidden, z_one, cot, vectors, *pieces)


def third_kernel(n_up, n_down, where, d_ref, slope_ref, z_ref, inv_ref, vec_ref, *refs):
    up_pieces, down_pieces, refs = refs[:n_up], refs[n_up : n_up + n_down], refs[n_up + n_down :]
    pre_ref, low_ref, one_ref, one_low_ref, ctx_ref, sum_ref, bias_ref, *refs = refs
    up, down, sem, down_sem = refs
    step = pl.program_id(0)
    ff = slope_ref.shape[2]
    width = ctx_ref.shape[2]

    @pl.when(step == 0)
    def _():
        waits = piece_copies(where, down_pieces, down, down_sem)
        waits += piece_copies(where, up_pieces, up, sem, True)
        for copy in waits:
            copy.wait()
        sum_ref[...] = jnp.zeros_like(sum_ref)
        bias_ref[...] = jnp.zeros_like(bias_ref)

    d_two = d_ref[...]
    d_two_low = d_two.astype(BF)
    d_normed = d_two
    for half in range(2):
        for at in range(0, ff, 512):
            span = slice(at, at + 512)
            d_pre = mm(d_two_low, down[half, :, span], NN) * slope_ref[half, :, span].astype(F32)
            d_pre = d_pre.astype(BF)
            pre_ref[half, :, span] = d_pre
            bias_ref[half, 0:1, span] += column_sum(d_pre.astype(F32))
            d_normed = d_normed + mm(d_pre, up[half, :, width + at : width + at + 512], NT)
    z = z_ref[...]
    low_ref[...] = (z * vec_ref[1:2] + vec_ref[2:3]).astype(BF)
    d_one = row_norm_back(d_normed, z, inv_ref[:, 0:1], vec_ref[1:2])
    one_ref[...] = d_one
    sum_ref[0:1] += column_sum(d_normed * z)
    sum_ref[1:2] += column_sum(d_normed)
    sum_ref[2:3] += column_sum(d_one)
    d_one_low = d_one.astype(BF)
    one_low_ref[...] = d_one_low
    for half in range(2):
        ctx_ref[half] = mm(d_one_low, up[half, :, :width], NN).astype(BF)


def third_part(where, d_two, slope, z_one, inv_one, vectors, up_pieces, down_pieces, width, tile=256):
    seq, d_model = d_two.shape
    ff = slope.shape[2]
    return pl.pallas_call(
        functools.partial(third_kernel, len(up_pieces), len(down_pieces)),
        out_shape=(
            jax.ShapeDtypeStruct((2, seq, ff), BF),
            jax.ShapeDtypeStruct((seq, d_model), BF),
            jax.ShapeDtypeStruct((seq, d_model), F32),
            jax.ShapeDtypeStruct((seq, d_model), BF),
            jax.ShapeDtypeStruct((2, seq, width), BF),
            jax.ShapeDtypeStruct((8, d_model), F32),
            jax.ShapeDtypeStruct((2, 8, ff), F32),
        ),
        grid_spec=pltpu.PrefetchScalarGridSpec(
            num_scalar_prefetch=1,
            grid=(seq // tile,),
            in_specs=[
                row_tile(tile, d_model),
                halves_tile(tile, ff),
                row_tile(tile, d_model),
                row_tile(tile, 128),
                whole_spec(vectors),
            ]
            + [ANYWHERE] * (len(up_pieces) + len(down_pieces)),
            out_specs=[
                halves_tile(tile, ff),
                row_tile(tile, d_model),
                row_tile(tile, d_model),
                row_tile(tile, d_model),
                halves_tile(tile, width),
                pl.BlockSpec((8, d_model), lambda i, w: (0, 0)),
                pl.BlockSpec((2, 8, ff), lambda i, w: (0, 0, 0)),
            ],
            scratch_shapes=[
                pltpu.VMEM((2, d_model, width + ff), BF),
                pltpu.VMEM((2, d_model, ff), BF),
                pltpu.SemaphoreType.DMA((8, 4)),
                pltpu.SemaphoreType.DMA((8, 4)),
            ],
        ),
        cost_estimate=cost(25.6),
        name="third_part",
    )(where, d_two, slope, z_one, inv_one, vectors, *up_pieces, *down_pieces)


def add(first, second):
    return (first.astype(F32) + second.astype(F32)).astype(BF)


def core_stage(keep, send):
    return move(send, MOVE_CORE), keep


def flip_stage(moves, got, keep):
    return move(add(keep[1], got[1]), moves), add(keep[0], got[0])


def z_stage(*terms):
    sums = [functools.reduce(jnp.add, [t[k].astype(F32) for t in terms]) for k in range(4)]
    parts = [move(part.astype(BF), moves) for part, moves in zip(sums[1:], MOVE_Z)]
    return parts, sums[0]


def z_sum(parts, keep):
    return keep + parts[0].astype(F32) + parts[1].astype(F32) + parts[2].astype(F32)


def lane_mask(head, rows):
    lanes = lax.broadcasted_iota(jnp.int32, (rows, PAIR), 1)
    return (lanes < HD) if head == 0 else (lanes >= HD)


def attn_fwd_kernel(table, qkv_ref, ctx_ref, prob_ref):
    pair = pl.program_id(0)
    q_ref, k_ref, v_ref = (qkv_ref.at[:, n * PAIR : (n + 1) * PAIR] for n in range(3))
    lanes = lax.broadcasted_iota(jnp.int32, (1, HALF), 1)
    for half in range(2):
        rows = pl.ds(half * HALF, HALF)
        query = q_ref[rows, :] * jnp.asarray(HD**-0.5, BF)
        parts = []
        for head in range(2):
            at = (pair * 2 + head) * 4
            start = (half ^ table[at]) * HALF
            flags = [table[at + 1 + n] == 1 for n in range(3)]
            key_lo = k_ref[pl.ds(pl.multiple_of(start, BLOCK), BLOCK), :]
            key_hi = k_ref[pl.ds(pl.multiple_of(start + BLOCK, BLOCK), BLOCK), :]
            masked = jnp.where(lane_mask(head, HALF), query, jnp.zeros_like(query))
            score_lo = mm(key_lo, masked, NT)
            score_hi = mm(key_hi, masked[BLOCK:], NT)
            no_lo = jnp.where(
                lanes < BLOCK,
                jnp.where(flags[0], 0.0, -1e30),
                jnp.where(flags[1], 0.0, -1e30),
            ).astype(F32)
            no_hi = jnp.where(flags[2], 0.0, -1e30).astype(F32)
            top_lo = jnp.max(score_lo, axis=0, keepdims=True) + no_lo
            top_hi = jnp.max(score_hi, axis=0, keepdims=True) + no_hi
            top = jnp.concatenate(
                [top_lo[:, :BLOCK], jnp.maximum(top_lo[:, BLOCK:], top_hi)], axis=1
            )
            ref_lo = jnp.where(no_lo < 0.0, 1e30, top)
            ref_hi = jnp.where(no_hi < 0.0, 1e30, top[:, BLOCK:])
            exp_lo = jnp.exp(score_lo - ref_lo)
            exp_hi = jnp.exp(score_hi - ref_hi)
            sum_lo = jnp.sum(exp_lo, axis=0, keepdims=True)
            sum_hi = jnp.sum(exp_hi, axis=0, keepdims=True)
            total = jnp.concatenate([sum_lo[:, :BLOCK], sum_lo[:, BLOCK:] + sum_hi], axis=1)
            scale = jnp.where(total > 0.0, 1.0 / jnp.where(total > 0.0, total, 1.0), 0.0)
            prob_lo = (exp_lo * scale).astype(BF)
            prob_hi = (exp_hi * scale[:, BLOCK:]).astype(BF)
            prob_ref[0, head, half, :, :HALF] = prob_lo
            prob_ref[0, head, half, :, HALF:] = prob_hi
            val_lo = v_ref[pl.ds(pl.multiple_of(start, BLOCK), BLOCK), :].T
            val_hi = v_ref[pl.ds(pl.multiple_of(start + BLOCK, BLOCK), BLOCK), :].T
            side = slice(head * HD, (head + 1) * HD)
            out_lo = mm(val_lo[side], prob_lo, NN)
            out_hi = mm(val_hi[side], prob_hi, NN)
            parts.append(
                jnp.concatenate([out_lo[:, :BLOCK], out_lo[:, BLOCK:] + out_hi], axis=1)
            )
        ctx_ref[rows, :] = jnp.concatenate(parts, axis=0).T.astype(BF)


def attn_fwd(table, proj):
    seq, width = proj.shape
    pairs = width // 3 // PAIR
    return pl.pallas_call(
        attn_fwd_kernel,
        out_shape=(
            jax.ShapeDtypeStruct((seq, width // 3), BF),
            jax.ShapeDtypeStruct((pairs, 2, 2, BLOCK, HALF + BLOCK), BF),
        ),
        grid_spec=pltpu.PrefetchScalarGridSpec(
            num_scalar_prefetch=1,
            grid=(pairs,),
            in_specs=[pl.BlockSpec((seq, 3 * PAIR), lambda p, t: (0, p))],
            out_specs=[
                pl.BlockSpec((seq, PAIR), lambda p, t: (0, p)),
                pl.BlockSpec((1, 2, 2, BLOCK, HALF + BLOCK), lambda p, t: (p, 0, 0, 0, 0)),
            ],
        ),
        cost_estimate=cost(0.5),
        name="attn_fwd",
    )(table, proj)


def attn_bwd_kernel(table, qkv_ref, d_ref, prob_ref, out_ref, sum_ref, k_acc, v_acc):
    pair = pl.program_id(0)
    q_ref, k_ref, v_ref = (qkv_ref.at[:, n * PAIR : (n + 1) * PAIR] for n in range(3))
    for half in range(2):
        rows = pl.ds(half * HALF, HALF)
        query = q_ref[rows, :] * jnp.asarray(HD**-0.5, BF)
        d_ctx = d_ref[rows, :]
        parts = []
        for head in range(2):
            at = (pair * 2 + head) * 4
            start = (half ^ table[at]) * HALF
            at_lo = pl.ds(pl.multiple_of(start, BLOCK), BLOCK)
            at_hi = pl.ds(pl.multiple_of(start + BLOCK, BLOCK), BLOCK)
            keep = lane_mask(head, HALF)
            query_h = jnp.where(keep, query, jnp.zeros_like(query))
            d_ctx_h = jnp.where(keep, d_ctx, jnp.zeros_like(d_ctx))
            prob_lo = prob_ref[0, head, half, :, :HALF]
            prob_hi = prob_ref[0, head, half, :, HALF:]
            d_w_lo = mm(v_ref[at_lo, :], d_ctx_h, NT)
            d_w_hi = mm(v_ref[at_hi, :], d_ctx_h[BLOCK:], NT)
            wide_lo = prob_lo.astype(F32)
            wide_hi = prob_hi.astype(F32)
            dot_lo = jnp.sum(wide_lo * d_w_lo, axis=0, keepdims=True)
            dot_hi = jnp.sum(wide_hi * d_w_hi, axis=0, keepdims=True)
            dot = jnp.concatenate([dot_lo[:, :BLOCK], dot_lo[:, BLOCK:] + dot_hi], axis=1)
            d_s_lo = (wide_lo * (d_w_lo - dot)).astype(BF)
            d_s_hi = (wide_hi * (d_w_hi - dot[:, BLOCK:])).astype(BF)
            dk_lo = mm(d_s_lo, query_h, NN)
            dk_hi = mm(d_s_hi, query_h[BLOCK:], NN)
            dv_lo = mm(prob_lo, d_ctx_h, NN)
            dv_hi = mm(prob_hi, d_ctx_h[BLOCK:], NN)
            k_acc[head, at_lo, :] = dk_lo
            k_acc[head, at_hi, :] = dk_hi
            v_acc[head, at_lo, :] = dv_lo
            v_acc[head, at_hi, :] = dv_hi
            key_lo = k_ref[at_lo, :].T
            key_hi = k_ref[at_hi, :].T
            side = slice(head * HD, (head + 1) * HD)
            dq_lo = mm(key_lo[side], d_s_lo, NN)
            dq_hi = mm(key_hi[side], d_s_hi, NN)
            parts.append(jnp.concatenate([dq_lo[:, :BLOCK], dq_lo[:, BLOCK:] + dq_hi], axis=1))
        out_ref[rows, :PAIR] = (jnp.concatenate(parts, axis=0).T * HD**-0.5).astype(BF)
    out_ref[:, PAIR : 2 * PAIR] = (k_acc[0] + k_acc[1]).astype(BF)
    out_ref[:, 2 * PAIR :] = (v_acc[0] + v_acc[1]).astype(BF)
    sums = jnp.sum(out_ref[...].astype(F32), axis=0, keepdims=True)
    sum_ref[0] = jnp.broadcast_to(sums, sum_ref.shape[1:])


def attn_bwd(table, proj, d_context, half, probs):
    seq, width = proj.shape
    pairs = width // 3 // PAIR
    return pl.pallas_call(
        attn_bwd_kernel,
        out_shape=(
            jax.ShapeDtypeStruct((seq, width), BF),
            jax.ShapeDtypeStruct((pairs, 8, 3 * PAIR), F32),
        ),
        grid_spec=pltpu.PrefetchScalarGridSpec(
            num_scalar_prefetch=1,
            grid=(pairs,),
            in_specs=[
                pl.BlockSpec((seq, 3 * PAIR), lambda p, t: (0, p)),
                pl.BlockSpec((None, seq, PAIR), lambda p, t: (half, 0, p)),
                pl.BlockSpec((1, 2, 2, BLOCK, HALF + BLOCK), lambda p, t: (p, 0, 0, 0, 0)),
            ],
            out_specs=[
                pl.BlockSpec((seq, 3 * PAIR), lambda p, t: (0, p)),
                pl.BlockSpec((1, 8, 3 * PAIR), lambda p, t: (p, 0, 0)),
            ],
            scratch_shapes=[pltpu.VMEM((2, seq, PAIR), F32)] * 2,
        ),
        cost_estimate=cost(11.3),
        name="attn_bwd",
    )(table, proj, d_context, probs)


def gelu_both(values):
    half = 0.5 * (1.0 + lax.erf(values * (0.5**0.5)))
    slope = half + values * jnp.exp(-0.5 * values * values) * 0.3989422804014327
    return values * half, slope


def body(
    dp_size,
    tokens,
    grad_out,
    head_perm,
    block_mask,
    w_qkv,
    b_qv,
    w_out,
    b_out,
    gain_one,
    shift_one,
    w_up,
    b_up,
    w_down,
    b_down,
    gain_two,
    shift_two,
):
    seq = tokens.shape[0] // head_perm.shape[0]
    rows = w_qkv.shape[0]
    width = w_qkv.shape[2]
    d_model = tokens.shape[1]
    dp_at = lax.axis_index("dp")
    mp_at = lax.axis_index("mp")
    where = jnp.stack([dp_at // 4, (dp_at // 2) % 2, dp_at % 2, mp_at]).astype(jnp.int32)

    table = jnp.concatenate([head_perm[:, :, None], block_mask], axis=2).astype(jnp.int32)
    table = table.reshape(2, -1)
    table_own = lax.dynamic_index_in_dim(table, mp_at, 0, keepdims=False)
    table_other = swap_mp(lax.dynamic_index_in_dim(table, 1 - mp_at, 0, keepdims=False))

    small = jnp.stack(
        [
            b_out,
            gain_one,
            shift_one,
            b_down,
            gain_two,
            shift_two,
            b_up[:rows],
            b_up[rows:],
            b_qv.reshape(-1),
        ],
        axis=1,
    )
    small = jnp.pad(small, ((0, 0), (0, SMALL - small.shape[1])))
    pairs = width // PAIR
    by_pair = w_qkv.reshape(rows, 3, pairs, PAIR).transpose(0, 2, 1, 3).reshape(rows, 3 * width)
    shard_qkv = jnp.concatenate([by_pair, small], axis=1)
    shard_up = jnp.concatenate([w_out.T, w_up], axis=1)
    shard_down = w_down.T
    staged = dp_size == 16

    def plain_gather(shard):
        full = lax.all_gather(shard, "dp", axis=0, tiled=True)
        return full, swap_mp(full)

    def gather_z(shard):
        return jnp.stack([shard] + [move(shard, moves) for moves in MOVE_Z])

    def gather_core(*pieces):
        return (*pieces, *(move(piece, MOVE_CORE) for piece in pieces))

    if staged:
        qkv_z = gather_z(shard_qkv)
        qkv_y = move(qkv_z, MOVE_Y)
        qkv_x = move(qkv_z, MOVE_X)
        up_parts = [move(after(shard_up, qkv_z), moves) for moves in MOVE_Z]
        down_whole = lax.all_gather(after(shard_down, qkv_z), AXES)
        down_pieces = (down_whole.reshape(dp_size, 2, *shard_down.shape),)
        qkv_y, *up_parts = lax.optimization_barrier((qkv_y, *up_parts))
        qkv_own = gather_core(qkv_z, qkv_y)
        qkv_xy = move(qkv_y, MOVE_X)
        up_z = jnp.stack([shard_up, *up_parts])
        tokens_in, table_other, qkv_x, up_z = lax.optimization_barrier(
            (tokens, table_other, qkv_x, up_z)
        )
        up_a, up_b = move(up_z, MOVE_FIRST), move(up_z, MOVE_SECOND)
    else:
        qkv_own, qkv_other = ((piece,) for piece in plain_gather(shard_qkv))
        up_pieces = plain_gather(shard_up)
        down_pieces = plain_gather(shard_down)
        tokens_in = tokens

    ff = w_up.shape[1]

    def project_half(values, pieces):
        return project(where, values, pieces, rows, seq, 3 * width, ff)

    proj_own, vectors, bias_own = project_half(tokens_in, qkv_own)
    if staged:
        proj_own, qkv_xy = lax.optimization_barrier((proj_own, qkv_xy))
        qkv_other = gather_core(qkv_x, qkv_xy)
    ctx_own, probs_own = attn_fwd(table_own, proj_own)
    if staged:
        ctx_own, up_a = lax.optimization_barrier((ctx_own, up_a))
    proj_other, _, bias_other = project_half(after(tokens, ctx_own), qkv_other)
    if staged:
        proj_other, up_a = lax.optimization_barrier((proj_other, up_a))
        up_c = move(up_a, MOVE_SECOND)
        up_pieces = gather_core(up_z, up_a, up_b)
    ctx_other, probs_other = attn_fwd(table_other, proj_other)
    if staged:
        ctx_other, up_c = lax.optimization_barrier((ctx_other, up_c))
        up_pieces = (*up_pieces[:3], up_c, *up_pieces[3:], move(up_c, MOVE_CORE))
    tables, proj = (table_own, table_other), (proj_own, proj_other)
    probs = (probs_own, probs_other)
    ctx = (ctx_own, ctx_other)
    qkv_pieces = (*qkv_own, *qkv_other)
    z_one, inv_one, hidden, slope = first_part(
        where, tokens, ctx, vectors, (bias_own, bias_other), up_pieces
    )

    def place(whole, other):
        return lax.dynamic_update_slice_in_dim(
            whole, other.astype(whole.dtype), (1 - mp_at) * seq, 0
        )

    out_whole, out_own, d_two, sums_two, down_grad = second_part(
        where, staged, hidden, z_one, grad_out, vectors, down_pieces
    )
    out_other = swap_mp(out_own)

    def plain_scatter(own, other):
        summed = own.astype(F32) + swap_mp(other).astype(F32)
        return lax.psum_scatter(summed, "dp", scatter_dimension=0, tiled=True)

    if staged:
        down_grad = down_grad.reshape(2 * dp_size, *shard_down.shape)
        s_down = lax.psum_scatter(down_grad, AXES, scatter_dimension=0)
    else:
        s_down = plain_scatter(*down_grad)
    d_pre, normed_low, d_one, d_one_low, d_ctx, sums_one, sums_up = third_part(
        where, d_two, slope, z_one, inv_one, vectors, up_pieces, down_pieces, width
    )
    up_parts = grads(
        where,
        staged,
        rows,
        [normed_low, d_one_low],
        [(d_pre, d_pre), ctx],
        (sums_two, sums_one, sums_up),
    )
    d_ctx_other = d_ctx
    if staged:
        up_got, up_keep = core_stage(*up_parts)
        d_ctx_other, out_other, up_keep = lax.optimization_barrier((d_ctx, out_other, up_keep))
    else:
        s_up = plain_scatter(*up_parts[0])
    d_proj_other, sums_other = attn_bwd(tables[1], proj[1], d_ctx_other, 1, probs[1])
    if staged:
        d_proj_other, up_got = lax.optimization_barrier((d_proj_other, up_got))
        up_got, up_keep = flip_stage(MOVE_REDUCE[0], up_got, up_keep)
        d_proj_other, up_keep = lax.optimization_barrier((d_proj_other, up_keep))
    other_parts = grads(where, staged, rows, [tokens], [(d_proj_other,)], (sums_other,))
    d_ctx_own = d_ctx
    if staged:
        qo_got, qo_keep = core_stage(*other_parts)
        d_ctx_own, qo_keep = lax.optimization_barrier((d_ctx, qo_keep))
    d_proj_own, sums_own = attn_bwd(tables[0], proj[0], d_ctx_own, 0, probs[0])
    d_proj_last = d_proj_own
    if staged:
        d_proj_own, up_got, qo_got = lax.optimization_barrier((d_proj_own, up_got, qo_got))
        up_got, up_keep = flip_stage(MOVE_REDUCE[1], up_got, up_keep)
        qo_got, qo_keep = flip_stage(MOVE_Y, qo_got, qo_keep)
        d_proj_last, up_keep, qo_keep = lax.optimization_barrier((d_proj_own, up_keep, qo_keep))
    d_input, in_low = last_part(where, (d_proj_last, d_proj_other), d_one, qkv_pieces)
    tokens_in = tokens
    if staged:
        in_both = lax.all_gather(in_low, "mp")
        tokens_in, in_low, up_got, qo_got = lax.optimization_barrier(
            (tokens, in_low, up_got, qo_got)
        )
        qo_in = move(add(qo_keep, qo_got), MOVE_X)
        up_parts, up_keep = z_stage(up_got, up_keep)
        tokens_in, up_keep = lax.optimization_barrier((tokens_in, up_keep))
    else:
        in_other = swap_mp(in_low)
    own_parts = grads(where, staged, rows, [tokens_in], [(d_proj_own,)], (sums_own,))
    if staged:
        qs_got, qs_keep = core_stage(*own_parts)
        qs_keep, *up_parts = lax.optimization_barrier((qs_keep, *up_parts))
        qs_got, qs_keep = flip_stage(MOVE_Y, qs_got, qs_keep)
        out_other, qs_keep, s_down = lax.optimization_barrier((out_other, qs_keep, s_down))
        s_down = s_down.astype(F32)
        out_whole = place(out_whole, out_other)
        out_whole, qs_got = lax.optimization_barrier((out_whole, qs_got))
        s_up = z_sum(up_parts, up_keep)
        qs_parts, qs_keep = z_stage(qs_got, qs_keep, qo_in)
        in_both, qs_keep = lax.optimization_barrier((in_both, qs_keep))
        in_other = lax.dynamic_index_in_dim(in_both, 1 - mp_at, 0, keepdims=False)
        d_input = place(d_input, in_other)
        d_input, qs_keep = lax.optimization_barrier((d_input, qs_keep))
        s_qkv = z_sum(qs_parts, qs_keep)[0]
    else:
        out_whole = place(out_whole, out_other)
        d_input = place(d_input, in_other)
        s_qkv = plain_scatter(own_parts[0][0], other_parts[0][0])

    cols = s_up[:, ff + width :].T
    g_w_qkv = s_qkv[:, : 3 * width].reshape(rows, pairs, 3, PAIR).transpose(0, 2, 1, 3)
    return (
        out_whole,
        d_input,
        g_w_qkv.reshape(rows, 3, width),
        s_qkv[:, 3 * width].reshape(2, rows // 2),
        s_up[:, ff : ff + width].T,
        cols[0],
        cols[1],
        cols[2],
        s_up[:, :ff],
        cols[6:8].reshape(-1),
        s_down.T,
        cols[3],
        cols[4],
        cols[5],
    )


def solution(mesh):
    placed = (
        P("dp", None),
        P("dp", None),
        P("dp", "mp"),
        P("dp", "mp", None),
        P("dp", None, "mp"),
        P(None, ("mp", "dp")),
        P("mp", "dp"),
        P("dp"),
        P("dp"),
        P("dp"),
        P("dp", "mp"),
        P(("mp", "dp")),
        P("mp", "dp"),
        P("dp"),
        P("dp"),
        P("dp"),
    )
    return jax.shard_map(
        functools.partial(body, mesh.shape["dp"]),
        mesh=mesh,
        in_specs=placed,
        out_specs=(
            P("dp", None),
            P("dp", None),
            P("dp", None, "mp"),
            P(None, ("mp", "dp")),
            P("mp", "dp"),
            P("dp"),
            P("dp"),
            P("dp"),
            P("dp", "mp"),
            P(("mp", "dp")),
            P("mp", "dp"),
            P("dp"),
            P("dp"),
            P("dp"),
        ),
        check_vma=False,
    )
```
